256 devices in a mesh: beam: 8 (over y_hi, x), blk: 32 (over y_lo, z, core).
Axes of the slice: x: 4, y: 4 (y_hi: 2, y_lo: 2; y = y_hi * 2 + y_lo), z: 8, core: 2. Of those that a mesh axis runs over, the one named last changes fastest.
Arguments:
- hidden_in: bfloat16 [256, 4096], P('beam', 'blk'), may hold values from -250 to 250
- self_gain: bfloat16 [4096], P('blk'), may hold values from 0.099609375 to 1.8984375
- w_self: bfloat16 [4096, 3, 4096], P(None, None, 'blk'), may hold values from -0.09375 to 0.09375
- w_self_out: bfloat16 [4096, 4096], P('blk'), may hold values from -0.1875 to 0.1875
- cross_gain: bfloat16 [4096], P('blk'), may hold values from 0.099609375 to 1.8984375
- w_cross_q: bfloat16 [4096, 4096], P('blk'), may hold values from -0.09375 to 0.09375
- w_cross_out: bfloat16 [4096, 4096], P(None, 'blk'), may hold values from -0.09375 to 0.09375
- cache_kv: bfloat16 [256, 128, 64, 128], P('beam', None, 'blk'), may hold values from -1000 to 1000
- memory_kv: bfloat16 [8192, 8192], P('blk'), may hold values from -1000 to 1000
- parents: int32 [256], replicated, may hold values from 0 to 255
- prefix_len: int32 [256], replicated, may hold values from 65 to 128, as said below
Outputs:
- result: bfloat16 [256, 4096], P('beam', 'blk')
The draws below stay inside these ranges and needn't reach their ends.
Inputs may be any that keep to these rules, and one draw needn't show every extreme that they name: New hypothesis i continues the cache of old hypothesis parents[i]. Cache positions below prefix_len[i] hold decoded tokens of new hypothesis i.
All inputs are finite; a program needn't handle non-finite values.
Results may differ from the reference program's by a relative error of at most 0.013.
Values may be sent and summed in bfloat16 or wider, within the bound.
A program may use at most 128 MiB of HBM per device.

```python
import math
import jax
import jax.numpy as jnp
import numpy as np
from jax import lax

D = 4096
HEADS = 64
HEAD_DIM = 64
MEM_DEV = 256
CACHE = 128
HW = 4096
HYPS = 256
MEM = 8192
N_BLK = 32


def rough_keys(key, row_total, head_width):
    draws = jnp.clip(jax.random.normal(key, (row_total, head_width), jnp.float32), -6.0, 6.0)
    spread_keys = draws * 2.5
    return spread_keys


def draw_memory_kv(key, part):
    head_width = HEADS * HEAD_DIM
    keys_part = rough_keys(jax.random.fold_in(key, 11), MEM, head_width)
    values_part = jnp.clip(jax.random.normal(jax.random.fold_in(key, 12), (MEM, head_width), jnp.float32), -6.0, 6.0)
    return jnp.concatenate([keys_part, values_part], axis=1).astype(jnp.bfloat16)


def draw_cache_kv(key, part):
    head_width = HEADS * HEAD_DIM
    keys_part = rough_keys(jax.random.fold_in(key, 21), HYPS * CACHE, head_width).reshape(HYPS, CACHE, HEADS, HEAD_DIM)
    values_part = jnp.clip(jax.random.normal(jax.random.fold_in(key, 22), (HYPS, CACHE, HEADS, HEAD_DIM), jnp.float32), -6.0, 6.0)
    return jnp.concatenate([keys_part, values_part], axis=3).astype(jnp.bfloat16)


def draw_hidden_in(key, part):
    draws = jnp.clip(jax.random.normal(jax.random.fold_in(key, 31), (HYPS, D), jnp.float32), -6.0, 6.0)
    columns = jnp.arange(D).astype(jnp.float32) / D
    rough = jax.random.uniform(jax.random.fold_in(key, 32), (D,), jnp.float32, 0.5, 1.5)
    draws = draws * (3.0 ** columns * rough)[None, :]
    return draws.astype(jnp.bfloat16)


def draw_prefix_len(key, part):
    shortest = CACHE // 2 + 1
    lengths = jax.random.randint(jax.random.fold_in(key, 41), (HYPS,), shortest, CACHE + 1, jnp.int32)
    longest_at = jax.random.randint(jax.random.fold_in(key, 42), (), 0, HYPS, jnp.int32)
    step_over = jax.random.randint(jax.random.fold_in(key, 43), (), 1, HYPS, jnp.int32)
    shortest_at = (longest_at + step_over) % HYPS
    positions = jnp.arange(HYPS, dtype=jnp.int32)
    lengths = jnp.where(positions == longest_at, CACHE, lengths)
    lengths = jnp.where(positions == shortest_at, shortest, lengths)
    return lengths.astype(jnp.int32)


def place_ends(drawn, own_key, smallest, high):
    index_at = [jax.random.randint(jax.random.fold_in(own_key, axis), (), 0, length) for axis, length in enumerate(drawn.shape)]
    widest = drawn.shape.index(max(drawn.shape))
    neighbour = index_at[:widest] + [(index_at[widest] + 1) % drawn.shape[widest]] + index_at[widest + 1:]
    return drawn.at[tuple(index_at)].set(smallest).at[tuple(neighbour)].set(high)


def strengthened(drawn, own_key, source, target, blocks, factor):
    owner, partner = [(jnp.arange(drawn.shape[dim]) // (drawn.shape[dim] // blocks)).reshape([-1 if axis == dim else 1 for axis in range(drawn.ndim)]) for dim in (source, target)]
    chosen = jax.random.permutation(own_key, blocks)[partner]
    strong = (owner == chosen) | (owner == (partner + blocks // 2) % blocks)
    return jnp.where(strong, factor * drawn, drawn)


def block_scale(own_key, shape, cuts, least, largest):
    def one(position, blocks):
        steps = jax.random.uniform(jax.random.fold_in(jax.random.fold_in(own_key, 6), position), (blocks,), jnp.float32, least / len(cuts), largest / len(cuts))
        return jnp.repeat(jnp.exp(steps), shape[position] // blocks).reshape((-1,) + (1,) * (len(shape) - position - 1))

    gain = one(*cuts[0])
    for cut in cuts[1:]:
        gain = gain * one(*cut)
    return gain


def rank_table(count, skew):
    weights = [(1 << 20) // math.isqrt(rank ** skew) + 1 for rank in range(1, count + 1)]
    deviation = 1 + sum(weights) // (1 << 30)
    return np.cumsum(np.array([max(1, weight // deviation) for weight in weights]))


def skewed_ids(stream_key, shape, number_of, skew):
    grid = rank_table(number_of, skew)
    lot = jax.random.randint(jax.random.fold_in(stream_key, 1), shape, 0, int(grid[number_of - 1]))
    grade = jnp.searchsorted(jnp.asarray(grid, jnp.int32), lot, side="right")
    return jax.random.permutation(jax.random.fold_in(stream_key, 2), number_of)[grade].astype(jnp.int32)


def centred(key, extent, deviation, reach, split=(), kind=jnp.bfloat16):
    array = deviation * jax.random.normal(key, extent, jnp.float32)
    if split:
        array = array * block_scale(key, extent, split, -0.22, 0.18)
    return jnp.clip(array, -reach, reach).astype(kind)


def gaussian_with(key, extent, scale, most, split, heavy, kind=jnp.bfloat16):
    entries = scale * jax.random.normal(key, extent, jnp.float32)
    if split:
        entries = entries * block_scale(key, extent, split, -0.22, 0.18)
    return jnp.clip(strengthened(entries, jax.random.fold_in(key, 3), *heavy), -most, most).astype(kind)


def setup_inputs(seed: int = 0) -> dict:
    streams_of = jax.random.split(jax.random.key(seed), 12)
    return {
        "hidden_in": draw_hidden_in(jax.random.fold_in(streams_of[11], 71), 0),
        "self_gain": jnp.clip(1.0 + 0.18 * jax.random.normal(streams_of[1], (D,), jnp.float32), 0.099609375, 1.8984375).astype(jnp.bfloat16),
        "w_self": centred(streams_of[2], (D, 3, HW), D ** -0.5, 0.09375, ((2, 32),)),
        "w_self_out": gaussian_with(streams_of[3], (HW, D), HW ** -0.5, 0.1875, ((0, 32),), (0, 1, 32, 2.75)),
        "cross_gain": jnp.clip(1.0 + 0.18 * jax.random.normal(streams_of[4], (D,), jnp.float32), 0.099609375, 1.8984375).astype(jnp.bfloat16),
        "w_cross_q": centred(streams_of[5], (D, HW), D ** -0.5, 0.09375, ((0, 32),)),
        "w_cross_out": centred(streams_of[6], (HW, D), HW ** -0.5, 0.09375, ((1, 32),)),
        "cache_kv": draw_cache_kv(jax.random.fold_in(streams_of[11], 71), 0),
        "memory_kv": draw_memory_kv(jax.random.fold_in(streams_of[11], 71), 0),
        "parents": place_ends(skewed_ids(streams_of[9], (HYPS,), HYPS, 2), jax.random.fold_in(streams_of[9], 3), 0, HYPS - 1).astype(jnp.int32),
        "prefix_len": draw_prefix_len(jax.random.fold_in(streams_of[11], 71), 0),
    }


NEG = -1e+30
EPS = 1e-06

def soft_parts(scores, visible):
    masked = jnp.where(visible, scores, NEG)
    maxima = lax.optimization_barrier(jnp.max(masked, axis=-1))
    weights = jnp.where(visible, jnp.exp(masked - maxima[..., None]), 0.0)
    rounded = weights.astype(jnp.bfloat16)
    totals = lax.optimization_barrier(jnp.sum(rounded.astype(jnp.float32), axis=-1))
    return (maxima, totals, rounded)

def finish_cross(maxima, totals, weighted):
    highest = lax.optimization_barrier(jnp.max(maxima, axis=0))
    factor = jnp.exp(maxima - highest[None])
    numerator = lax.optimization_barrier(jnp.sum(factor[..., None] * weighted, axis=0))
    denominator = lax.optimization_barrier(jnp.sum(factor * totals, axis=0))
    attended = numerator / denominator[..., None]
    return attended.reshape(attended.shape[0], -1).astype(jnp.bfloat16)

def reference(hidden_in, self_gain, w_self, w_self_out, cross_gain, w_cross_q, w_cross_out, cache_kv, memory_kv, parents, prefix_len):
    head_width = HEADS * HEAD_DIM
    score_scale = HEAD_DIM ** (-0.5)
    inputs = hidden_in.astype(jnp.float32)
    self_mean = lax.optimization_barrier(jnp.mean(inputs * inputs, axis=1))
    scaled = (inputs * self_gain.astype(jnp.float32)).astype(jnp.bfloat16)
    flat_weight = w_self.reshape(D, 3 * head_width)
    projected = (jnp.dot(scaled, flat_weight, preferred_element_type=jnp.float32) * lax.rsqrt(self_mean + EPS)[:, None]).astype(jnp.bfloat16)
    projected = projected.reshape(HYPS, 3, HEADS, HEAD_DIM)
    queries = projected[:, 0].astype(jnp.float32)
    own_keys = projected[:, 1].astype(jnp.float32)
    own_value = projected[:, 2].astype(jnp.float32)
    own_score = lax.optimization_barrier(jnp.sum(queries * own_keys, axis=-1)) * score_scale
    visible = jnp.arange(CACHE, dtype=jnp.int32)[None, :] < prefix_len[:, None]

    def head_stats(head_index):
        cache_head = lax.dynamic_index_in_dim(cache_kv, head_index, axis=2, keepdims=False)
        cache_head = jnp.take(cache_head, parents, axis=0).astype(jnp.float32)
        query = lax.dynamic_index_in_dim(queries, head_index, axis=1, keepdims=False)
        scores = jnp.einsum('id,ipd->ip', query, cache_head[..., :HEAD_DIM]) * score_scale
        maxima, totals, rounded = soft_parts(scores, visible)
        weighted = jnp.einsum('ip,ipd->id', rounded.astype(jnp.float32), cache_head[..., HEAD_DIM:])
        return (maxima, totals, weighted)
    cache_max, cache_total, cache_sum = lax.map(head_stats, jnp.arange(HEADS, dtype=jnp.int32))
    cache_max = cache_max.T
    cache_total = cache_total.T
    cache_sum = jnp.transpose(cache_sum, (1, 0, 2))
    highest = jnp.maximum(cache_max, own_score)
    factor = jnp.exp(cache_max - highest)
    own_weight = jnp.exp(own_score - highest)
    numerator = cache_sum * factor[..., None] + own_weight[..., None] * own_value
    denominator = cache_total * factor + own_weight
    self_attended = (numerator / denominator[..., None]).reshape(HYPS, head_width).astype(jnp.bfloat16)
    middle = (inputs + jnp.dot(self_attended, w_self_out, preferred_element_type=jnp.float32)).astype(jnp.bfloat16)
    middle_wide = middle.astype(jnp.float32)
    cross_mean = lax.optimization_barrier(jnp.mean(middle_wide * middle_wide, axis=1))
    cross_scaled = (middle_wide * cross_gain.astype(jnp.float32)).astype(jnp.bfloat16)
    cross_queries = (jnp.dot(cross_scaled, w_cross_q, preferred_element_type=jnp.float32) * lax.rsqrt(cross_mean + EPS)[:, None]).astype(jnp.bfloat16)
    cross_heads = cross_queries.reshape(HYPS, HEADS, HEAD_DIM).astype(jnp.float32)

    def memory_block(block_index):
        first_row = (block_index * MEM_DEV).astype(jnp.int32)
        memory_part = lax.dynamic_slice_in_dim(memory_kv, first_row, MEM_DEV, 0).astype(jnp.float32)
        key_heads = memory_part[:, :head_width].reshape(MEM_DEV, HEADS, HEAD_DIM)
        value_heads = memory_part[:, head_width:].reshape(MEM_DEV, HEADS, HEAD_DIM)
        scores = jnp.einsum('ihd,phd->ihp', cross_heads, key_heads) * score_scale
        every = jnp.ones((1, 1, MEM_DEV), dtype=jnp.bool_)
        maxima, totals, rounded = soft_parts(scores, every)
        weighted = jnp.einsum('ihp,phd->ihd', rounded.astype(jnp.float32), value_heads)
        return (maxima, totals, weighted)
    memory_max, memory_total, memory_sum = lax.map(memory_block, jnp.arange(N_BLK, dtype=jnp.int32))
    cross_attended = finish_cross(memory_max, memory_total, memory_sum)
    return (middle_wide + jnp.dot(cross_attended, w_cross_out, preferred_element_type=jnp.float32)).astype(jnp.bfloat16)
```

```python
import functools

import jax
import jax.numpy as jnp
from jax import lax
from jax.experimental import pallas as pl
from jax.experimental.pallas import tpu as pltpu
from jax.sharding import PartitionSpec as P

MESH = pl.DeviceIdType.MESH
F32 = jnp.float32
BF16 = jnp.bfloat16
NEG = -1e30
EPS = 1e-06
LANES = 128
VMEM_BYTES = 64000000


def aligned(block, size=LANES):
    return pl.ds(pl.multiple_of(block * size, size), size)


def split3(x):
    high = x.astype(BF16).astype(F32)
    rest = x - high
    middle = rest.astype(BF16).astype(F32)
    return high, middle, rest - middle


def place(index, pieces):
    out = jnp.zeros(index.shape, F32)
    for at, piece in enumerate(pieces):
        out = jnp.where(index == at, piece, out)
    return out


NT = (((1,), (1,)), ((), ()))


def kernel(
    nb, nc, d_model,
    hid_ref, sgain_ref, cgain_ref, parents_ref, plen_ref,
    wself_hbm, wso_hbm, wcq_hbm, wco_hbm, cache_hbm, mem_hbm,
    out_ref,
    wself, wso, wcq, wco, wcop, cache, mem, vt_mem, kt, vt, lhs_q, lhs_p,
    s_a, g_a, s_c, g_c, s_d, r_d, s_e, r_e, s_f, r_f, s_q, g_q, s_g, r_g, s_h, g_h,
    load_sem,
    a_send, a_recv, c_send, c_recv, d_send, d_recv, e_send, e_recv,
    f_send, f_recv, q_send, q_recv, g_send, g_recv, h_send, h_recv,
):
    rows = hid_ref.shape[0]
    hyps = nb * rows
    half = nc // 2
    groups = half
    score_scale = 64 ** (-0.5)
    b = lax.axis_index("beam")
    c = lax.axis_index("blk")
    core = lax.rem(c, 2)
    partner = c + 1 - 2 * core

    loads = [
        pltpu.make_async_copy(cache_hbm, cache, load_sem.at[0]),
        pltpu.make_async_copy(wself_hbm.at[0], wself.at[:, pl.ds(0, LANES)], load_sem.at[1]),
        pltpu.make_async_copy(wself_hbm.at[1], wself.at[:, pl.ds(LANES, LANES)], load_sem.at[2]),
        pltpu.make_async_copy(wself_hbm.at[2], wself.at[:, pl.ds(2 * LANES, LANES)], load_sem.at[3]),
        pltpu.make_async_copy(mem_hbm, mem, load_sem.at[4]),
        pltpu.make_async_copy(wso_hbm, wso, load_sem.at[5]),
        pltpu.make_async_copy(wcq_hbm, wcq, load_sem.at[6]),
        pltpu.make_async_copy(wco_hbm, wco, load_sem.at[7]),
    ]
    for load in loads:
        load.start()

    barrier = pltpu.get_barrier_semaphore()

    def greet_blk(k, carry):
        pl.semaphore_signal(barrier, inc=1, device_id=(b, lax.rem(c + k, nc)), device_id_type=MESH)
        return carry

    def greet_beam(k, carry):
        pl.semaphore_signal(barrier, inc=1, device_id=(lax.rem(b + k, nb), c), device_id_type=MESH)
        return carry

    lax.fori_loop(1, nc, greet_blk, 0)
    lax.fori_loop(1, nb, greet_beam, 0)

    def remote(src, dst, send, recv, where):
        return pltpu.make_async_remote_copy(
            src_ref=src, dst_ref=dst, send_sem=send, recv_sem=recv, device_id=where, device_id_type=MESH
        )

    def gather_start(src, dst, send, recv):
        mine = dst.at[:, aligned(c)]
        remote(src, mine, send.at[0], recv.at[c], (b, partner)).start()

        def step(k, carry):
            remote(src, mine, send.at[k], recv.at[c], (b, lax.rem(c + 2 * k, nc))).start()
            return carry

        lax.fori_loop(1, half, step, 0)

    def gather_wait(src, dst, send, recv):
        def passed(k, carry):
            source = lax.rem(c + 2 * k, nc)
            block = dst.at[:, aligned(source)]
            remote(src, block, send.at[k], recv.at[source], (b, partner)).wait_recv()
            remote(block, block, send.at[half + k], recv.at[source], (b, partner)).start()
            return carry

        lax.fori_loop(1, half, passed, 0)

        def other(k, carry):
            source = lax.rem(partner + 2 * k, nc)
            block = dst.at[:, aligned(source)]
            remote(src, block, send.at[k], recv.at[source], (b, partner)).wait_recv()
            return carry

        lax.fori_loop(0, half, other, 0)

    def gather_drain(src, dst, send, recv):
        def step(k, carry):
            remote(src, dst.at[:, aligned(c)], send.at[k], recv.at[c], (b, partner)).wait_send()
            return carry

        lax.fori_loop(0, half, step, 0)

        def forwarded(k, carry):
            remote(src, dst.at[:, aligned(c)], send.at[half + k], recv.at[c], (b, partner)).wait_send()
            return carry

        lax.fori_loop(1, half, forwarded, 0)

    def scatter_start(src, dst, send, recv):
        def step(k, carry):
            target = lax.rem(c + k, nc)
            remote(src.at[:, aligned(target)], dst.at[c], send.at[k], recv.at[c], (b, target)).start()
            return carry

        lax.fori_loop(1, nc, step, 0)

    def scatter_sum(src, dst, send, recv):
        def step(k, total):
            source = lax.rem(c + k, nc)
            remote(src.at[:, aligned(c)], dst.at[source], send.at[k], recv.at[source], (b, source)).wait_recv()
            return total + dst[source].astype(F32)

        return lax.fori_loop(1, nc, step, src[:, aligned(c)].astype(F32))

    def scatter_drain(src, dst, send, recv):
        def step(k, carry):
            remote(src.at[:, aligned(c)], dst.at[c], send.at[k], recv.at[c], (b, partner)).wait_send()
            return carry

        lax.fori_loop(1, nc, step, 0)

    first = hid_ref[...]
    s_a[pl.ds(0, rows), :] = first
    gain_rows = jnp.broadcast_to(sgain_ref[...], (16, LANES))
    s_a[pl.ds(rows, 16), :] = gain_rows
    g_a[pl.ds(0, rows), aligned(c)] = first
    g_a[pl.ds(rows, 16), aligned(c)] = gain_rows
    pl.semaphore_wait(barrier, nc + nb - 2)
    gather_start(s_a, g_a, a_send, a_recv)

    loads[0].wait()
    width = 2 * cache.shape[0] // (2 * rows)

    def arrange(r, carry):
        x = cache[aligned(r, width), :].astype(F32)
        rolled = pltpu.roll(x, 64, 1)
        even = lax.rem(lax.broadcasted_iota(jnp.int32, x.shape, 0), 2) == 0
        low = lax.broadcasted_iota(jnp.int32, x.shape, 1) < 64
        keys = jnp.where(even, jnp.where(low, x, 0.0), jnp.where(low, 0.0, rolled))
        values = jnp.where(even, jnp.where(low, rolled, 0.0), jnp.where(low, 0.0, x))
        kt[:, aligned(r)] = keys.astype(BF16)
        vt[aligned(r, width), :] = values.astype(BF16)
        return carry

    lax.fori_loop(0, rows, arrange, 0)
    local_wide = jnp.broadcast_to(parents_ref[...], (LANES, hyps)).T - b * rows
    plen_wide = jnp.broadcast_to(plen_ref[...], (LANES, hyps)).T
    for load in loads[1:4]:
        load.wait()
    gather_wait(s_a, g_a, a_send, a_recv)

    wide = g_a[pl.ds(0, rows), :].astype(F32)
    gain = g_a[pl.ds(rows, 16), :].astype(F32)[0:1, :]
    self_mean = jnp.sum(wide * wide, axis=1, keepdims=True) * (1.0 / d_model)
    scaled = (wide * gain).astype(BF16)
    projected = jnp.dot(scaled, wself[...], preferred_element_type=F32) * lax.rsqrt(self_mean + EPS)
    projected = projected.astype(BF16)
    queries = projected[:, :LANES]

    s_c[...] = queries
    g_c[aligned(b, rows), :] = queries
    my_queries = g_c.at[aligned(b, rows), :]

    def send_c(k, carry):
        remote(s_c, my_queries, c_send.at[k], c_recv.at[b], (lax.rem(b + k, nb), c)).start()
        return carry

    lax.fori_loop(1, nb, send_c, 0)

    own_values = projected[:, 2 * LANES :].astype(F32)
    products = queries.astype(F32) * projected[:, LANES : 2 * LANES].astype(F32)
    low = lax.broadcasted_iota(jnp.int32, products.shape, 1) < 64
    own_0 = jnp.sum(jnp.where(low, products, 0.0), axis=1, keepdims=True) * score_scale
    own_1 = jnp.sum(jnp.where(low, 0.0, products), axis=1, keepdims=True) * score_scale

    loads[4].wait()
    head_width = mem.shape[1] // 2

    def turn(g, carry):
        block = mem[:, pl.ds(pl.multiple_of(head_width + g * 256, 256), 256)]
        vt_mem[aligned(g, 256), :] = block.T
        return carry

    lax.fori_loop(0, groups, turn, 0)

    def wait_c(k, carry):
        source = lax.rem(b + k, nb)
        remote(s_c, g_c.at[aligned(source, rows), :], c_send.at[k], c_recv.at[source], (source, c)).wait_recv()
        return carry

    lax.fori_loop(1, nb, wait_c, 0)

    all_queries = g_c[...].astype(F32)

    def spread_q(r, carry):
        lhs_q[:, aligned(r)] = jnp.where(local_wide == r, all_queries, 0.0).astype(BF16)
        return carry

    lax.fori_loop(0, rows, spread_q, 0)
    scores = lax.dot_general(lhs_q[...], kt[...], NT, preferred_element_type=F32) * score_scale
    lane = lax.broadcasted_iota(jnp.int32, scores.shape, 1)
    even = lax.rem(lane, 2) == 0
    tiles = width // LANES
    visible = lax.div(lane, 2) < jnp.concatenate([plen_wide] * tiles, axis=1)
    masked = jnp.where(visible, scores, NEG)
    max_0 = jnp.max(jnp.where(even, masked, NEG), axis=1, keepdims=True)
    max_1 = jnp.max(jnp.where(even, NEG, masked), axis=1, keepdims=True)
    weights = jnp.where(visible, jnp.exp(masked - jnp.where(even, max_0, max_1)), 0.0).astype(BF16).astype(F32)
    total_0 = jnp.sum(jnp.where(even, weights, 0.0), axis=1, keepdims=True)
    total_1 = jnp.sum(jnp.where(even, 0.0, weights), axis=1, keepdims=True)
    local_width = jnp.concatenate([local_wide] * tiles, axis=1)

    def spread_p(r, carry):
        lhs_p[:, aligned(r, width)] = jnp.where(local_width == r, weights, 0.0).astype(BF16)
        return carry

    lax.fori_loop(0, rows, spread_p, 0)
    summed = jnp.dot(lhs_p[...], vt[...], preferred_element_type=F32)
    lane = lax.broadcasted_iota(jnp.int32, summed.shape, 1)
    here = (local_wide >= 0) & (local_wide < rows)
    part = summed / jnp.where(lane < 64, total_0, total_1)
    pieces = split3(max_0 + jnp.log(total_0)) + split3(max_1 + jnp.log(total_1))
    s_d[:, pl.ds(0, LANES)] = part.astype(BF16)
    s_d[:, pl.ds(LANES, LANES)] = jnp.where(here, place(lane, pieces), 0.0).astype(BF16)

    def send_d(k, carry):
        target = lax.rem(b + k, nb)
        remote(s_d.at[aligned(target, rows), :], r_d.at[b], d_send.at[k], d_recv.at[b], (target, c)).start()
        return carry

    lax.fori_loop(1, nb, send_d, 0)

    loads[7].wait()
    quarter = 2 * rows

    def permute(g, carry):
        for which in range(2):
            for head in range(4):
                wcop[pl.ds(pl.multiple_of(g * 256 + which * 128 + head * 32, 32), 32), :] = wco[
                    pl.ds(pl.multiple_of(g * 256 + head * 64 + which * 32, 32), 32), :
                ]
        return carry

    lax.fori_loop(0, groups, permute, 0)
    loads[5].wait()
    loads[6].wait()

    def wait_d(k, total):
        source = lax.rem(b + k, nb)
        remote(s_d.at[aligned(b, rows), :], r_d.at[source], d_send.at[k], d_recv.at[source], (source, c)).wait_recv()
        return total + r_d[source].astype(F32)

    back = lax.fori_loop(1, nb, wait_d, s_d[aligned(b, rows), :].astype(F32))
    stats = back[:, LANES:]
    log_0 = stats[:, 0:1] + stats[:, 1:2] + stats[:, 2:3]
    log_1 = stats[:, 3:4] + stats[:, 4:5] + stats[:, 5:6]
    cache_log = jnp.where(low, log_0, log_1)
    own_log = jnp.where(low, own_0, own_1)
    top = jnp.maximum(cache_log, own_log)
    cache_weight = jnp.exp(cache_log - top)
    own_weight = jnp.exp(own_log - top)
    attended = (cache_weight * back[:, :LANES] + own_weight * own_values) / (cache_weight + own_weight)

    s_e[...] = jnp.dot(attended.astype(BF16), wso[...], preferred_element_type=F32).astype(BF16)
    scatter_start(s_e, r_e, e_send, e_recv)
    mixed = scatter_sum(s_e, r_e, e_send, e_recv)
    middle = (first.astype(F32) + mixed).astype(BF16).astype(F32)

    cross_scaled = (middle * cgain_ref[...].astype(F32)).astype(BF16)
    s_f[...] = jnp.dot(cross_scaled, wcq[...], preferred_element_type=F32).astype(BF16)
    scatter_start(s_f, r_f, f_send, f_recv)
    squares = jnp.broadcast_to(jnp.sum(middle * middle, axis=1, keepdims=True), (rows, LANES))
    squares = jnp.concatenate([squares] * (LANES // rows), axis=0).T[0:1, :]
    row16 = lax.broadcasted_iota(jnp.int32, (16, LANES), 0)
    square_rows = place(row16, split3(squares)).astype(BF16)
    s_q[pl.ds(rows, 16), :] = square_rows
    g_q[pl.ds(rows, 16), aligned(c)] = square_rows
    raw = scatter_sum(s_f, r_f, f_send, f_recv).astype(BF16)
    s_q[pl.ds(0, rows), :] = raw
    g_q[pl.ds(0, rows), aligned(c)] = raw
    gather_start(s_q, g_q, q_send, q_recv)
    gather_wait(s_q, g_q, q_send, q_recv)

    def add_squares(k, total):
        return total + g_q[pl.ds(rows, 16), aligned(k)].astype(F32)

    sums = lax.fori_loop(0, nc, add_squares, jnp.zeros((16, LANES), F32))
    mean = (sums[0:1, :] + sums[1:2, :] + sums[2:3, :]) * (1.0 / d_model)
    factor = lax.rsqrt(mean + EPS) * score_scale

    own_block = (
        lax.div(lax.broadcasted_iota(jnp.int32, (LANES, 256), 0), rows)
        == lax.div(lax.broadcasted_iota(jnp.int32, (LANES, 256), 1), 64)
    )
    lane_head = lax.div(lax.broadcasted_iota(jnp.int32, (64, LANES), 1), rows)

    def remember(i, carry):
        g = lax.rem(lax.div(c, 2) + 1 + i, groups)
        query = g_q[pl.ds(0, rows), aligned(g, 256)].astype(F32)
        query = jnp.where(own_block, jnp.concatenate([query] * 4, axis=0), 0.0).astype(BF16)
        score = lax.dot_general(mem[:, aligned(g, 256)], query, NT, preferred_element_type=F32) * factor
        most = jnp.max(score, axis=0, keepdims=True)
        weight = jnp.exp(score - most).astype(BF16)
        total = jnp.sum(weight.astype(F32), axis=0, keepdims=True)
        spread = jnp.dot(vt_mem[aligned(g, 256), :], weight, preferred_element_type=F32)
        taken = jnp.where(lane_head == 0, spread[0:64], 0.0)
        for head in range(1, 4):
            taken = jnp.where(lane_head == head, spread[head * 64 : head * 64 + 64], taken)
        stat = place(row16, split3(most) + split3(total)).astype(BF16)
        for which in range(2):
            target = 2 * g + which
            s_g[target, pl.ds(0, 32), :] = taken[which * 32 : which * 32 + 32].astype(BF16)
            s_g[target, pl.ds(32, 16), :] = stat

            @pl.when(target != c)
            def _():
                remote(
                    s_g.at[target], r_g.at[c], g_send.at[target], g_recv.at[c], (b, target)
                ).start()

        return carry

    lax.fori_loop(0, groups, remember, 0)
    r_g[c] = s_g[c]

    def wait_g(k, top):
        source = lax.rem(c + k, nc)
        remote(s_g.at[c], r_g.at[source], g_send.at[c], g_recv.at[source], (b, source)).wait_recv()
        stat = r_g[source, pl.ds(32, 16), :].astype(F32)
        return jnp.maximum(top, stat[0:1] + stat[1:2] + stat[2:3])

    stat = s_g[c, pl.ds(32, 16), :].astype(F32)
    top = lax.fori_loop(1, nc, wait_g, stat[0:1] + stat[1:2] + stat[2:3])
    over = jnp.zeros((32, LANES), F32)
    under = jnp.zeros((1, LANES), F32)
    for source in range(nc):
        stat = r_g[source, pl.ds(32, 16), :].astype(F32)
        share = jnp.exp(stat[0:1] + stat[1:2] + stat[2:3] - top)
        under = under + share * (stat[3:4] + stat[4:5] + stat[5:6])
        over = over + share * r_g[source, pl.ds(0, 32), :].astype(F32)
    turned = (over / under).T
    crossed = jnp.concatenate([turned[rows * head : rows * head + rows] for head in range(4)], axis=1).astype(BF16)

    s_h[...] = crossed
    g_h[:, aligned(c)] = crossed
    gather_start(s_h, g_h, h_send, h_recv)
    gather_wait(s_h, g_h, h_send, h_recv)
    out_ref[...] = (middle + jnp.dot(g_h[...], wcop[...], preferred_element_type=F32)).astype(BF16)

    gather_drain(s_a, g_a, a_send, a_recv)
    gather_drain(s_q, g_q, q_send, q_recv)
    gather_drain(s_h, g_h, h_send, h_recv)
    scatter_drain(s_e, r_e, e_send, e_recv)
    scatter_drain(s_f, r_f, f_send, f_recv)

    def drain_beam(k, carry):
        remote(s_c, my_queries, c_send.at[k], c_recv.at[b], (b, partner)).wait_send()
        remote(s_d.at[aligned(b, rows), :], r_d.at[b], d_send.at[k], d_recv.at[b], (b, partner)).wait_send()
        return carry

    lax.fori_loop(1, nb, drain_beam, 0)

    def drain_g(k, carry):
        target = lax.rem(c + k, nc)
        remote(s_g.at[target], r_g.at[c], g_send.at[target], g_recv.at[c], (b, target)).wait_send()
        return carry

    lax.fori_loop(1, nc, drain_g, 0)


def body(
    nb, nc, hidden_in, self_gain, w_self, w_self_out, cross_gain, w_cross_q, w_cross_out, cache_kv, memory_kv, parents, prefix_len
):
    rows = hidden_in.shape[0]
    d_model = w_self.shape[0]
    hyps = nb * rows
    cache_rows = cache_kv.shape[0] * cache_kv.shape[1] * cache_kv.shape[2]
    mem_count, mem_width = memory_kv.shape
    width = cache_rows // rows
    vmem = pl.BlockSpec(memory_space=pltpu.VMEM)
    hbm = pl.BlockSpec(memory_space=pl.ANY)
    wide = nc * LANES

    def v(*shape):
        return pltpu.VMEM(shape, BF16)

    def sems(count):
        return pltpu.SemaphoreType.DMA((count,))

    return pl.pallas_call(
        functools.partial(kernel, nb, nc, d_model),
        out_shape=jax.ShapeDtypeStruct((rows, LANES), BF16),
        in_specs=[vmem] * 5 + [hbm] * 6,
        out_specs=vmem,
        scratch_shapes=[
            v(d_model, 3 * LANES), v(LANES, wide), v(LANES, mem_width // 2), v(mem_width // 2, LANES), v(mem_width // 2, LANES),
            v(cache_rows, LANES), v(mem_count, mem_width), v(mem_width // 2, mem_count),
            v(width, rows * LANES), v(cache_rows, LANES), v(hyps, rows * LANES), v(hyps, rows * width),
            v(rows + 16, LANES), v(rows + 16, wide),
            v(rows, LANES), v(hyps, LANES),
            v(hyps, 2 * LANES), v(nb, rows, 2 * LANES),
            v(rows, wide), v(nc, rows, LANES),
            v(rows, wide), v(nc, rows, LANES),
            v(rows + 16, LANES), v(rows + 16, wide),
            v(nc, 48, LANES), v(nc, 48, LANES),
            v(rows, LANES), v(rows, wide),
            sems(8),
            sems(nc), sems(nc), sems(nb), sems(nb), sems(nb), sems(nb), sems(nc), sems(nc),
            sems(nc), sems(nc), sems(nc), sems(nc), sems(nc), sems(nc), sems(nc), sems(nc),
        ],
        compiler_params=pltpu.CompilerParams(
            collective_id=0, has_side_effects=True, vmem_limit_bytes=VMEM_BYTES
        ),
    )(
        hidden_in,
        self_gain.reshape(1, LANES),
        cross_gain.reshape(1, LANES),
        parents.reshape(1, hyps),
        prefix_len.reshape(1, hyps),
        jnp.transpose(w_self, (1, 0, 2)),
        w_self_out,
        w_cross_q,
        w_cross_out,
        cache_kv.reshape(cache_rows, LANES),
        memory_kv,
    )


def solution(mesh):
    return jax.shard_map(
        functools.partial(body, mesh.shape["beam"], mesh.shape["blk"]),
        mesh=mesh,
        in_specs=(
            P("beam", "blk"),
            P("blk"),
            P(None, None, "blk"),
            P("blk", None),
            P("blk"),
            P("blk", None),
            P(None, "blk"),
            P("beam", None, "blk", None),
            P("blk", None),
            P(),
            P(),
        ),
        out_specs=P("beam", "blk"),
        check_vma=False,
    )
```

```python
import functools

import jax
import jax.numpy as jnp
from jax import lax
from jax.experimental import pallas as pl
from jax.experimental.pallas import tpu as pltpu
from jax.sharding import PartitionSpec as P

MESH = pl.DeviceIdType.MESH
F32 = jnp.float32
BF16 = jnp.bfloat16
NEG = -1e30
EPS = 1e-06
LANES = 128
VMEM_BYTES = 64000000


def aligned(block, size=LANES):
    return pl.ds(pl.multiple_of(block * size, size), size)


def split3(x):
    high = x.astype(BF16).astype(F32)
    rest = x - high
    middle = rest.astype(BF16).astype(F32)
    return high, middle, rest - middle


def place(index, pieces):
    out = jnp.zeros(index.shape, F32)
    for at, piece in enumerate(pieces):
        out = jnp.where(index == at, piece, out)
    return out


NT = (((1,), (1,)), ((), ()))


def kernel(
    nb, nc, d_model,
    hid_ref, sgain_ref, cgain_ref, parents_ref, plen_ref,
    wself_hbm, wso_hbm, wcq_hbm, wco_hbm, cache_hbm, mem_hbm,
    out_ref,
    wself, wso, wcq, wco, cache, keys, values, vt_mem, kt, vt, lhs_q, acc,
    s_a, g_a, s_x, g_x, s_c, g_c, s_d, r_d, s_t, g_t, s_e, r_e, s_m, g_m, s_f, r_f, s_q, g_q, s_g, r_g, s_h, g_h,
    load_sem, swap_send, swap_recv,
    a_send, a_recv, c_send, c_recv, d_send, d_recv, e_send, e_recv,
    f_send, f_recv, q_send, q_recv, g_send, g_recv, h_send, h_recv,
):
    rows = hid_ref.shape[0]
    hyps = nb * rows
    half = nc // 2
    groups = half // 2
    score_scale = 64 ** (-0.5)
    head_width = mem_hbm.shape[1] // 2
    mem_rows = mem_hbm.shape[0]
    b = lax.axis_index("beam")
    c = lax.axis_index("blk")
    chip = lax.div(c, 2)
    core = lax.rem(c, 2)
    partner = c + 1 - 2 * core
    other_core = 1 - core
    steps = sorted(range(1, half), key=lambda k: -min(k % 8, 8 - k % 8))

    loads = [
        pltpu.make_async_copy(cache_hbm, cache, load_sem.at[0]),
        pltpu.make_async_copy(wself_hbm.at[0], wself.at[:, pl.ds(0, LANES)], load_sem.at[1]),
        pltpu.make_async_copy(wself_hbm.at[1], wself.at[:, pl.ds(LANES, LANES)], load_sem.at[2]),
        pltpu.make_async_copy(wself_hbm.at[2], wself.at[:, pl.ds(2 * LANES, LANES)], load_sem.at[3]),
        pltpu.make_async_copy(wco_hbm, wco, load_sem.at[4]),
    ]
    for load in loads:
        load.start()
    loaded = set()
    drains = []

    def ready(*which):
        for at in which:
            loads[at].wait()
            loaded.add(at)

    shared = [
        (wso_hbm, 0, wso, LANES), (wcq_hbm, 0, wcq, LANES),
        (mem_hbm, 0, keys, mem_rows), (mem_hbm, nc, values, mem_rows),
    ]

    def keep(g, carry):
        for at, (source, offset, target, height) in enumerate(shared):
            pltpu.make_async_copy(
                source.at[:, aligned(offset + 2 * g + core)],
                target.at[aligned(core, height), aligned(g)],
                load_sem.at[5 + at],
            ).start()
        return carry

    lax.fori_loop(0, half, keep, 0)

    barrier = pltpu.get_barrier_semaphore()

    def greet_blk(k, carry):
        pl.semaphore_signal(barrier, inc=1, device_id=(b, lax.rem(c + 2 * k, nc)), device_id_type=MESH)
        return carry

    def greet_beam(k, carry):
        pl.semaphore_signal(barrier, inc=1, device_id=(lax.rem(b + k, nb), c), device_id_type=MESH)
        return carry

    lax.fori_loop(1, half, greet_blk, 0)
    lax.fori_loop(1, nb, greet_beam, 0)
    pl.semaphore_signal(barrier, inc=1, device_id=(b, partner), device_id_type=MESH)

    def remote(src, dst, send, recv, where):
        return pltpu.make_async_remote_copy(
            src_ref=src, dst_ref=dst, send_sem=send, recv_sem=recv, device_id=where, device_id_type=MESH
        )

    def peer(k):
        return (b, lax.rem(c + 2 * k, nc))

    def chip_at(k):
        return lax.rem(chip + k, half)

    def swap_start():
        def step(at, g, carry):
            source, offset, target, height = shared[at]
            remote(
                source.at[:, aligned(offset + 2 * g + other_core)],
                target.at[aligned(core, height), aligned(g)],
                swap_send.at[at], swap_recv.at[at], (b, partner),
            ).start()
            return carry

        for at in range(len(shared)):
            lax.fori_loop(0, half, functools.partial(step, at), 0)

    def swapped(at, which):
        source, offset, target, height = shared[at]
        return remote(
            target.at[aligned(which, height), :], target.at[aligned(which, height), :],
            swap_send.at[at], swap_recv.at[at], (b, partner),
        )

    def swap_wait(at):
        source, offset, target, height = shared[at]
        mine = target.at[aligned(core, height), :]
        pltpu.make_async_copy(mine, mine, load_sem.at[5 + at]).wait()
        swapped(at, other_core).wait_recv()

    def swap_drain():
        for at in range(len(shared)):
            swapped(at, core).wait_send()

    def pair_start(src, dst, at):
        remote(src, dst.at[:, aligned(core)], swap_send.at[at], swap_recv.at[at], (b, partner)).start()
        drains.append(lambda: remote(src, dst.at[:, aligned(core)], swap_send.at[at], swap_recv.at[at], (b, partner)).wait_send())

    def pair_wait(src, dst, at):
        remote(src, dst.at[:, aligned(other_core)], swap_send.at[at], swap_recv.at[at], (b, partner)).wait_recv()

    def gather_start(src, dst, send, recv):
        mine = dst.at[:, aligned(c)]
        for k in steps:
            remote(src, mine, send.at[k], recv.at[c], peer(k)).start()
        remote(src, mine, send.at[0], recv.at[c], (b, partner)).start()
        drains.append(functools.partial(gather_drain, src, dst, send, recv))

    def gather_pass(src, dst, send, recv):
        for k in steps:
            source = lax.rem(c + 2 * (half - k), nc)
            block = dst.at[:, aligned(source)]
            remote(src, block, send.at[k], recv.at[source], (b, partner)).wait_recv()
            remote(block, block, send.at[half + k], recv.at[source], (b, partner)).start()

    def gather_wait(src, dst, send, recv):
        def other(k, carry):
            source = lax.rem(partner + 2 * k, nc)
            block = dst.at[:, aligned(source)]
            remote(src, block, send.at[0], recv.at[source], (b, partner)).wait_recv()
            return carry

        lax.fori_loop(0, half, other, 0)

    def gather_drain(src, dst, send, recv):
        def step(k, carry):
            remote(src, dst.at[:, aligned(c)], send.at[k], recv.at[c], (b, partner)).wait_send()
            return carry

        lax.fori_loop(0, half, step, 0)

        def forwarded(k, carry):
            remote(src, dst.at[:, aligned(c)], send.at[half + k], recv.at[c], (b, partner)).wait_send()
            return carry

        lax.fori_loop(1, half, forwarded, 0)

    def scatter_start(src, dst, send, recv):
        for k in steps:
            remote(src.at[:, aligned(chip_at(k))], dst.at[chip], send.at[k], recv.at[chip], peer(k)).start()
        drains.append(functools.partial(simple_drain, src.at[:, aligned(chip)], send))

    def simple_drain(block, send):
        def step(k, carry):
            remote(block, block, send.at[k], send.at[k], (b, partner)).wait_send()
            return carry

        lax.fori_loop(1, half, step, 0)

    def scatter_sum(src, dst, send, recv):
        total = src[:, aligned(chip)].astype(F32)
        for k in steps:
            source = chip_at(half - k)
            remote(src.at[:, aligned(chip)], dst.at[source], send.at[k], recv.at[source], (b, partner)).wait_recv()
            total = total + dst[source].astype(F32)
        return total

    first = hid_ref[...]
    gain_rows = jnp.broadcast_to(sgain_ref[...].astype(F32), (8, LANES)).astype(BF16)
    s_a[pl.ds(0, rows), :] = first
    s_a[pl.ds(rows, 8), :] = gain_rows
    g_a[pl.ds(0, rows), aligned(c)] = first
    g_a[pl.ds(rows, 8), aligned(c)] = gain_rows
    cgain_rows = jnp.broadcast_to(cgain_ref[...].astype(F32), (8, LANES))
    s_x[...] = cgain_rows
    g_x[:, aligned(core)] = cgain_rows
    pl.semaphore_wait(barrier, half + nb - 1)
    gather_start(s_a, g_a, a_send, a_recv)
    pair_start(s_x, g_x, 4)

    ready(0)
    width = cache.shape[0] // rows

    def arrange(r, carry):
        x = cache[aligned(r, width), :].astype(F32)
        rolled = pltpu.roll(x, 64, 1)
        even = lax.rem(lax.broadcasted_iota(jnp.int32, x.shape, 0), 2) == 0
        low = lax.broadcasted_iota(jnp.int32, x.shape, 1) < 64
        kt[:, aligned(r)] = jnp.where(even, jnp.where(low, x, 0.0), jnp.where(low, 0.0, rolled)).astype(BF16)
        vt[:, aligned(r)] = jnp.where(even, jnp.where(low, rolled, 0.0), jnp.where(low, 0.0, x)).astype(BF16)
        return carry

    lax.fori_loop(0, rows, arrange, 0)
    local_wide = jnp.broadcast_to(parents_ref[...], (LANES, hyps)).T - b * rows
    plen_wide = jnp.broadcast_to(plen_ref[...], (LANES, hyps)).T
    ready(1, 2, 3)
    gather_pass(s_a, g_a, a_send, a_recv)
    swap_start()
    drains.append(swap_drain)
    gather_wait(s_a, g_a, a_send, a_recv)

    wide = g_a[pl.ds(0, rows), :].astype(F32)
    gain = g_a[pl.ds(rows, 8), :].astype(F32)[0:1, :]
    self_scale = lax.rsqrt(jnp.sum(wide * wide, axis=1, keepdims=True) * (1.0 / d_model) + EPS)
    scaled = (wide * gain).astype(BF16)
    queries = (jnp.dot(scaled, wself[:, pl.ds(0, LANES)], preferred_element_type=F32) * self_scale).astype(BF16)

    s_c[...] = queries
    g_c[aligned(b, rows), :] = queries
    my_queries = g_c.at[aligned(b, rows), :]

    def send_c(k, carry):
        remote(s_c, my_queries, c_send.at[k], c_recv.at[b], (lax.rem(b + k, nb), c)).start()
        return carry

    lax.fori_loop(1, nb, send_c, 0)

    def drain_c():
        def step(k, carry):
            remote(s_c, my_queries, c_send.at[k], c_recv.at[b], (b, partner)).wait_send()
            return carry

        lax.fori_loop(1, nb, step, 0)

    drains.append(drain_c)
    projected = jnp.dot(scaled, wself[:, pl.ds(LANES, 2 * LANES)], preferred_element_type=F32) * self_scale
    projected = projected.astype(BF16).astype(F32)
    own_values = projected[:, LANES:]
    products = queries.astype(F32) * projected[:, :LANES]
    low = lax.broadcasted_iota(jnp.int32, products.shape, 1) < 64
    own_0 = jnp.sum(jnp.where(low, products, 0.0), axis=1, keepdims=True) * score_scale
    own_1 = jnp.sum(jnp.where(low, 0.0, products), axis=1, keepdims=True) * score_scale

    def wait_c(k, carry):
        source = lax.rem(b + k, nb)
        remote(s_c, g_c.at[aligned(source, rows), :], c_send.at[k], c_recv.at[source], (source, c)).wait_recv()
        return carry

    lax.fori_loop(1, nb, wait_c, 0)

    all_queries = g_c[...].astype(F32)

    def spread_q(r, carry):
        lhs_q[:, aligned(r)] = jnp.where(local_wide == r, all_queries, 0.0).astype(BF16)
        return carry

    lax.fori_loop(0, rows, spread_q, 0)
    scores = lax.dot_general(lhs_q[...], kt[...], NT, preferred_element_type=F32) * score_scale
    lane = lax.broadcasted_iota(jnp.int32, scores.shape, 1)
    even = lax.rem(lane, 2) == 0
    tiles = width // LANES
    visible = lax.div(lane, 2) < jnp.concatenate([plen_wide] * tiles, axis=1)
    masked = jnp.where(visible, scores, NEG)
    max_0 = jnp.max(jnp.where(even, masked, NEG), axis=1, keepdims=True)
    max_1 = jnp.max(jnp.where(even, NEG, masked), axis=1, keepdims=True)
    weights = jnp.where(visible, jnp.exp(masked - jnp.where(even, max_0, max_1)), 0.0).astype(BF16)
    lhs_q[:, pl.ds(0, width)] = weights
    weights = weights.astype(F32)
    total_0 = jnp.sum(jnp.where(even, weights, 0.0), axis=1, keepdims=True)
    total_1 = jnp.sum(jnp.where(even, 0.0, weights), axis=1, keepdims=True)
    acc[...] = jnp.zeros(acc.shape, F32)

    def select(r, carry):
        both = jnp.dot(lhs_q[:, pl.ds(0, width)], vt[:, aligned(r, 2 * LANES)], preferred_element_type=F32)
        picked = jnp.where(local_wide == 2 * r, both[:, :LANES], acc[...])
        acc[...] = jnp.where(local_wide == 2 * r + 1, both[:, LANES:], picked)
        return carry

    lax.fori_loop(0, rows // 2, select, 0)
    summed = acc[...]
    lane = lax.broadcasted_iota(jnp.int32, summed.shape, 1)
    here = (local_wide >= 0) & (local_wide < rows)
    part = summed / jnp.where(lane < 64, total_0, total_1)
    pieces = split3(max_0 + jnp.log(total_0)) + split3(max_1 + jnp.log(total_1))
    s_d[:, pl.ds(0, LANES)] = part.astype(BF16)
    s_d[:, pl.ds(LANES, LANES)] = jnp.where(here, place(lane, pieces), 0.0).astype(BF16)

    def send_d(k, carry):
        target = lax.rem(b + k, nb)
        remote(s_d.at[aligned(target, rows), :], r_d.at[b], d_send.at[k], d_recv.at[b], (target, c)).start()
        return carry

    lax.fori_loop(1, nb, send_d, 0)

    def drain_d():
        def step(k, carry):
            remote(s_d.at[aligned(b, rows), :], r_d.at[b], d_send.at[k], d_recv.at[b], (b, partner)).wait_send()
            return carry

        lax.fori_loop(1, nb, step, 0)

    drains.append(drain_d)
    swap_wait(0)
    swap_wait(1)
    ready(4)

    def wait_d(k, total):
        source = lax.rem(b + k, nb)
        remote(s_d.at[aligned(b, rows), :], r_d.at[source], d_send.at[k], d_recv.at[source], (source, c)).wait_recv()
        return total + r_d[source].astype(F32)

    back = lax.fori_loop(1, nb, wait_d, s_d[aligned(b, rows), :].astype(F32))
    stats = back[:, LANES:]
    log_0 = stats[:, 0:1] + stats[:, 1:2] + stats[:, 2:3]
    log_1 = stats[:, 3:4] + stats[:, 4:5] + stats[:, 5:6]
    cache_log = jnp.where(low, log_0, log_1)
    own_log = jnp.where(low, own_0, own_1)
    top = jnp.maximum(cache_log, own_log)
    cache_weight = jnp.exp(cache_log - top)
    own_weight = jnp.exp(own_log - top)
    attended = (cache_weight * back[:, :LANES] + own_weight * own_values) / (cache_weight + own_weight)
    attended = attended.astype(BF16)
    s_t[...] = attended
    g_t[:, aligned(core)] = attended
    pair_start(s_t, g_t, 5)
    pair_wait(s_t, g_t, 5)

    s_e[...] = jnp.dot(g_t[...], wso[...], preferred_element_type=F32).astype(BF16)
    scatter_start(s_e, r_e, e_send, e_recv)
    swap_wait(2)
    swap_wait(3)

    def turn(g, carry):
        vt_mem[aligned(g, 256), :] = values[:, aligned(g, 256)].T
        return carry

    lax.fori_loop(0, groups, turn, 0)
    mixed = scatter_sum(s_e, r_e, e_send, e_recv)
    middle_16 = (first.astype(F32) + mixed).astype(BF16)
    middle = middle_16.astype(F32)

    s_m[...] = middle_16
    g_m[:, aligned(core)] = middle_16
    pair_start(s_m, g_m, 6)
    pair_wait(s_x, g_x, 4)
    pair_wait(s_m, g_m, 6)
    both_middle = g_m[...].astype(F32)
    cross_scaled = (both_middle * g_x[0:1, :]).astype(BF16)
    s_f[...] = jnp.dot(cross_scaled, wcq[...], preferred_element_type=F32).astype(BF16)
    scatter_start(s_f, r_f, f_send, f_recv)
    squares = jnp.broadcast_to(jnp.sum(both_middle * both_middle, axis=1, keepdims=True), (rows, LANES))
    squares = jnp.concatenate([squares] * (LANES // rows), axis=0).T[0:1, :]
    row8 = lax.broadcasted_iota(jnp.int32, (8, LANES), 0)
    square_rows = place(row8, split3(squares)).astype(BF16)
    s_q[pl.ds(rows, 8), :] = square_rows
    g_q[pl.ds(rows, 8), aligned(chip)] = square_rows
    raw = scatter_sum(s_f, r_f, f_send, f_recv).astype(BF16)
    s_q[pl.ds(0, rows), :] = raw
    g_q[pl.ds(0, rows), aligned(chip)] = raw

    for k in steps:
        remote(s_q, g_q.at[:, aligned(chip)], q_send.at[k], q_recv.at[chip], peer(k)).start()
    drains.append(functools.partial(simple_drain, s_q, q_send))
    for k in steps:
        source = chip_at(half - k)
        remote(s_q, g_q.at[:, aligned(source)], q_send.at[k], q_recv.at[source], (b, partner)).wait_recv()
    sums = jnp.zeros((8, LANES), F32)
    for k in range(half):
        sums = sums + g_q[pl.ds(rows, 8), pl.ds(k * LANES, LANES)].astype(F32)
    mean = (sums[0:1, :] + sums[1:2, :] + sums[2:3, :]) * (1.0 / d_model)
    factor = lax.rsqrt(mean + EPS) * score_scale

    own_block = (
        lax.div(lax.broadcasted_iota(jnp.int32, (LANES, 256), 0), rows)
        == lax.div(lax.broadcasted_iota(jnp.int32, (LANES, 256), 1), 64)
    )
    lane_head = lax.div(lax.broadcasted_iota(jnp.int32, (64, LANES), 1), rows)
    left = lax.broadcasted_iota(jnp.int32, (32, LANES), 1) < 64

    def deliver(g):
        for which in range(2):
            target = 2 * g + which

            @pl.when(target != chip)
            def _():
                remote(
                    s_g.at[target], r_g.at[chip], g_send.at[target], g_recv.at[chip], (b, 2 * target + core)
                ).start()

    offsets = sorted(range(groups), key=lambda k: -min(k % 4, 4 - k % 4) if k else 1)
    previous = None
    for offset in offsets:
        g = lax.rem(lax.div(chip, 2) + offset, groups)
        query = g_q[pl.ds(0, rows), aligned(g, 256)].astype(F32)
        query = jnp.where(own_block, jnp.concatenate([query] * 4, axis=0), 0.0).astype(BF16)
        score = lax.dot_general(keys[:, aligned(g, 256)], query, NT, preferred_element_type=F32) * factor
        most = jnp.max(score, axis=0, keepdims=True)
        weight = jnp.exp(score - most).astype(BF16)
        total = jnp.sum(weight.astype(F32), axis=0, keepdims=True)
        spread = jnp.dot(vt_mem[aligned(g, 256), :], weight, preferred_element_type=F32)
        taken = jnp.where(lane_head == 0, spread[0:64], 0.0)
        for head in range(1, 4):
            taken = jnp.where(lane_head == head, spread[head * 64 : head * 64 + 64], taken)
        stat = place(row8, split3(most) + split3(total))
        turned = pltpu.roll(taken, 64, 1)
        turned_stat = pltpu.roll(stat, 64, 1)
        s_g[2 * g, pl.ds(0, 32), :] = jnp.where(left, taken[0:32], turned[32:64]).astype(BF16)
        s_g[2 * g, pl.ds(32, 8), :] = jnp.where(left[0:8], stat, turned_stat).astype(BF16)
        s_g[2 * g + 1, pl.ds(0, 32), :] = jnp.where(left, turned[0:32], taken[32:64]).astype(BF16)
        s_g[2 * g + 1, pl.ds(32, 8), :] = jnp.where(left[0:8], turned_stat, stat).astype(BF16)
        if previous is not None:
            deliver(previous)
        previous = g
    deliver(previous)
    r_g[chip] = s_g[chip]

    def drain_g():
        for k in steps:
            target = chip_at(k)
            remote(s_g.at[target], r_g.at[chip], g_send.at[target], g_recv.at[chip], peer(k)).wait_send()

    drains.append(drain_g)
    for k in steps:
        source = chip_at(half - k)
        remote(s_g.at[chip], r_g.at[source], g_send.at[chip], g_recv.at[source], peer(half - k)).wait_recv()
    stats = [r_g[source, pl.ds(32, 8), :].astype(F32) for source in range(half)]
    mosts = [stat[0:1] + stat[1:2] + stat[2:3] for stat in stats]
    top = functools.reduce(jnp.maximum, mosts)
    over = jnp.zeros((32, LANES), F32)
    under = jnp.zeros((1, LANES), F32)
    for source in range(half):
        share = jnp.exp(mosts[source] - top)
        stat = stats[source]
        under = under + share * (stat[3:4] + stat[4:5] + stat[5:6])
        over = over + share * r_g[source, pl.ds(0, 32), :].astype(F32)
    turned = (over / under).T
    crossed = jnp.concatenate([turned[rows * at : rows * at + rows] for at in (0, 2, 1, 3)], axis=1).astype(BF16)

    s_h[...] = crossed
    g_h[:, aligned(c)] = crossed
    gather_start(s_h, g_h, h_send, h_recv)
    gather_pass(s_h, g_h, h_send, h_recv)
    gather_wait(s_h, g_h, h_send, h_recv)
    out_ref[...] = (middle + jnp.dot(g_h[...], wco[...], preferred_element_type=F32)).astype(BF16)

    for drain in drains:
        drain()


def body(
    nb, nc, hidden_in, self_gain, w_self, w_self_out, cross_gain, w_cross_q, w_cross_out, cache_kv, memory_kv, parents, prefix_len
):
    rows = hidden_in.shape[0]
    d_model = w_self.shape[0]
    hyps = nb * rows
    cache_rows = cache_kv.shape[0] * cache_kv.shape[1] * cache_kv.shape[2]
    mem_count, mem_width = memory_kv.shape
    width = cache_rows // rows
    vmem = pl.BlockSpec(memory_space=pltpu.VMEM)
    hbm = pl.BlockSpec(memory_space=pl.ANY)
    wide = nc * LANES
    chips = nc // 2

    def v(*shape):
        return pltpu.VMEM(shape, BF16)

    def sems(count):
        return pltpu.SemaphoreType.DMA((count,))

    return pl.pallas_call(
        functools.partial(kernel, nb, nc, d_model),
        out_shape=jax.ShapeDtypeStruct((rows, LANES), BF16),
        in_specs=[vmem] * 5 + [hbm] * 6,
        out_specs=vmem,
        scratch_shapes=[
            v(d_model, 3 * LANES), v(2 * LANES, wide // 2), v(2 * LANES, wide // 2), v(mem_width // 2, LANES),
            v(cache_rows, LANES), v(2 * mem_count, wide // 2), v(2 * mem_count, wide // 2), v(wide // 2, 2 * mem_count),
            v(width, rows * LANES), v(width, rows * LANES), v(hyps, rows * LANES), pltpu.VMEM((hyps, LANES), F32),
            v(rows + 8, LANES), v(rows + 8, wide), pltpu.VMEM((8, LANES), F32), pltpu.VMEM((8, 2 * LANES), F32),
            v(rows, LANES), v(hyps, LANES),
            v(hyps, 2 * LANES), v(nb, rows, 2 * LANES),
            v(rows, LANES), v(rows, 2 * LANES),
            v(rows, wide // 2), v(chips, rows, LANES),
            v(rows, LANES), v(rows, 2 * LANES),
            v(rows, wide // 2), v(chips, rows, LANES),
            v(rows + 8, LANES), v(rows + 8, wide // 2),
            v(chips, 40, LANES), v(chips, 40, LANES),
            v(rows, LANES), v(rows, wide),
            sems(9), sems(7), sems(7),
            sems(nc), sems(nc), sems(nb), sems(nb), sems(nb), sems(nb), sems(chips), sems(chips),
            sems(chips), sems(chips), sems(chips), sems(chips), sems(chips), sems(chips), sems(nc), sems(nc),
        ],
        compiler_params=pltpu.CompilerParams(
            collective_id=0, has_side_effects=True, vmem_limit_bytes=VMEM_BYTES
        ),
    )(
        hidden_in,
        self_gain.reshape(1, LANES),
        cross_gain.reshape(1, LANES),
        parents.reshape(1, hyps),
        prefix_len.reshape(1, hyps),
        jnp.transpose(w_self, (1, 0, 2)),
        w_self_out,
        w_cross_q,
        w_cross_out,
        cache_kv.reshape(cache_rows, LANES),
        memory_kv,
    )


def solution(mesh):
    return jax.shard_map(
        functools.partial(body, mesh.shape["beam"], mesh.shape["blk"]),
        mesh=mesh,
        in_specs=(
            P("beam", "blk"),
            P("blk"),
            P(None, None, "blk"),
            P("blk", None),
            P("blk"),
            P("blk", None),
            P(None, "blk"),
            P("beam", None, "blk", None),
            P("blk", None),
            P(),
            P(),
        ),
        out_specs=P("beam", "blk"),
        check_vma=False,
    )
```

```python
import functools

import jax
import jax.numpy as jnp
from jax import lax
from jax.experimental import pallas as pl
from jax.experimental.pallas import tpu as pltpu
from jax.sharding import PartitionSpec as P

MESH = pl.DeviceIdType.MESH
F32 = jnp.float32
BF16 = jnp.bfloat16
NEG = -1e30
EPS = 1e-06
LANES = 128
VMEM_BYTES = 64000000


def aligned(block, size=LANES):
    return pl.ds(pl.multiple_of(block * size, size), size)


def split3(x):
    high = x.astype(BF16).astype(F32)
    rest = x - high
    middle = rest.astype(BF16).astype(F32)
    return high, middle, rest - middle


def place(index, pieces):
    out = jnp.zeros(index.shape, F32)
    for at, piece in enumerate(pieces):
        out = jnp.where(index == at, piece, out)
    return out


NT = (((1,), (1,)), ((), ()))


def kernel(
    nb, nc, d_model,
    hid_hbm, sgain_hbm, cgain_hbm, parents_hbm, plen_hbm,
    wself_hbm, wso_hbm, wcq_hbm, wco_hbm, cache_hbm, mem_hbm,
    out_hbm,
    sgain, cgain, parents, plen, result,
    wself, wso, wcq, wco, cache, keys, values, vt_mem, kt, vt, lhs_q, acc,
    s_a, g_a, s_x, g_x, s_c, g_c, s_d, r_d, s_t, g_t, s_e, r_e, s_m, g_m, s_f, r_f, s_q, g_q, s_g, r_g, s_h, g_h, s_p, r_p, s_o, r_o,
    load_sem, swap_send, swap_recv,
    a_send, a_recv, c_send, c_recv, d_send, d_recv, e_send, e_recv,
    f_send, f_recv, q_send, q_recv, g_send, g_recv, h_send, h_recv,
):
    rows = hid_hbm.shape[0]
    hyps = nb * rows
    half = nc // 2
    groups = half // 2
    score_scale = 64 ** (-0.5)
    head_width = mem_hbm.shape[1] // 2
    mem_rows = mem_hbm.shape[0]
    b = lax.axis_index("beam")
    c = lax.axis_index("blk")
    chip = lax.div(c, 2)
    core = lax.rem(c, 2)
    partner = c + 1 - 2 * core
    other_core = 1 - core
    steps = sorted(range(1, half), key=lambda k: -min(k % 8, 8 - k % 8))

    barrier = pltpu.get_barrier_semaphore()

    def greet_blk(k, carry):
        pl.semaphore_signal(barrier, inc=1, device_id=(b, lax.rem(c + 2 * k, nc)), device_id_type=MESH)
        return carry

    def greet_beam(k, carry):
        pl.semaphore_signal(barrier, inc=1, device_id=(lax.rem(b + k, nb), c), device_id_type=MESH)
        return carry

    lax.fori_loop(1, half, greet_blk, 0)
    lax.fori_loop(1, nb, greet_beam, 0)
    pl.semaphore_signal(barrier, inc=1, device_id=(b, partner), device_id_type=MESH)

    loads = [
        pltpu.make_async_copy(hid_hbm, s_a.at[pl.ds(0, rows), :], load_sem.at[0]),
        pltpu.make_async_copy(sgain_hbm, sgain, load_sem.at[1]),
        pltpu.make_async_copy(cgain_hbm, cgain, load_sem.at[2]),
        pltpu.make_async_copy(parents_hbm, parents, load_sem.at[3]),
        pltpu.make_async_copy(plen_hbm, plen, load_sem.at[4]),
        pltpu.make_async_copy(cache_hbm, cache, load_sem.at[5]),
    ]
    for load in loads:
        load.start()
    loaded = set()
    drains = []
    swap_done = set()
    swap_begun = set()
    pair_open = []

    def ready(*which):
        for at in which:
            loads[at].wait()
            loaded.add(at)

    def columns(source, target, offset=0):
        height = source.shape[0]
        return (
            lambda g, side: source.at[:, aligned(offset + 2 * g + side)],
            lambda g, who: target.at[aligned(who, height), aligned(g)],
            lambda who: target.at[aligned(who, height), :],
        )

    def kind(which):
        return (
            lambda g, side: wself_hbm.at[which, aligned(2 * g + side), :],
            lambda g, who: wself.at[aligned(g), aligned(3 * who + which)],
            lambda who: wself.at[:, aligned(3 * who + which)],
        )

    out_rows = (
        lambda g, side: wco_hbm.at[aligned(2 * g + side), :],
        lambda g, who: wco.at[aligned(g), aligned(who)],
        lambda who: wco.at[:, aligned(who)],
    )
    shared = [
        kind(0), kind(1), kind(2), columns(wso_hbm, wso), columns(wcq_hbm, wcq),
        columns(mem_hbm, keys), columns(mem_hbm, values, nc), out_rows,
    ]

    def keep(g, carry):
        for at, (block, place_at, whole) in enumerate(shared):
            pltpu.make_async_copy(block(g, core), place_at(g, core), load_sem.at[6 + at]).start()
        return carry

    lax.fori_loop(0, half, keep, 0)

    def remote(src, dst, send, recv, where):
        return pltpu.make_async_remote_copy(
            src_ref=src, dst_ref=dst, send_sem=send, recv_sem=recv, device_id=where, device_id_type=MESH
        )

    def peer(k):
        return (b, lax.rem(c + 2 * k, nc))

    def chip_at(k):
        return lax.rem(chip + k, half)

    def swap_start(*which):
        def step(g, carry):
            for at in which:
                block, place_at, whole = shared[at]
                remote(
                    block(g, other_core), place_at(g, core), swap_send.at[at], swap_recv.at[at], (b, partner)
                ).start()
            return carry

        lax.fori_loop(0, half, step, 0)
        swap_begun.update(which)

        def drain():
            for at in which:
                mine = shared[at][2](core)
                remote(mine, mine, swap_send.at[at], swap_recv.at[at], (b, partner)).wait_send()

        drains.append(drain)

    def swap_wait(*which):
        for at in which:
            swap_done.add(at)
            mine, theirs = shared[at][2](core), shared[at][2](other_core)
            pltpu.make_async_copy(mine, mine, load_sem.at[6 + at]).wait()
            if at in swap_begun:
                remote(theirs, theirs, swap_send.at[at], swap_recv.at[at], (b, partner)).wait_recv()

    def pair(src, dst, at):
        return remote(src, dst, swap_send.at[at], swap_recv.at[at], (b, partner))

    def pair_start(src, dst, at):
        pair(src, dst, at).start()
        pair_open.append((src, dst, at))
        drains.append(lambda: pair(src, dst, at).wait_send())

    def pair_wait(src, dst, at):
        pair_open[:] = [p for p in pair_open if p[2] != at]
        pair(src, dst, at).wait_recv()

    def gather_start(src, dst, send, recv):
        for k in steps:
            remote(src, dst.at[:, aligned(chip)], send.at[k], recv.at[chip], peer(k)).start()
        drains.append(functools.partial(simple_drain, src, send))

    def gather_wait(src, dst, send, recv):
        for k in steps:
            source = chip_at(half - k)
            remote(src, dst.at[:, aligned(source)], send.at[k], recv.at[source], (b, partner)).wait_recv()

    def scatter_start(src, dst, send, recv):
        for k in steps:
            remote(src.at[:, aligned(chip_at(k))], dst.at[chip], send.at[k], recv.at[chip], peer(k)).start()
        drains.append(functools.partial(simple_drain, src.at[:, aligned(chip)], send))

    def simple_drain(block, send):
        def step(k, carry):
            remote(block, block, send.at[k], send.at[k], (b, partner)).wait_send()
            return carry

        lax.fori_loop(1, half, step, 0)

    def scatter_sum(src, dst, send, recv):
        total = src[:, aligned(chip)].astype(F32)
        for k in steps:
            source = chip_at(half - k)
            remote(src.at[:, aligned(chip)], dst.at[source], send.at[k], recv.at[source], (b, partner)).wait_recv()
            total = total + dst[source].astype(F32)
        return total

    ready(0, 1, 2)
    first = s_a[pl.ds(0, rows), :]
    gain_rows = jnp.broadcast_to(sgain[...].astype(F32), (8, LANES)).astype(BF16)
    s_a[pl.ds(rows, 8), :] = gain_rows
    g_a[pl.ds(0, rows), aligned(chip)] = first
    g_a[pl.ds(rows, 8), aligned(chip)] = gain_rows
    cgain_rows = jnp.broadcast_to(cgain[...].astype(F32), (8, LANES))
    s_x[...] = cgain_rows
    g_x[:, aligned(core)] = cgain_rows
    pl.semaphore_wait(barrier, half + nb - 1)
    gather_start(s_a, g_a, a_send, a_recv)
    pair_start(s_x, g_x.at[:, aligned(core)], 8)
    swap_start(0, 1, 2)

    ready(5)
    width = cache.shape[0] // rows

    def arrange(r, carry):
        x = cache[aligned(r, width), :].astype(F32)
        rolled = pltpu.roll(x, 64, 1)
        even = lax.rem(lax.broadcasted_iota(jnp.int32, x.shape, 0), 2) == 0
        low = lax.broadcasted_iota(jnp.int32, x.shape, 1) < 64
        kt[:, aligned(r)] = jnp.where(even, jnp.where(low, x, 0.0), jnp.where(low, 0.0, rolled)).astype(BF16)
        vt[:, aligned(r)] = jnp.where(even, jnp.where(low, rolled, 0.0), jnp.where(low, 0.0, x)).astype(BF16)
        return carry

    lax.fori_loop(0, rows, arrange, 0)
    ready(3, 4)
    local_wide = jnp.broadcast_to(parents[...], (LANES, hyps)).T - b * rows
    plen_wide = jnp.broadcast_to(plen[...], (LANES, hyps)).T
    swap_wait(0, 1, 2)
    gather_wait(s_a, g_a, a_send, a_recv)

    wide = g_a[pl.ds(0, rows), :].astype(F32)
    gain = g_a[pl.ds(rows, 8), :].astype(F32)[0:1, :]
    squares = jnp.broadcast_to(jnp.sum(wide * wide, axis=1, keepdims=True), (rows, LANES))
    scaled = (wide * gain).astype(BF16)
    partial = jnp.dot(scaled, wself[...], preferred_element_type=F32)
    for who in range(2):
        s_p[:, pl.ds(512 * who, 384)] = partial[:, 384 * who : 384 * who + 384]
        s_p[:, pl.ds(512 * who + 384, LANES)] = squares
    pair_start(s_p.at[:, aligned(other_core, 512)], r_p, 9)
    pair_wait(s_p.at[:, aligned(other_core, 512)], r_p, 9)
    joined = s_p[:, aligned(core, 512)] + r_p[...]
    self_scale = lax.rsqrt(joined[:, 384:] * (1.0 / d_model) + EPS)
    queries = (joined[:, :LANES] * self_scale).astype(BF16)

    s_c[...] = queries
    g_c[aligned(b, rows), :] = queries
    my_queries = g_c.at[aligned(b, rows), :]

    def send_c(k, carry):
        remote(s_c, my_queries, c_send.at[k], c_recv.at[b], (lax.rem(b + k, nb), c)).start()
        return carry

    lax.fori_loop(1, nb, send_c, 0)

    def drain_c():
        def step(k, carry):
            remote(s_c, my_queries, c_send.at[k], c_recv.at[b], (b, partner)).wait_send()
            return carry

        lax.fori_loop(1, nb, step, 0)

    drains.append(drain_c)
    swap_start(3, 4, 5, 6, 7)
    own_values = (joined[:, 2 * LANES : 3 * LANES] * self_scale).astype(BF16).astype(F32)
    products = queries.astype(F32) * (joined[:, LANES : 2 * LANES] * self_scale).astype(BF16).astype(F32)
    low = lax.broadcasted_iota(jnp.int32, products.shape, 1) < 64
    own_0 = jnp.sum(jnp.where(low, products, 0.0), axis=1, keepdims=True) * score_scale
    own_1 = jnp.sum(jnp.where(low, 0.0, products), axis=1, keepdims=True) * score_scale

    def wait_c(k, carry):
        source = lax.rem(b + k, nb)
        remote(s_c, g_c.at[aligned(source, rows), :], c_send.at[k], c_recv.at[source], (source, c)).wait_recv()
        return carry

    lax.fori_loop(1, nb, wait_c, 0)

    all_queries = g_c[...].astype(F32)

    def spread_q(r, carry):
        lhs_q[:, aligned(r)] = jnp.where(local_wide == r, all_queries, 0.0).astype(BF16)
        return carry

    lax.fori_loop(0, rows, spread_q, 0)
    scores = lax.dot_general(lhs_q[...], kt[...], NT, preferred_element_type=F32) * score_scale
    lane = lax.broadcasted_iota(jnp.int32, scores.shape, 1)
    even = lax.rem(lane, 2) == 0
    tiles = width // LANES
    visible = lax.div(lane, 2) < jnp.concatenate([plen_wide] * tiles, axis=1)
    masked = jnp.where(visible, scores, NEG)
    max_0 = jnp.max(jnp.where(even, masked, NEG), axis=1, keepdims=True)
    max_1 = jnp.max(jnp.where(even, NEG, masked), axis=1, keepdims=True)
    weights = jnp.where(visible, jnp.exp(masked - jnp.where(even, max_0, max_1)), 0.0).astype(BF16)
    lhs_q[:, pl.ds(0, width)] = weights
    weights = weights.astype(F32)
    total_0 = jnp.sum(jnp.where(even, weights, 0.0), axis=1, keepdims=True)
    total_1 = jnp.sum(jnp.where(even, 0.0, weights), axis=1, keepdims=True)
    acc[...] = jnp.zeros(acc.shape, F32)

    def select(r, carry):
        both = jnp.dot(lhs_q[:, pl.ds(0, width)], vt[:, aligned(r, 2 * LANES)], preferred_element_type=F32)
        picked = jnp.where(local_wide == 2 * r, both[:, :LANES], acc[...])
        acc[...] = jnp.where(local_wide == 2 * r + 1, both[:, LANES:], picked)
        return carry

    lax.fori_loop(0, rows // 2, select, 0)
    summed = acc[...]
    lane = lax.broadcasted_iota(jnp.int32, summed.shape, 1)
    here = (local_wide >= 0) & (local_wide < rows)
    part = summed / jnp.where(lane < 64, total_0, total_1)
    pieces = split3(max_0 + jnp.log(total_0)) + split3(max_1 + jnp.log(total_1))
    s_d[:, pl.ds(0, LANES)] = part.astype(BF16)
    s_d[:, pl.ds(LANES, LANES)] = jnp.where(here, place(lane, pieces), 0.0).astype(BF16)

    def send_d(k, carry):
        target = lax.rem(b + k, nb)
        remote(s_d.at[aligned(target, rows), :], r_d.at[b], d_send.at[k], d_recv.at[b], (target, c)).start()
        return carry

    lax.fori_loop(1, nb, send_d, 0)

    def drain_d():
        def step(k, carry):
            remote(s_d.at[aligned(b, rows), :], r_d.at[b], d_send.at[k], d_recv.at[b], (b, partner)).wait_send()
            return carry

        lax.fori_loop(1, nb, step, 0)

    drains.append(drain_d)
    swap_wait(3, 4)

    def wait_d(k, total):
        source = lax.rem(b + k, nb)
        remote(s_d.at[aligned(b, rows), :], r_d.at[source], d_send.at[k], d_recv.at[source], (source, c)).wait_recv()
        return total + r_d[source].astype(F32)

    back = lax.fori_loop(1, nb, wait_d, s_d[aligned(b, rows), :].astype(F32))
    stats = back[:, LANES:]
    log_0 = stats[:, 0:1] + stats[:, 1:2] + stats[:, 2:3]
    log_1 = stats[:, 3:4] + stats[:, 4:5] + stats[:, 5:6]
    cache_log = jnp.where(low, log_0, log_1)
    own_log = jnp.where(low, own_0, own_1)
    top = jnp.maximum(cache_log, own_log)
    cache_weight = jnp.exp(cache_log - top)
    own_weight = jnp.exp(own_log - top)
    attended = (cache_weight * back[:, :LANES] + own_weight * own_values) / (cache_weight + own_weight)
    attended = attended.astype(BF16)
    s_t[...] = attended
    g_t[:, aligned(core)] = attended
    pair_start(s_t, g_t.at[:, aligned(core)], 10)
    pair_wait(s_t, g_t.at[:, aligned(other_core)], 10)

    s_e[...] = jnp.dot(g_t[...], wso[...], preferred_element_type=F32).astype(BF16)
    scatter_start(s_e, r_e, e_send, e_recv)
    swap_wait(5, 6, 7)

    def turn(g, carry):
        vt_mem[aligned(g, 256), :] = values[:, aligned(g, 256)].T
        return carry

    lax.fori_loop(0, groups, turn, 0)
    mixed = scatter_sum(s_e, r_e, e_send, e_recv)
    middle_16 = (first.astype(F32) + mixed).astype(BF16)
    middle = middle_16.astype(F32)

    s_m[...] = middle_16
    g_m[:, aligned(core)] = middle_16
    pair_start(s_m, g_m.at[:, aligned(core)], 11)
    pair_wait(s_x, g_x.at[:, aligned(other_core)], 8)
    pair_wait(s_m, g_m.at[:, aligned(other_core)], 11)
    both_middle = g_m[...].astype(F32)
    cross_scaled = (both_middle * g_x[0:1, :]).astype(BF16)
    s_f[...] = jnp.dot(cross_scaled, wcq[...], preferred_element_type=F32).astype(BF16)
    scatter_start(s_f, r_f, f_send, f_recv)
    squares = jnp.broadcast_to(jnp.sum(both_middle * both_middle, axis=1, keepdims=True), (rows, LANES))
    squares = jnp.concatenate([squares] * (LANES // rows), axis=0).T[0:1, :]
    row8 = lax.broadcasted_iota(jnp.int32, (8, LANES), 0)
    square_rows = place(row8, split3(squares)).astype(BF16)
    s_q[pl.ds(rows, 8), :] = square_rows
    g_q[pl.ds(rows, 8), aligned(chip)] = square_rows
    raw = scatter_sum(s_f, r_f, f_send, f_recv).astype(BF16)
    s_q[pl.ds(0, rows), :] = raw
    g_q[pl.ds(0, rows), aligned(chip)] = raw

    gather_start(s_q, g_q, q_send, q_recv)
    gather_wait(s_q, g_q, q_send, q_recv)
    sums = jnp.zeros((8, LANES), F32)
    for k in range(half):
        sums = sums + g_q[pl.ds(rows, 8), pl.ds(k * LANES, LANES)].astype(F32)
    mean = (sums[0:1, :] + sums[1:2, :] + sums[2:3, :]) * (1.0 / d_model)
    factor = lax.rsqrt(mean + EPS) * score_scale

    own_block = (
        lax.div(lax.broadcasted_iota(jnp.int32, (LANES, 256), 0), rows)
        == lax.div(lax.broadcasted_iota(jnp.int32, (LANES, 256), 1), 64)
    )
    lane_head = lax.div(lax.broadcasted_iota(jnp.int32, (64, LANES), 1), rows)
    left = lax.broadcasted_iota(jnp.int32, (32, LANES), 1) < 64

    def deliver(g):
        for which in range(2):
            target = 2 * g + which

            @pl.when(target != chip)
            def _():
                remote(
                    s_g.at[target], r_g.at[chip], g_send.at[target], g_recv.at[chip], (b, 2 * target + core)
                ).start()

    offsets = sorted(range(groups), key=lambda k: -min(k % 4, 4 - k % 4) if k else 1)
    previous = None
    for offset in offsets:
        g = lax.rem(lax.div(chip, 2) + offset, groups)
        query = g_q[pl.ds(0, rows), aligned(g, 256)].astype(F32)
        query = jnp.where(own_block, jnp.concatenate([query] * 4, axis=0), 0.0).astype(BF16)
        score = lax.dot_general(keys[:, aligned(g, 256)], query, NT, preferred_element_type=F32) * factor
        most = jnp.max(score, axis=0, keepdims=True)
        weight = jnp.exp(score - most).astype(BF16)
        total = jnp.sum(weight.astype(F32), axis=0, keepdims=True)
        spread = jnp.dot(vt_mem[aligned(g, 256), :], weight, preferred_element_type=F32)
        taken = jnp.where(lane_head == 0, spread[0:64], 0.0)
        for head in range(1, 4):
            taken = jnp.where(lane_head == head, spread[head * 64 : head * 64 + 64], taken)
        stat = place(row8, split3(most) + split3(total))
        turned = pltpu.roll(taken, 64, 1)
        turned_stat = pltpu.roll(stat, 64, 1)
        s_g[2 * g, pl.ds(0, 32), :] = jnp.where(left, taken[0:32], turned[32:64]).astype(BF16)
        s_g[2 * g, pl.ds(32, 8), :] = jnp.where(left[0:8], stat, turned_stat).astype(BF16)
        s_g[2 * g + 1, pl.ds(0, 32), :] = jnp.where(left, turned[0:32], taken[32:64]).astype(BF16)
        s_g[2 * g + 1, pl.ds(32, 8), :] = jnp.where(left[0:8], turned_stat, stat).astype(BF16)
        if previous is not None:
            deliver(previous)
        previous = g
    deliver(previous)
    r_g[chip] = s_g[chip]

    def drain_g():
        for k in steps:
            target = chip_at(k)
            remote(s_g.at[target], r_g.at[chip], g_send.at[target], g_recv.at[chip], peer(k)).wait_send()

    drains.append(drain_g)
    for k in steps:
        source = chip_at(half - k)
        remote(s_g.at[chip], r_g.at[source], g_send.at[chip], g_recv.at[source], peer(half - k)).wait_recv()
    stats = [r_g[source, pl.ds(32, 8), :].astype(F32) for source in range(half)]
    mosts = [stat[0:1] + stat[1:2] + stat[2:3] for stat in stats]
    top = functools.reduce(jnp.maximum, mosts)
    over = jnp.zeros((32, LANES), F32)
    under = jnp.zeros((1, LANES), F32)
    for source in range(half):
        share = jnp.exp(mosts[source] - top)
        stat = stats[source]
        under = under + share * (stat[3:4] + stat[4:5] + stat[5:6])
        over = over + share * r_g[source, pl.ds(0, 32), :].astype(F32)
    turned = (over / under).T
    crossed = jnp.concatenate([turned[rows * at : rows * at + rows] for at in (0, 2, 1, 3)], axis=1).astype(BF16)

    s_h[...] = crossed
    g_h[:, aligned(chip)] = crossed
    gather_start(s_h, g_h, h_send, h_recv)
    gather_wait(s_h, g_h, h_send, h_recv)
    s_o[...] = jnp.dot(g_h[...], wco[...], preferred_element_type=F32)
    theirs = s_o.at[:, aligned(other_core)]
    pair_start(theirs, r_o, 12)
    pair_wait(theirs, r_o, 12)
    result[...] = (middle + s_o[:, aligned(core)] + r_o[...]).astype(BF16)
    leave = pltpu.make_async_copy(result, out_hbm, load_sem.at[14])
    leave.start()

    for drain in drains:
        drain()
    leave.wait()


def body(
    nb, nc, hidden_in, self_gain, w_self, w_self_out, cross_gain, w_cross_q, w_cross_out, cache_kv, memory_kv, parents, prefix_len
):
    rows = hidden_in.shape[0]
    d_model = w_self.shape[0]
    hyps = nb * rows
    cache_rows = cache_kv.shape[0] * cache_kv.shape[1] * cache_kv.shape[2]
    mem_count, mem_width = memory_kv.shape
    width = cache_rows // rows
    hbm = pl.BlockSpec(memory_space=pl.ANY)
    wide = nc * LANES
    chips = nc // 2

    def v(*shape):
        return pltpu.VMEM(shape, BF16)

    def f(*shape):
        return pltpu.VMEM(shape, F32)

    def sems(count):
        return pltpu.SemaphoreType.DMA((count,))

    return pl.pallas_call(
        functools.partial(kernel, nb, nc, d_model),
        out_shape=jax.ShapeDtypeStruct((rows, LANES), BF16),
        in_specs=[hbm] * 11,
        out_specs=hbm,
        scratch_shapes=[
            v(1, LANES), v(1, LANES), pltpu.VMEM((1, hyps), jnp.int32), pltpu.VMEM((1, hyps), jnp.int32), v(rows, LANES),
            v(d_model // 2, 6 * LANES), v(2 * LANES, wide // 2), v(2 * LANES, wide // 2), v(wide // 2, 2 * LANES),
            v(cache_rows, LANES), v(2 * mem_count, wide // 2), v(2 * mem_count, wide // 2), v(wide // 2, 2 * mem_count),
            v(width, rows * LANES), v(width, rows * LANES), v(hyps, rows * LANES), pltpu.VMEM((hyps, LANES), F32),
            v(rows + 8, LANES), v(rows + 8, wide // 2), pltpu.VMEM((8, LANES), F32), pltpu.VMEM((8, 2 * LANES), F32),
            v(rows, LANES), v(hyps, LANES),
            v(hyps, 2 * LANES), v(nb, rows, 2 * LANES),
            v(rows, LANES), v(rows, 2 * LANES),
            v(rows, wide // 2), v(chips, rows, LANES),
            v(rows, LANES), v(rows, 2 * LANES),
            v(rows, wide // 2), v(chips, rows, LANES),
            v(rows + 8, LANES), v(rows + 8, wide // 2),
            v(chips, 40, LANES), v(chips, 40, LANES),
            v(rows, LANES), v(rows, wide // 2),
            f(rows, 8 * LANES), f(rows, 4 * LANES), f(rows, 2 * LANES), f(rows, LANES),
            sems(15), sems(13), sems(13),
            sems(chips), sems(chips), sems(nb), sems(nb), sems(nb), sems(nb), sems(chips), sems(chips),
            sems(chips), sems(chips), sems(chips), sems(chips), sems(chips), sems(chips), sems(chips), sems(chips),
        ],
        compiler_params=pltpu.CompilerParams(
            collective_id=0, has_side_effects=True, vmem_limit_bytes=VMEM_BYTES
        ),
    )(
        hidden_in,
        self_gain.reshape(1, LANES),
        cross_gain.reshape(1, LANES),
        parents.reshape(1, hyps),
        prefix_len.reshape(1, hyps),
        jnp.transpose(w_self, (1, 0, 2)),
        w_self_out,
        w_cross_q,
        w_cross_out,
        cache_kv.reshape(cache_rows, LANES),
        memory_kv,
    )


def solution(mesh):
    return jax.shard_map(
        functools.partial(body, mesh.shape["beam"], mesh.shape["blk"]),
        mesh=mesh,
        in_specs=(
            P("beam", "blk"),
            P("blk"),
            P(None, None, "blk"),
            P("blk", None),
            P("blk"),
            P("blk", None),
            P(None, "blk"),
            P("beam", None, "blk", None),
            P("blk", None),
            P(),
            P(),
        ),
        out_specs=P("beam", "blk"),
        check_vma=False,
    )
```

```python
import functools

import jax
import jax.numpy as jnp
from jax import lax
from jax.experimental import pallas as pl
from jax.experimental.pallas import tpu as pltpu
from jax.sharding import PartitionSpec as P

MESH = pl.DeviceIdType.MESH
F32 = jnp.float32
BF16 = jnp.bfloat16
NEG = -1e30
EPS = 1e-06
LANES = 128
VMEM_BYTES = 64000000
AT_ONCE = 2


def aligned(block, size=LANES):
    return pl.ds(pl.multiple_of(block * size, size), size)


def split3(x):
    high = x.astype(BF16).astype(F32)
    rest = x - high
    middle = rest.astype(BF16).astype(F32)
    return high, middle, rest - middle


def place(index, pieces):
    out = jnp.zeros(index.shape, F32)
    for at, piece in enumerate(pieces):
        out = jnp.where(index == at, piece, out)
    return out


NT = (((1,), (1,)), ((), ()))


def kernel(
    nb, nc, d_model,
    hid_hbm, sgain_hbm, cgain_hbm, parents_hbm, plen_hbm,
    wself_hbm, wso_hbm, wcq_hbm, wco_hbm, cache_hbm, mem_hbm,
    out_hbm,
    sgain, cgain, parents, plen, result,
    wself, wso, wcq, wco, cache, keys, values, vt_mem, kt, vt, lhs_q, acc,
    s_a, g_a, s_x, g_x, s_c, g_c, s_d, r_d, s_t, g_t, s_e, r_e, s_m, g_m, s_f, r_f, s_q, g_q, s_g, r_g, s_h, g_h, s_p, r_p, s_o, r_o,
    load_sem, swap_send, swap_recv,
    a_send, a_recv, c_send, c_recv, d_send, d_recv, e_send, e_recv,
    f_send, f_recv, q_send, q_recv, g_send, g_recv, h_send, h_recv,
):
    rows = hid_hbm.shape[0]
    hyps = nb * rows
    half = nc // 2
    groups = half // 2
    score_scale = 64 ** (-0.5)
    head_width = mem_hbm.shape[1] // 2
    mem_rows = mem_hbm.shape[0]
    b = lax.axis_index("beam")
    c = lax.axis_index("blk")
    chip = lax.div(c, 2)
    core = lax.rem(c, 2)
    partner = c + 1 - 2 * core
    other_core = 1 - core
    steps = sorted(range(1, half), key=lambda k: -min(k % 8, 8 - k % 8))

    barrier = pltpu.get_barrier_semaphore()

    def greet_blk(k, carry):
        pl.semaphore_signal(barrier, inc=1, device_id=(b, lax.rem(c + 2 * k, nc)), device_id_type=MESH)
        return carry

    def greet_beam(k, carry):
        pl.semaphore_signal(barrier, inc=1, device_id=(lax.rem(b + k, nb), c), device_id_type=MESH)
        return carry

    lax.fori_loop(1, half, greet_blk, 0)
    lax.fori_loop(1, nb, greet_beam, 0)
    pl.semaphore_signal(barrier, inc=1, device_id=(b, partner), device_id_type=MESH)

    loads = [
        pltpu.make_async_copy(hid_hbm, s_a.at[pl.ds(0, rows), :], load_sem.at[0]),
        pltpu.make_async_copy(sgain_hbm, sgain, load_sem.at[1]),
        pltpu.make_async_copy(cgain_hbm, cgain, load_sem.at[2]),
        pltpu.make_async_copy(parents_hbm, parents, load_sem.at[3]),
        pltpu.make_async_copy(plen_hbm, plen, load_sem.at[4]),
        pltpu.make_async_copy(cache_hbm, cache, load_sem.at[5]),
    ]
    for load in loads:
        load.start()
    loaded = set()
    drains = []
    swap_done = set()
    swap_begun = set()
    pair_open = []

    def ready(*which):
        for at in which:
            loads[at].wait()
            loaded.add(at)

    def columns(source, target, offset=0):
        height = source.shape[0]
        return (
            lambda g, side: source.at[:, aligned(offset + 2 * g + side)],
            lambda g, who: target.at[aligned(who, height), aligned(g)],
            lambda who: target.at[aligned(who, height), :],
        )

    def kind(which):
        return (
            lambda g, side: wself_hbm.at[which, aligned(2 * g + side), :],
            lambda g, who: wself.at[aligned(g), aligned(3 * who + which)],
            lambda who: wself.at[:, aligned(3 * who + which)],
        )

    out_rows = (
        lambda g, side: wco_hbm.at[aligned(2 * g + side), :],
        lambda g, who: wco.at[aligned(g), aligned(who)],
        lambda who: wco.at[:, aligned(who)],
    )
    shared = [
        kind(0), kind(1), kind(2), columns(wso_hbm, wso), columns(wcq_hbm, wcq),
        columns(mem_hbm, keys), columns(mem_hbm, values, nc), out_rows,
    ]

    def keep(g, carry):
        for at, (block, place_at, whole) in enumerate(shared):
            pltpu.make_async_copy(block(g, core), place_at(g, core), load_sem.at[6 + at]).start()
        return carry

    lax.fori_loop(0, half, keep, 0)

    def remote(src, dst, send, recv, where):
        return pltpu.make_async_remote_copy(
            src_ref=src, dst_ref=dst, send_sem=send, recv_sem=recv, device_id=where, device_id_type=MESH
        )

    def peer(k):
        return (b, lax.rem(c + 2 * k, nc))

    def chip_at(k):
        return lax.rem(chip + k, half)

    def swap_start(*which):
        def step(g, carry):
            for at in which:
                block, place_at, whole = shared[at]
                remote(
                    block(g, other_core), place_at(g, core), swap_send.at[at], swap_recv.at[at], (b, partner)
                ).start()
            return carry

        lax.fori_loop(0, half, step, 0)
        swap_begun.update(which)

        def drain():
            for at in which:
                mine = shared[at][2](core)
                remote(mine, mine, swap_send.at[at], swap_recv.at[at], (b, partner)).wait_send()

        drains.append(drain)

    def swap_wait(*which):
        for at in which:
            swap_done.add(at)
            mine, theirs = shared[at][2](core), shared[at][2](other_core)
            pltpu.make_async_copy(mine, mine, load_sem.at[6 + at]).wait()
            if at in swap_begun:
                remote(theirs, theirs, swap_send.at[at], swap_recv.at[at], (b, partner)).wait_recv()

    def pair(src, dst, at):
        return remote(src, dst, swap_send.at[at], swap_recv.at[at], (b, partner))

    def pair_start(src, dst, at):
        pair(src, dst, at).start()
        pair_open.append((src, dst, at))
        drains.append(lambda: pair(src, dst, at).wait_send())

    def pair_wait(src, dst, at):
        pair_open[:] = [p for p in pair_open if p[2] != at]
        pair(src, dst, at).wait_recv()

    def gather_start(src, dst, send, recv):
        for k in steps:
            remote(src, dst.at[chip], send.at[k], recv.at[chip], peer(k)).start()
        drains.append(functools.partial(simple_drain, src, send))

    def gather_wait(src, dst, send, recv):
        for k in steps:
            source = chip_at(half - k)
            remote(src, dst.at[source], send.at[k], recv.at[source], (b, partner)).wait_recv()

    def gathered(dst):
        return jnp.concatenate([dst[at, pl.ds(0, rows), :] for at in range(half)], axis=1)

    def scatter_start(src, dst, send, recv):
        for k in steps:
            remote(src.at[chip_at(k)], dst.at[chip], send.at[k], recv.at[chip], peer(k)).start()
        drains.append(functools.partial(simple_drain, src.at[chip], send))

    def simple_drain(block, send):
        def step(k, carry):
            remote(block, block, send.at[k], send.at[k], (b, partner)).wait_send()
            return carry

        lax.fori_loop(1, half, step, 0)

    def scatter_fill(src, terms):
        for at in range(half):
            src[at] = terms[:, at * LANES : at * LANES + LANES].astype(BF16)

    def scatter_sum(src, dst, send, recv):
        total = src[chip].astype(F32)
        for k in steps:
            source = chip_at(half - k)
            remote(src.at[chip], dst.at[source], send.at[k], recv.at[source], (b, partner)).wait_recv()
            total = total + dst[source].astype(F32)
        return total

    ready(0, 1, 2)
    first = s_a[pl.ds(0, rows), :]
    gain_rows = jnp.broadcast_to(sgain[...].astype(F32), (8, LANES)).astype(BF16)
    s_a[pl.ds(rows, 8), :] = gain_rows
    g_a[chip, pl.ds(0, rows), :] = first
    g_a[chip, pl.ds(rows, 8), :] = gain_rows
    cgain_rows = jnp.broadcast_to(cgain[...].astype(F32), (8, LANES))
    s_x[...] = cgain_rows
    g_x[:, aligned(core)] = cgain_rows
    pl.semaphore_wait(barrier, half + nb - 1)
    gather_start(s_a, g_a, a_send, a_recv)
    pair_start(s_x, g_x.at[:, aligned(core)], 8)
    swap_start(0, 1, 2)

    ready(5)
    width = cache.shape[0] // rows

    def arrange(r, carry):
        x = cache[aligned(r, width), :].astype(F32)
        rolled = pltpu.roll(x, 64, 1)
        even = lax.rem(lax.broadcasted_iota(jnp.int32, x.shape, 0), 2) == 0
        low = lax.broadcasted_iota(jnp.int32, x.shape, 1) < 64
        kt[:, aligned(r)] = jnp.where(even, jnp.where(low, x, 0.0), jnp.where(low, 0.0, rolled)).astype(BF16)
        vt[:, aligned(r)] = jnp.where(even, jnp.where(low, rolled, 0.0), jnp.where(low, 0.0, x)).astype(BF16)
        return carry

    lax.fori_loop(0, rows, arrange, 0)
    ready(3, 4)
    local_wide = jnp.broadcast_to(parents[...], (LANES, hyps)).T - b * rows
    plen_wide = jnp.broadcast_to(plen[...], (LANES, hyps)).T
    swap_wait(0, 1, 2)
    gather_wait(s_a, g_a, a_send, a_recv)

    wide = gathered(g_a).astype(F32)
    gain = jnp.concatenate([g_a[at, pl.ds(rows, 8), :] for at in range(half)], axis=1).astype(F32)[0:1, :]
    squares = jnp.broadcast_to(jnp.sum(wide * wide, axis=1, keepdims=True), (rows, LANES))
    scaled = (wide * gain).astype(BF16)
    s_p[:, pl.ds(0, 384)] = jnp.dot(scaled, wself[:, aligned(other_core, 384)], preferred_element_type=F32)
    s_p[:, pl.ds(384, LANES)] = squares
    pair_start(s_p, r_p, 9)
    mine = jnp.dot(scaled, wself[:, aligned(core, 384)], preferred_element_type=F32)
    pair_wait(s_p, r_p, 9)
    joined = mine + r_p[:, pl.ds(0, 384)]
    self_scale = lax.rsqrt((squares + r_p[:, pl.ds(384, LANES)]) * (1.0 / d_model) + EPS)
    queries = (joined[:, :LANES] * self_scale).astype(BF16)

    s_c[...] = queries
    g_c[aligned(b, rows), :] = queries
    my_queries = g_c.at[aligned(b, rows), :]

    def send_c(k, carry):
        remote(s_c, my_queries, c_send.at[k], c_recv.at[b], (lax.rem(b + k, nb), c)).start()
        return carry

    lax.fori_loop(1, nb, send_c, 0)

    def drain_c():
        def step(k, carry):
            remote(s_c, my_queries, c_send.at[k], c_recv.at[b], (b, partner)).wait_send()
            return carry

        lax.fori_loop(1, nb, step, 0)

    drains.append(drain_c)
    swap_start(3, 4, 5, 6, 7)
    own_values = (joined[:, 2 * LANES : 3 * LANES] * self_scale).astype(BF16).astype(F32)
    products = queries.astype(F32) * (joined[:, LANES : 2 * LANES] * self_scale).astype(BF16).astype(F32)
    low = lax.broadcasted_iota(jnp.int32, products.shape, 1) < 64
    own_0 = jnp.sum(jnp.where(low, products, 0.0), axis=1, keepdims=True) * score_scale
    own_1 = jnp.sum(jnp.where(low, 0.0, products), axis=1, keepdims=True) * score_scale

    def wait_c(k, carry):
        source = lax.rem(b + k, nb)
        remote(s_c, g_c.at[aligned(source, rows), :], c_send.at[k], c_recv.at[source], (source, c)).wait_recv()
        return carry

    lax.fori_loop(1, nb, wait_c, 0)

    all_queries = g_c[...]
    nothing = jnp.zeros(all_queries.shape, BF16)
    local_16 = local_wide.astype(F32).astype(BF16)
    for r in range(rows):
        lhs_q[:, pl.ds(r * LANES, LANES)] = jnp.where(local_16 == r, all_queries, nothing)
    scores = lax.dot_general(lhs_q[...], kt[...], NT, preferred_element_type=F32) * score_scale
    lane = lax.broadcasted_iota(jnp.int32, scores.shape, 1)
    even = lax.rem(lane, 2) == 0
    tiles = width // LANES
    visible = lax.div(lane, 2) < jnp.concatenate([plen_wide] * tiles, axis=1)
    masked = jnp.where(visible, scores, NEG)
    max_0 = jnp.max(jnp.where(even, masked, NEG), axis=1, keepdims=True)
    max_1 = jnp.max(jnp.where(even, NEG, masked), axis=1, keepdims=True)
    weights = jnp.where(visible, jnp.exp(masked - jnp.where(even, max_0, max_1)), 0.0).astype(BF16)
    lhs_q[:, pl.ds(0, width)] = weights
    weights = weights.astype(F32)
    total_0 = jnp.sum(jnp.where(even, weights, 0.0), axis=1, keepdims=True)
    total_1 = jnp.sum(jnp.where(even, 0.0, weights), axis=1, keepdims=True)
    weights = lhs_q[:, pl.ds(0, width)]
    acc[...] = jnp.zeros(acc.shape, F32)
    for r in range(0, rows, 2):
        both = jnp.dot(weights, vt[:, pl.ds(r * LANES, 2 * LANES)], preferred_element_type=F32)
        picked = jnp.where(local_wide == r, both[:, :LANES], acc[...])
        acc[...] = jnp.where(local_wide == r + 1, both[:, LANES:], picked)
    summed = acc[...]
    lane = lax.broadcasted_iota(jnp.int32, summed.shape, 1)
    here = (local_wide >= 0) & (local_wide < rows)
    part = summed / jnp.where(lane < 64, total_0, total_1)
    pieces = split3(max_0 + jnp.log(total_0)) + split3(max_1 + jnp.log(total_1))
    s_d[:, pl.ds(0, LANES)] = part.astype(BF16)
    s_d[:, pl.ds(LANES, LANES)] = jnp.where(here, place(lane, pieces), 0.0).astype(BF16)

    def send_d(k, carry):
        target = lax.rem(b + k, nb)
        remote(s_d.at[aligned(target, rows), :], r_d.at[b], d_send.at[k], d_recv.at[b], (target, c)).start()
        return carry

    lax.fori_loop(1, nb, send_d, 0)

    def drain_d():
        def step(k, carry):
            remote(s_d.at[aligned(b, rows), :], r_d.at[b], d_send.at[k], d_recv.at[b], (b, partner)).wait_send()
            return carry

        lax.fori_loop(1, nb, step, 0)

    drains.append(drain_d)
    swap_wait(3, 4)

    def wait_d(k, total):
        source = lax.rem(b + k, nb)
        remote(s_d.at[aligned(b, rows), :], r_d.at[source], d_send.at[k], d_recv.at[source], (source, c)).wait_recv()
        return total + r_d[source].astype(F32)

    back = lax.fori_loop(1, nb, wait_d, s_d[aligned(b, rows), :].astype(F32))
    stats = back[:, LANES:]
    log_0 = stats[:, 0:1] + stats[:, 1:2] + stats[:, 2:3]
    log_1 = stats[:, 3:4] + stats[:, 4:5] + stats[:, 5:6]
    cache_log = jnp.where(low, log_0, log_1)
    own_log = jnp.where(low, own_0, own_1)
    top = jnp.maximum(cache_log, own_log)
    cache_weight = jnp.exp(cache_log - top)
    own_weight = jnp.exp(own_log - top)
    attended = (cache_weight * back[:, :LANES] + own_weight * own_values) / (cache_weight + own_weight)
    attended = attended.astype(BF16)
    s_t[...] = attended
    g_t[:, aligned(core)] = attended
    pair_start(s_t, g_t.at[:, aligned(core)], 10)

    terms = jnp.dot(attended, wso[aligned(core), :], preferred_element_type=F32)
    pair_wait(s_t, g_t.at[:, aligned(other_core)], 10)
    terms = terms + jnp.dot(g_t[:, aligned(other_core)], wso[aligned(other_core), :], preferred_element_type=F32)
    scatter_fill(s_e, terms)
    scatter_start(s_e, r_e, e_send, e_recv)
    swap_wait(5, 6, 7)

    def turn(g, carry):
        vt_mem[aligned(g, 256), :] = values[:, aligned(g, 256)].T
        return carry

    lax.fori_loop(0, groups, turn, 0)
    mixed = scatter_sum(s_e, r_e, e_send, e_recv)
    middle_16 = (first.astype(F32) + mixed).astype(BF16)
    middle = middle_16.astype(F32)

    s_m[...] = middle_16
    g_m[:, aligned(core)] = middle_16
    pair_start(s_m, g_m.at[:, aligned(core)], 11)
    pair_wait(s_x, g_x.at[:, aligned(other_core)], 8)
    pair_wait(s_m, g_m.at[:, aligned(other_core)], 11)
    both_middle = g_m[...].astype(F32)
    cross_scaled = (both_middle * g_x[0:1, :]).astype(BF16)
    scatter_fill(s_f, jnp.dot(cross_scaled, wcq[...], preferred_element_type=F32))
    scatter_start(s_f, r_f, f_send, f_recv)
    squares = jnp.broadcast_to(jnp.sum(both_middle * both_middle, axis=1, keepdims=True), (rows, LANES))
    squares = jnp.concatenate([squares] * (LANES // rows), axis=0).T[0:1, :]
    row8 = lax.broadcasted_iota(jnp.int32, (8, LANES), 0)
    square_rows = place(row8, split3(squares)).astype(BF16)
    s_q[pl.ds(rows, 8), :] = square_rows
    g_q[chip, pl.ds(rows, 8), :] = square_rows
    raw = scatter_sum(s_f, r_f, f_send, f_recv).astype(BF16)
    s_q[pl.ds(0, rows), :] = raw
    g_q[chip, pl.ds(0, rows), :] = raw

    gather_start(s_q, g_q, q_send, q_recv)
    gather_wait(s_q, g_q, q_send, q_recv)
    sums = jnp.zeros((8, LANES), F32)
    for k in range(half):
        sums = sums + g_q[k, pl.ds(rows, 8), :].astype(F32)
    mean = (sums[0:1, :] + sums[1:2, :] + sums[2:3, :]) * (1.0 / d_model)
    factor = lax.rsqrt(mean + EPS) * score_scale

    own_block = (
        lax.div(lax.broadcasted_iota(jnp.int32, (LANES, 256), 0), rows)
        == lax.div(lax.broadcasted_iota(jnp.int32, (LANES, 256), 1), 64)
    )
    lane_head = lax.div(lax.broadcasted_iota(jnp.int32, (64, LANES), 1), rows)
    left = lax.broadcasted_iota(jnp.int32, (32, LANES), 1) < 64

    def deliver(target):
        remote(s_g.at[target], r_g.at[chip], g_send.at[target], g_recv.at[chip], (b, 2 * target + core)).start()

    def remember(g):
        query = jnp.concatenate([g_q[2 * g, pl.ds(0, rows), :], g_q[2 * g + 1, pl.ds(0, rows), :]], axis=1).astype(F32)
        query = jnp.where(own_block, jnp.concatenate([query] * 4, axis=0), 0.0).astype(BF16)
        score = lax.dot_general(keys[:, aligned(g, 256)], query, NT, preferred_element_type=F32) * factor
        most = jnp.max(score, axis=0, keepdims=True)
        weight = jnp.exp(score - most).astype(BF16)
        total = jnp.sum(weight.astype(F32), axis=0, keepdims=True)
        spread = jnp.dot(vt_mem[aligned(g, 256), :], weight, preferred_element_type=F32)
        taken = jnp.where(lane_head == 0, spread[0:64], 0.0)
        for head in range(1, 4):
            taken = jnp.where(lane_head == head, spread[head * 64 : head * 64 + 64], taken)
        stat = place(row8, split3(most) + split3(total))
        turned = pltpu.roll(taken, 64, 1)
        turned_stat = pltpu.roll(stat, 64, 1)
        s_g[2 * g, pl.ds(0, 32), :] = jnp.where(left, taken[0:32], turned[32:64]).astype(BF16)
        s_g[2 * g, pl.ds(32, 8), :] = jnp.where(left[0:8], stat, turned_stat).astype(BF16)
        s_g[2 * g + 1, pl.ds(0, 32), :] = jnp.where(left, turned[0:32], taken[32:64]).astype(BF16)
        s_g[2 * g + 1, pl.ds(32, 8), :] = jnp.where(left[0:8], turned_stat, stat).astype(BF16)

    own_group = lax.div(chip, 2)
    offsets = sorted(range(groups), key=lambda k: -min(k % 4, 4 - k % 4) if k else 1)
    waiting = []
    for first_at in range(0, groups, AT_ONCE):
        now = offsets[first_at : first_at + AT_ONCE]
        for offset in now:
            remember(lax.rem(own_group + offset, groups))
        for target in waiting:
            deliver(target)
        waiting = []
        for offset in now:
            g = lax.rem(own_group + offset, groups)
            waiting += [2 * g, 2 * g + 1] if offset else [chip + 1 - 2 * lax.rem(chip, 2)]
    for target in waiting:
        deliver(target)
    r_g[chip] = s_g[chip]

    def drain_g():
        for k in steps:
            target = chip_at(k)
            remote(s_g.at[target], r_g.at[chip], g_send.at[target], g_recv.at[chip], peer(k)).wait_send()

    drains.append(drain_g)
    for k in steps:
        source = chip_at(half - k)
        remote(s_g.at[chip], r_g.at[source], g_send.at[chip], g_recv.at[source], peer(half - k)).wait_recv()
    stats = [r_g[source, pl.ds(32, 8), :].astype(F32) for source in range(half)]
    mosts = [stat[0:1] + stat[1:2] + stat[2:3] for stat in stats]
    top = functools.reduce(jnp.maximum, mosts)
    over = jnp.zeros((32, LANES), F32)
    under = jnp.zeros((1, LANES), F32)
    for source in range(half):
        share = jnp.exp(mosts[source] - top)
        stat = stats[source]
        under = under + share * (stat[3:4] + stat[4:5] + stat[5:6])
        over = over + share * r_g[source, pl.ds(0, 32), :].astype(F32)
    turned = (over / under).T
    crossed = jnp.concatenate([turned[rows * at : rows * at + rows] for at in (0, 2, 1, 3)], axis=1).astype(BF16)

    s_h[...] = crossed
    g_h[chip] = crossed
    gather_start(s_h, g_h, h_send, h_recv)
    gather_wait(s_h, g_h, h_send, h_recv)
    everything = gathered(g_h)
    s_o[...] = jnp.dot(everything, wco[:, aligned(other_core)], preferred_element_type=F32)
    pair_start(s_o, r_o, 12)
    mine = middle + jnp.dot(everything, wco[:, aligned(core)], preferred_element_type=F32)
    pair_wait(s_o, r_o, 12)
    result[...] = (mine + r_o[...]).astype(BF16)
    leave = pltpu.make_async_copy(result, out_hbm, load_sem.at[14])
    leave.start()

    for drain in drains:
        drain()
    leave.wait()


def body(
    nb, nc, hidden_in, self_gain, w_self, w_self_out, cross_gain, w_cross_q, w_cross_out, cache_kv, memory_kv, parents, prefix_len
):
    rows = hidden_in.shape[0]
    d_model = w_self.shape[0]
    hyps = nb * rows
    cache_rows = cache_kv.shape[0] * cache_kv.shape[1] * cache_kv.shape[2]
    mem_count, mem_width = memory_kv.shape
    width = cache_rows // rows
    hbm = pl.BlockSpec(memory_space=pl.ANY)
    wide = nc * LANES
    chips = nc // 2

    def v(*shape):
        return pltpu.VMEM(shape, BF16)

    def f(*shape):
        return pltpu.VMEM(shape, F32)

    def sems(count):
        return pltpu.SemaphoreType.DMA((count,))

    return pl.pallas_call(
        functools.partial(kernel, nb, nc, d_model),
        out_shape=jax.ShapeDtypeStruct((rows, LANES), BF16),
        in_specs=[hbm] * 11,
        out_specs=hbm,
        scratch_shapes=[
            v(1, LANES), v(1, LANES), pltpu.VMEM((1, hyps), jnp.int32), pltpu.VMEM((1, hyps), jnp.int32), v(rows, LANES),
            v(d_model // 2, 6 * LANES), v(2 * LANES, wide // 2), v(2 * LANES, wide // 2), v(wide // 2, 2 * LANES),
            v(cache_rows, LANES), v(2 * mem_count, wide // 2), v(2 * mem_count, wide // 2), v(wide // 2, 2 * mem_count),
            v(width, rows * LANES), v(width, rows * LANES), v(hyps, rows * LANES), pltpu.VMEM((hyps, LANES), F32),
            v(rows + 8, LANES), v(chips, rows + 8, LANES), pltpu.VMEM((8, LANES), F32), pltpu.VMEM((8, 2 * LANES), F32),
            v(rows, LANES), v(hyps, LANES),
            v(hyps, 2 * LANES), v(nb, rows, 2 * LANES),
            v(rows, LANES), v(rows, 2 * LANES),
            v(chips, rows, LANES), v(chips, rows, LANES),
            v(rows, LANES), v(rows, 2 * LANES),
            v(chips, rows, LANES), v(chips, rows, LANES),
            v(rows + 8, LANES), v(chips, rows + 8, LANES),
            v(chips, 40, LANES), v(chips, 40, LANES),
            v(rows, LANES), v(chips, rows, LANES),
            f(rows, 4 * LANES), f(rows, 4 * LANES), f(rows, LANES), f(rows, LANES),
            sems(15), sems(13), sems(13),
            sems(chips), sems(chips), sems(nb), sems(nb), sems(nb), sems(nb), sems(chips), sems(chips),
            sems(chips), sems(chips), sems(chips), sems(chips), sems(chips), sems(chips), sems(chips), sems(chips),
        ],
        compiler_params=pltpu.CompilerParams(
            collective_id=0, has_side_effects=True, vmem_limit_bytes=VMEM_BYTES
        ),
    )(
        hidden_in,
        self_gain.reshape(1, LANES),
        cross_gain.reshape(1, LANES),
        parents.reshape(1, hyps),
        prefix_len.reshape(1, hyps),
        jnp.transpose(w_self, (1, 0, 2)),
        w_self_out,
        w_cross_q,
        w_cross_out,
        cache_kv.reshape(cache_rows, LANES),
        memory_kv,
    )


def solution(mesh):
    return jax.shard_map(
        functools.partial(body, mesh.shape["beam"], mesh.shape["blk"]),
        mesh=mesh,
        in_specs=(
            P("beam", "blk"),
            P("blk"),
            P(None, None, "blk"),
            P("blk", None),
            P("blk"),
            P("blk", None),
            P(None, "blk"),
            P("beam", None, "blk", None),
            P("blk", None),
            P(),
            P(),
        ),
        out_specs=P("beam", "blk"),
        check_vma=False,
    )
```

```python
import functools

import jax
import jax.numpy as jnp
from jax import lax
from jax.experimental import pallas as pl
from jax.experimental.pallas import tpu as pltpu
from jax.sharding import PartitionSpec as P

MESH = pl.DeviceIdType.MESH
F32 = jnp.float32
BF16 = jnp.bfloat16
NEG = -1e30
EPS = 1e-06
LANES = 128
VMEM_BYTES = 64000000
AT_ONCE = 2


def aligned(block, size=LANES):
    return pl.ds(pl.multiple_of(block * size, size), size)


def split3(x):
    high = x.astype(BF16).astype(F32)
    rest = x - high
    middle = rest.astype(BF16).astype(F32)
    return high, middle, rest - middle


def place(index, pieces):
    out = jnp.zeros(index.shape, F32)
    for at, piece in enumerate(pieces):
        out = jnp.where(index == at, piece, out)
    return out


NT = (((1,), (1,)), ((), ()))


def kernel(
    nb, nc, d_model,
    hid_hbm, sgain_hbm, cgain_hbm, parents_hbm, plen_hbm,
    wself_hbm, wso_hbm, wcq_hbm, wco_hbm, cache_hbm, mem_hbm,
    out_ref,
    sgain, cgain, parents, plen,
    wself, wso, wcq, wco, cache, keys, values, vt_mem, kt, vt, lhs_q, acc,
    s_a, g_a, s_x, g_x, s_c, g_c, s_d, r_d, s_t, g_t, s_e, r_e, s_m, g_m, s_f, r_f, s_q, g_q, s_g, r_g, s_h, g_h, s_p, r_p, s_o, r_o,
    load_sem, swap_send, swap_recv,
    a_send, a_recv, c_send, c_recv, d_send, d_recv, e_send, e_recv,
    f_send, f_recv, q_send, q_recv, g_send, g_recv, h_send, h_recv,
):
    rows = hid_hbm.shape[0]
    hyps = nb * rows
    half = nc // 2
    groups = half // 2
    score_scale = 64 ** (-0.5)
    head_width = mem_hbm.shape[1] // 2
    mem_rows = mem_hbm.shape[0]
    b = lax.axis_index("beam")
    c = lax.axis_index("blk")
    chip = lax.div(c, 2)
    core = lax.rem(c, 2)
    partner = c + 1 - 2 * core
    other_core = 1 - core
    def hops(k):
        return min(k % 8, 8 - k % 8)

    def slot(k):
        return (k + 2) % half

    steps = sorted(range(1, half), key=lambda k: -hops(k))
    far = sorted(slot(k) for k in range(half) if hops(k) >= 3)
    near = [at for at in range(half) if at not in far]

    barrier = pltpu.get_barrier_semaphore()

    def greet_blk(k, carry):
        pl.semaphore_signal(barrier, inc=1, device_id=(b, lax.rem(c + 2 * k, nc)), device_id_type=MESH)
        return carry

    def greet_beam(k, carry):
        pl.semaphore_signal(barrier, inc=1, device_id=(lax.rem(b + k, nb), c), device_id_type=MESH)
        return carry

    lax.fori_loop(1, half, greet_blk, 0)
    lax.fori_loop(1, nb, greet_beam, 0)
    pl.semaphore_signal(barrier, inc=1, device_id=(b, partner), device_id_type=MESH)

    loads = [
        pltpu.make_async_copy(hid_hbm, s_a.at[pl.ds(0, rows), :], load_sem.at[0]),
        pltpu.make_async_copy(sgain_hbm, sgain, load_sem.at[1]),
        pltpu.make_async_copy(cgain_hbm, cgain, load_sem.at[2]),
        pltpu.make_async_copy(parents_hbm, parents, load_sem.at[3]),
        pltpu.make_async_copy(plen_hbm, plen, load_sem.at[4]),
        pltpu.make_async_copy(cache_hbm, cache, load_sem.at[5]),
    ]
    for load in loads:
        load.start()
    loaded = set()
    drains = []
    swap_done = set()
    swap_begun = set()
    pair_open = []

    def ready(*which):
        for at in which:
            loads[at].wait()
            loaded.add(at)

    def columns(source, target, offset=0, absolute=False):
        height = source.shape[0]
        return (
            lambda g, side: source.at[:, aligned(offset + 2 * g + side)],
            lambda k, g, who: target.at[aligned(who, height), aligned(g if absolute else k)],
            lambda who: target.at[aligned(who, height), :],
        )

    def kind(which):
        return (
            lambda g, side: wself_hbm.at[which, aligned(2 * g + side), :],
            lambda k, g, who: wself.at[aligned(k), aligned(3 * who + which)],
            lambda who: wself.at[:, aligned(3 * who + which)],
        )

    out_rows = (
        lambda g, side: wco_hbm.at[aligned(2 * g + side), :],
        lambda k, g, who: wco.at[aligned(k), aligned(who)],
        lambda who: wco.at[:, aligned(who)],
    )
    shared = [
        kind(0), kind(1), kind(2), columns(wso_hbm, wso), columns(wcq_hbm, wcq),
        columns(mem_hbm, keys, 0, True), columns(mem_hbm, values, nc, True), out_rows,
    ]

    def keep(k, carry):
        g, at_slot = lax.rem(chip + k, half), lax.rem(k + 2, half)
        for at, (block, place_at, whole) in enumerate(shared):
            pltpu.make_async_copy(block(g, core), place_at(at_slot, g, core), load_sem.at[6 + at]).start()
        return carry

    lax.fori_loop(0, half, keep, 0)

    def remote(src, dst, send, recv, where):
        return pltpu.make_async_remote_copy(
            src_ref=src, dst_ref=dst, send_sem=send, recv_sem=recv, device_id=where, device_id_type=MESH
        )

    def peer(k):
        return (b, lax.rem(c + 2 * k, nc))

    def chip_at(k):
        return lax.rem(chip + k, half)

    def swap_start(*which):
        def step(k, carry):
            g, at_slot = lax.rem(chip + k, half), lax.rem(k + 2, half)
            for at in which:
                block, place_at, whole = shared[at]
                remote(
                    block(g, other_core), place_at(at_slot, g, core), swap_send.at[at], swap_recv.at[at], (b, partner)
                ).start()
            return carry

        lax.fori_loop(0, half, step, 0)
        swap_begun.update(which)

        def drain():
            for at in which:
                mine = shared[at][2](core)
                remote(mine, mine, swap_send.at[at], swap_recv.at[at], (b, partner)).wait_send()

        drains.append(drain)

    def swap_wait(*which):
        for at in which:
            swap_done.add(at)
            mine, theirs = shared[at][2](core), shared[at][2](other_core)
            pltpu.make_async_copy(mine, mine, load_sem.at[6 + at]).wait()
            if at in swap_begun:
                remote(theirs, theirs, swap_send.at[at], swap_recv.at[at], (b, partner)).wait_recv()

    def pair(src, dst, at):
        return remote(src, dst, swap_send.at[at], swap_recv.at[at], (b, partner))

    def pair_start(src, dst, at):
        pair(src, dst, at).start()
        pair_open.append((src, dst, at))
        drains.append(lambda: pair(src, dst, at).wait_send())

    def pair_wait(src, dst, at):
        pair_open[:] = [p for p in pair_open if p[2] != at]
        pair(src, dst, at).wait_recv()

    def gather_start(src, dst, send, recv):
        for k in steps:
            remote(src, dst.at[slot(half - k)], send.at[k], recv.at[slot(half - k)], peer(k)).start()
        drains.append(functools.partial(simple_drain, src, send))

    def gather_wait(src, dst, send, recv, which):
        for k in reversed(steps):
            at = slot(half - k)
            if at in which:
                remote(src, dst.at[at], send.at[k], recv.at[at], (b, partner)).wait_recv()

    def scatter_send(src, dst, send, recv, which):
        for k in steps:
            if slot(k) in which:
                remote(
                    src.at[slot(k)], dst.at[slot(half - k)], send.at[k], recv.at[slot(half - k)], peer(k)
                ).start()

    def scatter_products(products, src, dst, send, recv):
        before = None
        for which in (far, near):
            if which:
                terms = products(which)
                for at, which_slot in enumerate(which):
                    src[which_slot] = terms[:, at * LANES : at * LANES + LANES].astype(BF16)
                if before:
                    scatter_send(src, dst, send, recv, before)
                before = which
        scatter_send(src, dst, send, recv, before)
        drains.append(functools.partial(simple_drain, src.at[0], send))

    def taken_columns(ref, rows_at, which):
        return jnp.concatenate([ref[rows_at, pl.ds(at * LANES, LANES)] for at in which], axis=1)

    def simple_drain(block, send):
        def step(k, carry):
            remote(block, block, send.at[k], send.at[k], (b, partner)).wait_send()
            return carry

        lax.fori_loop(1, half, step, 0)

    def scatter_sum(src, dst, send, recv):
        total = src[slot(0)].astype(F32)
        for k in reversed(steps):
            at = slot(half - k)
            remote(src.at[at], dst.at[at], send.at[k], recv.at[at], (b, partner)).wait_recv()
            total = total + dst[at].astype(F32)
        return total

    ready(0, 1, 2)
    first = s_a[pl.ds(0, rows), :]
    gain_rows = jnp.broadcast_to(sgain[...].astype(F32), (8, LANES)).astype(BF16)
    s_a[pl.ds(rows, 8), :] = gain_rows
    g_a[slot(0), pl.ds(0, rows), :] = first
    g_a[slot(0), pl.ds(rows, 8), :] = gain_rows
    cgain_rows = jnp.broadcast_to(cgain[...].astype(F32), (8, LANES))
    s_x[...] = cgain_rows
    g_x[:, aligned(core)] = cgain_rows
    pl.semaphore_wait(barrier, half + nb - 1)
    gather_start(s_a, g_a, a_send, a_recv)
    pair_start(s_x, g_x.at[:, aligned(core)], 8)
    swap_start(0, 1, 2)

    ready(5)
    width = cache.shape[0] // rows

    def arrange(r, carry):
        x = cache[aligned(r, width), :].astype(F32)
        rolled = pltpu.roll(x, 64, 1)
        even = lax.rem(lax.broadcasted_iota(jnp.int32, x.shape, 0), 2) == 0
        low = lax.broadcasted_iota(jnp.int32, x.shape, 1) < 64
        kt[:, aligned(r)] = jnp.where(even, jnp.where(low, x, 0.0), jnp.where(low, 0.0, rolled)).astype(BF16)
        vt[:, aligned(r)] = jnp.where(even, jnp.where(low, rolled, 0.0), jnp.where(low, 0.0, x)).astype(BF16)
        return carry

    lax.fori_loop(0, rows, arrange, 0)
    ready(3, 4)
    local_wide = jnp.broadcast_to(parents[...], (LANES, hyps)).T - b * rows
    plen_wide = jnp.broadcast_to(plen[...], (LANES, hyps)).T
    swap_wait(0, 1, 2)

    def project(which):
        wide = jnp.concatenate([g_a[at, pl.ds(0, rows), :] for at in which], axis=1).astype(F32)
        gain = jnp.concatenate([g_a[at, pl.ds(rows, 8), :] for at in which], axis=1).astype(F32)[0:1, :]
        scaled = (wide * gain).astype(BF16)

        def columns_of(who):
            weight = jnp.concatenate([wself[pl.ds(at * LANES, LANES), aligned(who, 384)] for at in which], axis=0)
            return jnp.dot(scaled, weight, preferred_element_type=F32)

        return jnp.sum(wide * wide, axis=1, keepdims=True), columns_of

    gather_wait(s_a, g_a, a_send, a_recv, near)
    squares, columns_of = project(near)
    theirs, mine = columns_of(other_core), columns_of(core)
    gather_wait(s_a, g_a, a_send, a_recv, far)
    if far:
        far_squares, columns_of = project(far)
        squares = squares + far_squares
        theirs = theirs + columns_of(other_core)
    squares = jnp.broadcast_to(squares, (rows, LANES))
    s_p[:, pl.ds(0, 384)] = theirs
    s_p[:, pl.ds(384, LANES)] = squares
    pair_start(s_p, r_p, 9)
    if far:
        mine = mine + columns_of(core)
    pair_wait(s_p, r_p, 9)
    joined = mine + r_p[:, pl.ds(0, 384)]
    self_scale = lax.rsqrt((squares + r_p[:, pl.ds(384, LANES)]) * (1.0 / d_model) + EPS)
    queries = (joined[:, :LANES] * self_scale).astype(BF16)

    s_c[...] = queries
    g_c[aligned(b, rows), :] = queries
    my_queries = g_c.at[aligned(b, rows), :]

    def send_c(k, carry):
        remote(s_c, my_queries, c_send.at[k], c_recv.at[b], (lax.rem(b + k, nb), c)).start()
        return carry

    lax.fori_loop(1, nb, send_c, 0)

    def drain_c():
        def step(k, carry):
            remote(s_c, my_queries, c_send.at[k], c_recv.at[b], (b, partner)).wait_send()
            return carry

        lax.fori_loop(1, nb, step, 0)

    drains.append(drain_c)
    swap_start(3, 4, 5, 6, 7)
    own_values = (joined[:, 2 * LANES : 3 * LANES] * self_scale).astype(BF16).astype(F32)
    products = queries.astype(F32) * (joined[:, LANES : 2 * LANES] * self_scale).astype(BF16).astype(F32)
    low = lax.broadcasted_iota(jnp.int32, products.shape, 1) < 64
    own_0 = jnp.sum(jnp.where(low, products, 0.0), axis=1, keepdims=True) * score_scale
    own_1 = jnp.sum(jnp.where(low, 0.0, products), axis=1, keepdims=True) * score_scale

    def wait_c(k, carry):
        source = lax.rem(b + k, nb)
        remote(s_c, g_c.at[aligned(source, rows), :], c_send.at[k], c_recv.at[source], (source, c)).wait_recv()
        return carry

    lax.fori_loop(1, nb, wait_c, 0)

    all_queries = g_c[...]
    nothing = jnp.zeros(all_queries.shape, BF16)
    local_16 = local_wide.astype(F32).astype(BF16)
    for r in range(rows):
        lhs_q[:, pl.ds(r * LANES, LANES)] = jnp.where(local_16 == r, all_queries, nothing)
    scores = lax.dot_general(lhs_q[...], kt[...], NT, preferred_element_type=F32) * score_scale
    lane = lax.broadcasted_iota(jnp.int32, scores.shape, 1)
    even = lax.rem(lane, 2) == 0
    tiles = width // LANES
    visible = lax.div(lane, 2) < jnp.concatenate([plen_wide] * tiles, axis=1)
    masked = jnp.where(visible, scores, NEG)
    max_0 = jnp.max(jnp.where(even, masked, NEG), axis=1, keepdims=True)
    max_1 = jnp.max(jnp.where(even, NEG, masked), axis=1, keepdims=True)
    weights = jnp.where(visible, jnp.exp(masked - jnp.where(even, max_0, max_1)), 0.0).astype(BF16)
    lhs_q[:, pl.ds(0, width)] = weights
    weights = weights.astype(F32)
    total_0 = jnp.sum(jnp.where(even, weights, 0.0), axis=1, keepdims=True)
    total_1 = jnp.sum(jnp.where(even, 0.0, weights), axis=1, keepdims=True)
    weights = lhs_q[:, pl.ds(0, width)]
    acc[...] = jnp.zeros(acc.shape, F32)
    for r in range(0, rows, 2):
        both = jnp.dot(weights, vt[:, pl.ds(r * LANES, 2 * LANES)], preferred_element_type=F32)
        picked = jnp.where(local_wide == r, both[:, :LANES], acc[...])
        acc[...] = jnp.where(local_wide == r + 1, both[:, LANES:], picked)
    summed = acc[...]
    lane = lax.broadcasted_iota(jnp.int32, summed.shape, 1)
    here = (local_wide >= 0) & (local_wide < rows)
    part = summed / jnp.where(lane < 64, total_0, total_1)
    pieces = split3(max_0 + jnp.log(total_0)) + split3(max_1 + jnp.log(total_1))
    s_d[:, pl.ds(0, LANES)] = part.astype(BF16)
    s_d[:, pl.ds(LANES, LANES)] = jnp.where(here, place(lane, pieces), 0.0).astype(BF16)

    def send_d(k, carry):
        target = lax.rem(b + k, nb)
        remote(s_d.at[aligned(target, rows), :], r_d.at[b], d_send.at[k], d_recv.at[b], (target, c)).start()
        return carry

    lax.fori_loop(1, nb, send_d, 0)

    def drain_d():
        def step(k, carry):
            remote(s_d.at[aligned(b, rows), :], r_d.at[b], d_send.at[k], d_recv.at[b], (b, partner)).wait_send()
            return carry

        lax.fori_loop(1, nb, step, 0)

    drains.append(drain_d)
    swap_wait(3, 4)

    def wait_d(k, total):
        source = lax.rem(b + k, nb)
        remote(s_d.at[aligned(b, rows), :], r_d.at[source], d_send.at[k], d_recv.at[source], (source, c)).wait_recv()
        return total + r_d[source].astype(F32)

    back = lax.fori_loop(1, nb, wait_d, s_d[aligned(b, rows), :].astype(F32))
    stats = back[:, LANES:]
    log_0 = stats[:, 0:1] + stats[:, 1:2] + stats[:, 2:3]
    log_1 = stats[:, 3:4] + stats[:, 4:5] + stats[:, 5:6]
    cache_log = jnp.where(low, log_0, log_1)
    own_log = jnp.where(low, own_0, own_1)
    top = jnp.maximum(cache_log, own_log)
    cache_weight = jnp.exp(cache_log - top)
    own_weight = jnp.exp(own_log - top)
    attended = (cache_weight * back[:, :LANES] + own_weight * own_values) / (cache_weight + own_weight)
    attended = attended.astype(BF16)
    s_t[...] = attended
    g_t[:, aligned(core)] = attended
    pair_start(s_t, g_t.at[:, aligned(core)], 10)

    mine = {
        len(which): jnp.dot(attended, taken_columns(wso, aligned(core), which), preferred_element_type=F32)
        for which in (far, near) if which
    }
    pair_wait(s_t, g_t.at[:, aligned(other_core)], 10)
    theirs = g_t[:, aligned(other_core)]
    scatter_products(
        lambda which: mine[len(which)]
        + jnp.dot(theirs, taken_columns(wso, aligned(other_core), which), preferred_element_type=F32),
        s_e, r_e, e_send, e_recv,
    )
    swap_wait(5, 6, 7)

    def turn(g, carry):
        vt_mem[aligned(g, 256), :] = values[:, aligned(g, 256)].T
        return carry

    lax.fori_loop(0, groups, turn, 0)
    mixed = scatter_sum(s_e, r_e, e_send, e_recv)
    middle_16 = (first.astype(F32) + mixed).astype(BF16)
    middle = middle_16.astype(F32)

    s_m[...] = middle_16
    g_m[:, aligned(core)] = middle_16
    pair_start(s_m, g_m.at[:, aligned(core)], 11)
    pair_wait(s_x, g_x.at[:, aligned(other_core)], 8)
    pair_wait(s_m, g_m.at[:, aligned(other_core)], 11)
    both_middle = g_m[...].astype(F32)
    cross_scaled = (both_middle * g_x[0:1, :]).astype(BF16)
    scatter_products(
        lambda which: jnp.dot(cross_scaled, taken_columns(wcq, slice(None), which), preferred_element_type=F32),
        s_f, r_f, f_send, f_recv,
    )
    squares = jnp.broadcast_to(jnp.sum(both_middle * both_middle, axis=1, keepdims=True), (rows, LANES))
    squares = jnp.concatenate([squares] * (LANES // rows), axis=0).T[0:1, :]
    row8 = lax.broadcasted_iota(jnp.int32, (8, LANES), 0)
    square_rows = place(row8, split3(squares)).astype(BF16)
    s_q[pl.ds(rows, 8), :] = square_rows
    g_q[slot(0), pl.ds(rows, 8), :] = square_rows
    raw = scatter_sum(s_f, r_f, f_send, f_recv).astype(BF16)
    s_q[pl.ds(0, rows), :] = raw
    g_q[slot(0), pl.ds(0, rows), :] = raw

    gather_start(s_q, g_q, q_send, q_recv)
    gather_wait(s_q, g_q, q_send, q_recv, far + near)
    sums = jnp.zeros((8, LANES), F32)
    for k in range(half):
        sums = sums + g_q[k, pl.ds(rows, 8), :].astype(F32)
    mean = (sums[0:1, :] + sums[1:2, :] + sums[2:3, :]) * (1.0 / d_model)
    factor = lax.rsqrt(mean + EPS) * score_scale

    own_block = (
        lax.div(lax.broadcasted_iota(jnp.int32, (LANES, 256), 0), rows)
        == lax.div(lax.broadcasted_iota(jnp.int32, (LANES, 256), 1), 64)
    )
    lane_head = lax.div(lax.broadcasted_iota(jnp.int32, (64, LANES), 1), rows)
    left = lax.broadcasted_iota(jnp.int32, (32, LANES), 1) < 64

    def deliver(target):
        remote(s_g.at[target], r_g.at[chip], g_send.at[target], g_recv.at[chip], (b, 2 * target + core)).start()

    def remember(g):
        query = jnp.concatenate(
            [g_q[lax.rem(2 * g + which - chip + half + 2, half), pl.ds(0, rows), :] for which in range(2)], axis=1
        ).astype(F32)
        query = jnp.where(own_block, jnp.concatenate([query] * 4, axis=0), 0.0).astype(BF16)
        score = lax.dot_general(keys[:, aligned(g, 256)], query, NT, preferred_element_type=F32) * factor
        most = jnp.max(score, axis=0, keepdims=True)
        weight = jnp.exp(score - most).astype(BF16)
        total = jnp.sum(weight.astype(F32), axis=0, keepdims=True)
        spread = jnp.dot(vt_mem[aligned(g, 256), :], weight, preferred_element_type=F32)
        taken = jnp.where(lane_head == 0, spread[0:64], 0.0)
        for head in range(1, 4):
            taken = jnp.where(lane_head == head, spread[head * 64 : head * 64 + 64], taken)
        stat = place(row8, split3(most) + split3(total))
        turned = pltpu.roll(taken, 64, 1)
        turned_stat = pltpu.roll(stat, 64, 1)
        s_g[2 * g, pl.ds(0, 32), :] = jnp.where(left, taken[0:32], turned[32:64]).astype(BF16)
        s_g[2 * g, pl.ds(32, 8), :] = jnp.where(left[0:8], stat, turned_stat).astype(BF16)
        s_g[2 * g + 1, pl.ds(0, 32), :] = jnp.where(left, turned[0:32], taken[32:64]).astype(BF16)
        s_g[2 * g + 1, pl.ds(32, 8), :] = jnp.where(left[0:8], turned_stat, stat).astype(BF16)

    own_group = lax.div(chip, 2)
    offsets = sorted(range(groups), key=lambda k: -min(k % 4, 4 - k % 4) if k else 1)
    waiting = []
    for first_at in range(0, groups, AT_ONCE):
        now = offsets[first_at : first_at + AT_ONCE]
        for offset in now:
            remember(lax.rem(own_group + offset, groups))
        for target in waiting:
            deliver(target)
        waiting = []
        for offset in now:
            g = lax.rem(own_group + offset, groups)
            waiting += [2 * g, 2 * g + 1] if offset else [chip + 1 - 2 * lax.rem(chip, 2)]
    for target in waiting:
        deliver(target)
    r_g[chip] = s_g[chip]

    def drain_g():
        for k in steps:
            target = chip_at(k)
            remote(s_g.at[target], r_g.at[chip], g_send.at[target], g_recv.at[chip], peer(k)).wait_send()

    drains.append(drain_g)
    for k in steps:
        source = chip_at(half - k)
        remote(s_g.at[chip], r_g.at[source], g_send.at[chip], g_recv.at[source], peer(half - k)).wait_recv()
    stats = [r_g[source, pl.ds(32, 8), :].astype(F32) for source in range(half)]
    mosts = [stat[0:1] + stat[1:2] + stat[2:3] for stat in stats]
    top = functools.reduce(jnp.maximum, mosts)
    over = jnp.zeros((32, LANES), F32)
    under = jnp.zeros((1, LANES), F32)
    for source in range(half):
        share = jnp.exp(mosts[source] - top)
        stat = stats[source]
        under = under + share * (stat[3:4] + stat[4:5] + stat[5:6])
        over = over + share * r_g[source, pl.ds(0, 32), :].astype(F32)
    turned = (over / under).T
    crossed = jnp.concatenate([turned[rows * at : rows * at + rows] for at in (0, 2, 1, 3)], axis=1).astype(BF16)

    s_h[...] = crossed
    g_h[slot(0)] = crossed
    gather_start(s_h, g_h, h_send, h_recv)

    def products(which, who):
        block = jnp.concatenate([g_h[at] for at in which], axis=1)
        weight = jnp.concatenate([wco[pl.ds(at * LANES, LANES), aligned(who)] for at in which], axis=0)
        return jnp.dot(block, weight, preferred_element_type=F32)

    gather_wait(s_h, g_h, h_send, h_recv, near)
    theirs, mine = products(near, other_core), middle + products(near, core)
    gather_wait(s_h, g_h, h_send, h_recv, far)
    if far:
        theirs = theirs + products(far, other_core)
    s_o[...] = theirs
    pair_start(s_o, r_o, 12)
    if far:
        mine = mine + products(far, core)
    pair_wait(s_o, r_o, 12)
    out_ref[...] = (mine + r_o[...]).astype(BF16)

    for drain in drains:
        drain()


def body(
    nb, nc, hidden_in, self_gain, w_self, w_self_out, cross_gain, w_cross_q, w_cross_out, cache_kv, memory_kv, parents, prefix_len
):
    rows = hidden_in.shape[0]
    d_model = w_self.shape[0]
    hyps = nb * rows
    cache_rows = cache_kv.shape[0] * cache_kv.shape[1] * cache_kv.shape[2]
    mem_count, mem_width = memory_kv.shape
    width = cache_rows // rows
    hbm = pl.BlockSpec(memory_space=pl.ANY)
    wide = nc * LANES
    chips = nc // 2

    def v(*shape):
        return pltpu.VMEM(shape, BF16)

    def f(*shape):
        return pltpu.VMEM(shape, F32)

    def sems(count):
        return pltpu.SemaphoreType.DMA((count,))

    return pl.pallas_call(
        functools.partial(kernel, nb, nc, d_model),
        out_shape=pltpu.VMEM((rows, LANES), BF16),
        in_specs=[hbm] * 11,
        out_specs=pl.BlockSpec(memory_space=pltpu.VMEM),
        scratch_shapes=[
            v(1, LANES), v(1, LANES), pltpu.VMEM((1, hyps), jnp.int32), pltpu.VMEM((1, hyps), jnp.int32),
            v(d_model // 2, 6 * LANES), v(2 * LANES, wide // 2), v(2 * LANES, wide // 2), v(wide // 2, 2 * LANES),
            v(cache_rows, LANES), v(2 * mem_count, wide // 2), v(2 * mem_count, wide // 2), v(wide // 2, 2 * mem_count),
            v(width, rows * LANES), v(width, rows * LANES), v(hyps, rows * LANES), pltpu.VMEM((hyps, LANES), F32),
            v(rows + 8, LANES), v(chips, rows + 8, LANES), pltpu.VMEM((8, LANES), F32), pltpu.VMEM((8, 2 * LANES), F32),
            v(rows, LANES), v(hyps, LANES),
            v(hyps, 2 * LANES), v(nb, rows, 2 * LANES),
            v(rows, LANES), v(rows, 2 * LANES),
            v(chips, rows, LANES), v(chips, rows, LANES),
            v(rows, LANES), v(rows, 2 * LANES),
            v(chips, rows, LANES), v(chips, rows, LANES),
            v(rows + 8, LANES), v(chips, rows + 8, LANES),
            v(chips, 40, LANES), v(chips, 40, LANES),
            v(rows, LANES), v(chips, rows, LANES),
            f(rows, 4 * LANES), f(rows, 4 * LANES), f(rows, LANES), f(rows, LANES),
            sems(15), sems(13), sems(13),
            sems(chips), sems(chips), sems(nb), sems(nb), sems(nb), sems(nb), sems(chips), sems(chips),
            sems(chips), sems(chips), sems(chips), sems(chips), sems(chips), sems(chips), sems(chips), sems(chips),
        ],
        compiler_params=pltpu.CompilerParams(
            collective_id=0, has_side_effects=True, vmem_limit_bytes=VMEM_BYTES
        ),
    )(
        hidden_in,
        self_gain.reshape(1, LANES),
        cross_gain.reshape(1, LANES),
        parents.reshape(1, hyps),
        prefix_len.reshape(1, hyps),
        jnp.transpose(w_self, (1, 0, 2)),
        w_self_out,
        w_cross_q,
        w_cross_out,
        cache_kv.reshape(cache_rows, LANES),
        memory_kv,
    )


def solution(mesh):
    return jax.shard_map(
        functools.partial(body, mesh.shape["beam"], mesh.shape["blk"]),
        mesh=mesh,
        in_specs=(
            P("beam", "blk"),
            P("blk"),
            P(None, None, "blk"),
            P("blk", None),
            P("blk"),
            P("blk", None),
            P(None, "blk"),
            P("beam", None, "blk", None),
            P("blk", None),
            P(),
            P(),
        ),
        out_specs=P("beam", "blk"),
        check_vma=False,
    )
```

```python
import functools

import jax
import jax.numpy as jnp
from jax import lax
from jax.experimental import pallas as pl
from jax.experimental.pallas import tpu as pltpu
from jax.sharding import PartitionSpec as P

MESH = pl.DeviceIdType.MESH
F32 = jnp.float32
BF16 = jnp.bfloat16
NEG = -1e30
EPS = 1e-06
LANES = 128
VMEM_BYTES = 64000000
AT_ONCE = 2


def aligned(block, size=LANES):
    return pl.ds(pl.multiple_of(block * size, size), size)


def split3(x):
    high = x.astype(BF16).astype(F32)
    rest = x - high
    middle = rest.astype(BF16).astype(F32)
    return high, middle, rest - middle


def place(index, pieces):
    out = jnp.zeros(index.shape, F32)
    for at, piece in enumerate(pieces):
        out = jnp.where(index == at, piece, out)
    return out


NT = (((1,), (1,)), ((), ()))


def kernel(
    nb, nc, d_model,
    hid_hbm, sgain_hbm, cgain_hbm, parents_hbm, plen_hbm,
    wself_hbm, wso_hbm, wcq_hbm, wco_hbm, cache_hbm, mem_hbm,
    out_ref,
    sgain, cgain, parents, plen,
    wself, wso, wcq, wco, cache, keys, values, vt_mem, kt, vt, lhs_q, acc,
    s_a, g_a, s_x, g_x, s_c, g_c, s_d, r_d, s_t, g_t, s_e, r_e, s_m, g_m, s_f, r_f, s_q, g_q, s_g, r_g, s_h, g_h, s_p, r_p, s_o, r_o, s_n, g_n,
    load_sem, swap_send, swap_recv,
    a_send, a_recv, c_send, c_recv, d_send, d_recv, e_send, e_recv,
    f_send, f_recv, q_send, q_recv, g_send, g_recv, h_send, h_recv, n_send, n_recv,
):
    rows = hid_hbm.shape[0]
    hyps = nb * rows
    half = nc // 2
    groups = half // 2
    score_scale = 64 ** (-0.5)
    head_width = mem_hbm.shape[1] // 2
    mem_rows = mem_hbm.shape[0]
    b = lax.axis_index("beam")
    c = lax.axis_index("blk")
    chip = lax.div(c, 2)
    core = lax.rem(c, 2)
    partner = c + 1 - 2 * core
    other_core = 1 - core
    def hops(k):
        return min(k % 8, 8 - k % 8)

    def slot(k):
        return (k + 2) % half

    steps = sorted(range(1, half), key=lambda k: -hops(k))
    far = sorted(slot(k) for k in range(half) if hops(k) >= 3)
    near = [at for at in range(half) if at not in far]

    barrier = pltpu.get_barrier_semaphore()

    def greet_blk(k, carry):
        pl.semaphore_signal(barrier, inc=1, device_id=(b, lax.rem(c + 2 * k, nc)), device_id_type=MESH)
        return carry

    def greet_beam(k, carry):
        pl.semaphore_signal(barrier, inc=1, device_id=(lax.rem(b + k, nb), c), device_id_type=MESH)
        return carry

    lax.fori_loop(1, half, greet_blk, 0)
    lax.fori_loop(1, nb, greet_beam, 0)
    pl.semaphore_signal(barrier, inc=1, device_id=(b, partner), device_id_type=MESH)

    loads = [
        pltpu.make_async_copy(hid_hbm, s_a.at[pl.ds(0, rows), :], load_sem.at[0]),
        pltpu.make_async_copy(sgain_hbm, sgain, load_sem.at[1]),
        pltpu.make_async_copy(cgain_hbm, cgain, load_sem.at[2]),
        pltpu.make_async_copy(parents_hbm, parents, load_sem.at[3]),
        pltpu.make_async_copy(plen_hbm, plen, load_sem.at[4]),
        pltpu.make_async_copy(cache_hbm, cache, load_sem.at[5]),
    ]
    for load in loads:
        load.start()
    loaded = set()
    drains = []
    swap_done = set()
    swap_begun = set()
    pair_open = []

    def ready(*which):
        for at in which:
            loads[at].wait()
            loaded.add(at)

    def columns(source, target, offset=0, absolute=False):
        height = source.shape[0]
        return (
            lambda g, side: source.at[:, aligned(offset + 2 * g + side)],
            lambda k, g, who: target.at[aligned(who, height), aligned(g if absolute else k)],
            lambda who: target.at[aligned(who, height), :],
        )

    def kind(which):
        return (
            lambda g, side: wself_hbm.at[which, aligned(2 * g + side), :],
            lambda k, g, who: wself.at[aligned(k), aligned(3 * who + which)],
            lambda who: wself.at[:, aligned(3 * who + which)],
        )

    out_rows = (
        lambda g, side: wco_hbm.at[aligned(2 * g + side), :],
        lambda k, g, who: wco.at[aligned(k), aligned(who)],
        lambda who: wco.at[:, aligned(who)],
    )
    shared = [
        kind(0), kind(1), kind(2), columns(wso_hbm, wso), columns(wcq_hbm, wcq),
        columns(mem_hbm, keys, 0, True), columns(mem_hbm, values, nc, True), out_rows,
    ]

    def keep(k, carry):
        g, at_slot = lax.rem(chip + k, half), lax.rem(k + 2, half)
        for at, (block, place_at, whole) in enumerate(shared):
            pltpu.make_async_copy(block(g, core), place_at(at_slot, g, core), load_sem.at[6 + at]).start()
        return carry

    lax.fori_loop(0, half, keep, 0)

    def remote(src, dst, send, recv, where):
        return pltpu.make_async_remote_copy(
            src_ref=src, dst_ref=dst, send_sem=send, recv_sem=recv, device_id=where, device_id_type=MESH
        )

    def peer(k):
        return (b, lax.rem(c + 2 * k, nc))

    def chip_at(k):
        return lax.rem(chip + k, half)

    def swap_start(*which):
        def step(k, carry):
            g, at_slot = lax.rem(chip + k, half), lax.rem(k + 2, half)
            for at in which:
                block, place_at, whole = shared[at]
                remote(
                    block(g, other_core), place_at(at_slot, g, core), swap_send.at[at], swap_recv.at[at], (b, partner)
                ).start()
            return carry

        lax.fori_loop(0, half, step, 0)
        swap_begun.update(which)

        def drain():
            for at in which:
                mine = shared[at][2](core)
                remote(mine, mine, swap_send.at[at], swap_recv.at[at], (b, partner)).wait_send()

        drains.append(drain)

    def swap_wait(*which):
        for at in which:
            swap_done.add(at)
            mine, theirs = shared[at][2](core), shared[at][2](other_core)
            pltpu.make_async_copy(mine, mine, load_sem.at[6 + at]).wait()
            if at in swap_begun:
                remote(theirs, theirs, swap_send.at[at], swap_recv.at[at], (b, partner)).wait_recv()

    def pair(src, dst, at):
        return remote(src, dst, swap_send.at[at], swap_recv.at[at], (b, partner))

    def pair_start(src, dst, at):
        pair(src, dst, at).start()
        pair_open.append((src, dst, at))
        drains.append(lambda: pair(src, dst, at).wait_send())

    def pair_wait(src, dst, at):
        pair_open[:] = [p for p in pair_open if p[2] != at]
        pair(src, dst, at).wait_recv()

    def gather_start(src, dst, send, recv):
        for k in steps:
            remote(src, dst.at[slot(half - k)], send.at[k], recv.at[slot(half - k)], peer(k)).start()
        drains.append(functools.partial(simple_drain, src, send))

    def gather_wait(src, dst, send, recv, which):
        for k in reversed(steps):
            at = slot(half - k)
            if at in which:
                remote(src, dst.at[at], send.at[k], recv.at[at], (b, partner)).wait_recv()

    def scatter_send(src, dst, send, recv, which):
        for k in steps:
            if slot(k) in which:
                remote(
                    src.at[slot(k)], dst.at[slot(half - k)], send.at[k], recv.at[slot(half - k)], peer(k)
                ).start()

    def scatter_products(products, src, dst, send, recv):
        before = None
        for which in (far, near):
            if which:
                terms = products(which)
                for at, which_slot in enumerate(which):
                    src[which_slot] = terms[:, at * LANES : at * LANES + LANES].astype(BF16)
                if before:
                    scatter_send(src, dst, send, recv, before)
                before = which
        scatter_send(src, dst, send, recv, before)
        drains.append(functools.partial(simple_drain, src.at[0], send))

    def taken_columns(ref, rows_at, which):
        return jnp.concatenate([ref[rows_at, pl.ds(at * LANES, LANES)] for at in which], axis=1)

    def simple_drain(block, send):
        def step(k, carry):
            remote(block, block, send.at[k], send.at[k], (b, partner)).wait_send()
            return carry

        lax.fori_loop(1, half, step, 0)

    def scatter_sum(src, dst, send, recv):
        total = src[slot(0)].astype(F32)
        for k in reversed(steps):
            at = slot(half - k)
            remote(src.at[at], dst.at[at], send.at[k], recv.at[at], (b, partner)).wait_recv()
            total = total + dst[at].astype(F32)
        return total

    ready(0, 1, 2)
    first = s_a[pl.ds(0, rows), :]
    gain_rows = jnp.broadcast_to(sgain[...].astype(F32), (8, LANES)).astype(BF16)
    s_a[pl.ds(rows, 8), :] = gain_rows
    g_a[slot(0), pl.ds(0, rows), :] = first
    g_a[slot(0), pl.ds(rows, 8), :] = gain_rows
    cgain_rows = jnp.broadcast_to(cgain[...].astype(F32), (8, LANES))
    s_x[...] = cgain_rows
    g_x[:, aligned(core)] = cgain_rows
    pl.semaphore_wait(barrier, half + nb - 1)
    gather_start(s_a, g_a, a_send, a_recv)
    pair_start(s_x, g_x.at[:, aligned(core)], 8)
    swap_start(0, 1, 2)

    ready(5)
    width = cache.shape[0] // rows

    def arrange(r, carry):
        x = cache[aligned(r, width), :].astype(F32)
        rolled = pltpu.roll(x, 64, 1)
        even = lax.rem(lax.broadcasted_iota(jnp.int32, x.shape, 0), 2) == 0
        low = lax.broadcasted_iota(jnp.int32, x.shape, 1) < 64
        kt[:, aligned(r)] = jnp.where(even, jnp.where(low, x, 0.0), jnp.where(low, 0.0, rolled)).astype(BF16)
        vt[:, aligned(r)] = jnp.where(even, jnp.where(low, rolled, 0.0), jnp.where(low, 0.0, x)).astype(BF16)
        return carry

    lax.fori_loop(0, rows, arrange, 0)
    ready(3, 4)
    local_wide = jnp.broadcast_to(parents[...], (LANES, hyps)).T - b * rows
    plen_wide = jnp.broadcast_to(plen[...], (LANES, hyps)).T
    swap_wait(0, 1, 2)

    def project(which):
        wide = jnp.concatenate([g_a[at, pl.ds(0, rows), :] for at in which], axis=1).astype(F32)
        gain = jnp.concatenate([g_a[at, pl.ds(rows, 8), :] for at in which], axis=1).astype(F32)[0:1, :]
        scaled = (wide * gain).astype(BF16)

        def columns_of(who):
            weight = jnp.concatenate([wself[pl.ds(at * LANES, LANES), aligned(who, 384)] for at in which], axis=0)
            return jnp.dot(scaled, weight, preferred_element_type=F32)

        return jnp.sum(wide * wide, axis=1, keepdims=True), columns_of

    gather_wait(s_a, g_a, a_send, a_recv, near)
    squares, columns_of = project(near)
    theirs, mine = columns_of(other_core), columns_of(core)
    gather_wait(s_a, g_a, a_send, a_recv, far)
    if far:
        far_squares, columns_of = project(far)
        squares = squares + far_squares
        theirs = theirs + columns_of(other_core)
    squares = jnp.broadcast_to(squares, (rows, LANES))
    s_p[:, pl.ds(0, 384)] = theirs
    s_p[:, pl.ds(384, LANES)] = squares
    pair_start(s_p, r_p, 9)
    if far:
        mine = mine + columns_of(core)
    pair_wait(s_p, r_p, 9)
    joined = mine + r_p[:, pl.ds(0, 384)]
    self_scale = lax.rsqrt((squares + r_p[:, pl.ds(384, LANES)]) * (1.0 / d_model) + EPS)
    queries = (joined[:, :LANES] * self_scale).astype(BF16)

    s_c[...] = queries
    g_c[aligned(b, rows), :] = queries
    my_queries = g_c.at[aligned(b, rows), :]

    def send_c(k, carry):
        remote(s_c, my_queries, c_send.at[k], c_recv.at[b], (lax.rem(b + k, nb), c)).start()
        return carry

    lax.fori_loop(1, nb, send_c, 0)

    def drain_c():
        def step(k, carry):
            remote(s_c, my_queries, c_send.at[k], c_recv.at[b], (b, partner)).wait_send()
            return carry

        lax.fori_loop(1, nb, step, 0)

    drains.append(drain_c)
    swap_start(3, 4, 5, 6, 7)
    own_values = (joined[:, 2 * LANES : 3 * LANES] * self_scale).astype(BF16).astype(F32)
    products = queries.astype(F32) * (joined[:, LANES : 2 * LANES] * self_scale).astype(BF16).astype(F32)
    low = lax.broadcasted_iota(jnp.int32, products.shape, 1) < 64
    own_0 = jnp.sum(jnp.where(low, products, 0.0), axis=1, keepdims=True) * score_scale
    own_1 = jnp.sum(jnp.where(low, 0.0, products), axis=1, keepdims=True) * score_scale

    def wait_c(k, carry):
        source = lax.rem(b + k, nb)
        remote(s_c, g_c.at[aligned(source, rows), :], c_send.at[k], c_recv.at[source], (source, c)).wait_recv()
        return carry

    lax.fori_loop(1, nb, wait_c, 0)

    all_queries = g_c[...]
    nothing = jnp.zeros(all_queries.shape, BF16)
    local_16 = local_wide.astype(F32).astype(BF16)
    for r in range(rows):
        lhs_q[:, pl.ds(r * LANES, LANES)] = jnp.where(local_16 == r, all_queries, nothing)
    scores = lax.dot_general(lhs_q[...], kt[...], NT, preferred_element_type=F32) * score_scale
    lane = lax.broadcasted_iota(jnp.int32, scores.shape, 1)
    even = lax.rem(lane, 2) == 0
    tiles = width // LANES
    visible = lax.div(lane, 2) < jnp.concatenate([plen_wide] * tiles, axis=1)
    masked = jnp.where(visible, scores, NEG)
    max_0 = jnp.max(jnp.where(even, masked, NEG), axis=1, keepdims=True)
    max_1 = jnp.max(jnp.where(even, NEG, masked), axis=1, keepdims=True)
    weights = jnp.where(visible, jnp.exp(masked - jnp.where(even, max_0, max_1)), 0.0).astype(BF16)
    lhs_q[:, pl.ds(0, width)] = weights
    weights = weights.astype(F32)
    total_0 = jnp.sum(jnp.where(even, weights, 0.0), axis=1, keepdims=True)
    total_1 = jnp.sum(jnp.where(even, 0.0, weights), axis=1, keepdims=True)
    weights = lhs_q[:, pl.ds(0, width)]
    acc[...] = jnp.zeros(acc.shape, F32)
    for r in range(0, rows, 2):
        both = jnp.dot(weights, vt[:, pl.ds(r * LANES, 2 * LANES)], preferred_element_type=F32)
        picked = jnp.where(local_wide == r, both[:, :LANES], acc[...])
        acc[...] = jnp.where(local_wide == r + 1, both[:, LANES:], picked)
    summed = acc[...]
    lane = lax.broadcasted_iota(jnp.int32, summed.shape, 1)
    here = (local_wide >= 0) & (local_wide < rows)
    part = summed / jnp.where(lane < 64, total_0, total_1)
    pieces = split3(max_0 + jnp.log(total_0)) + split3(max_1 + jnp.log(total_1))
    s_d[:, pl.ds(0, LANES)] = part.astype(BF16)
    s_d[:, pl.ds(LANES, LANES)] = jnp.where(here, place(lane, pieces), 0.0).astype(BF16)

    def send_d(k, carry):
        target = lax.rem(b + k, nb)
        remote(s_d.at[aligned(target, rows), :], r_d.at[b], d_send.at[k], d_recv.at[b], (target, c)).start()
        return carry

    lax.fori_loop(1, nb, send_d, 0)

    def drain_d():
        def step(k, carry):
            remote(s_d.at[aligned(b, rows), :], r_d.at[b], d_send.at[k], d_recv.at[b], (b, partner)).wait_send()
            return carry

        lax.fori_loop(1, nb, step, 0)

    drains.append(drain_d)
    swap_wait(3, 4)

    def wait_d(k, total):
        source = lax.rem(b + k, nb)
        remote(s_d.at[aligned(b, rows), :], r_d.at[source], d_send.at[k], d_recv.at[source], (source, c)).wait_recv()
        return total + r_d[source].astype(F32)

    back = lax.fori_loop(1, nb, wait_d, s_d[aligned(b, rows), :].astype(F32))
    stats = back[:, LANES:]
    log_0 = stats[:, 0:1] + stats[:, 1:2] + stats[:, 2:3]
    log_1 = stats[:, 3:4] + stats[:, 4:5] + stats[:, 5:6]
    cache_log = jnp.where(low, log_0, log_1)
    own_log = jnp.where(low, own_0, own_1)
    top = jnp.maximum(cache_log, own_log)
    cache_weight = jnp.exp(cache_log - top)
    own_weight = jnp.exp(own_log - top)
    attended = (cache_weight * back[:, :LANES] + own_weight * own_values) / (cache_weight + own_weight)
    attended = attended.astype(BF16)
    s_t[...] = attended
    g_t[:, aligned(core)] = attended
    pair_start(s_t, g_t.at[:, aligned(core)], 10)

    mine = {
        len(which): jnp.dot(attended, taken_columns(wso, aligned(core), which), preferred_element_type=F32)
        for which in (far, near) if which
    }
    pair_wait(s_t, g_t.at[:, aligned(other_core)], 10)
    theirs = g_t[:, aligned(other_core)]
    scatter_products(
        lambda which: mine[len(which)]
        + jnp.dot(theirs, taken_columns(wso, aligned(other_core), which), preferred_element_type=F32),
        s_e, r_e, e_send, e_recv,
    )
    swap_wait(5, 6, 7)

    def turn(g, carry):
        vt_mem[aligned(g, 256), :] = values[:, aligned(g, 256)].T
        return carry

    lax.fori_loop(0, groups, turn, 0)
    mixed = scatter_sum(s_e, r_e, e_send, e_recv)
    middle_16 = (first.astype(F32) + mixed).astype(BF16)
    middle = middle_16.astype(F32)

    s_m[...] = middle_16
    g_m[:, aligned(core)] = middle_16
    pair_start(s_m, g_m.at[:, aligned(core)], 11)
    pair_wait(s_x, g_x.at[:, aligned(other_core)], 8)
    pair_wait(s_m, g_m.at[:, aligned(other_core)], 11)
    both_middle = g_m[...].astype(F32)
    cross_scaled = (both_middle * g_x[0:1, :]).astype(BF16)
    scatter_products(
        lambda which: jnp.dot(cross_scaled, taken_columns(wcq, slice(None), which), preferred_element_type=F32),
        s_f, r_f, f_send, f_recv,
    )
    squares = jnp.broadcast_to(jnp.sum(both_middle * both_middle, axis=1, keepdims=True), (rows, LANES))
    squares = jnp.concatenate([squares] * (LANES // rows), axis=0).T[0:1, :]
    row8 = lax.broadcasted_iota(jnp.int32, (8, LANES), 0)
    square_rows = place(row8, split3(squares)).astype(BF16)
    s_n[...] = square_rows
    g_n[slot(0)] = square_rows
    gather_start(s_n, g_n, n_send, n_recv)
    raw = scatter_sum(s_f, r_f, f_send, f_recv).astype(BF16)

    s_q[...] = raw
    g_q[slot(0)] = raw
    gather_start(s_q, g_q, q_send, q_recv)
    gather_wait(s_n, g_n, n_send, n_recv, far + near)
    sums = jnp.zeros((8, LANES), F32)
    for at in range(half):
        sums = sums + g_n[at].astype(F32)
    mean = (sums[0:1, :] + sums[1:2, :] + sums[2:3, :]) * (1.0 / d_model)
    factor = lax.rsqrt(mean + EPS) * score_scale

    own_block = (
        lax.div(lax.broadcasted_iota(jnp.int32, (LANES, 256), 0), rows)
        == lax.div(lax.broadcasted_iota(jnp.int32, (LANES, 256), 1), 64)
    )
    lane_head = lax.div(lax.broadcasted_iota(jnp.int32, (64, LANES), 1), rows)
    left = lax.broadcasted_iota(jnp.int32, (32, LANES), 1) < 64

    def deliver(target):
        remote(s_g.at[target], r_g.at[chip], g_send.at[target], g_recv.at[chip], (b, 2 * target + core)).start()

    def slot_of(other):
        return lax.rem(other - chip + half + 2, half)

    def arrived(other):
        at = slot_of(other)
        remote(s_q, g_q.at[at], q_send.at[1], q_recv.at[at], (b, partner)).wait_recv()

    def remember(g):
        query = jnp.concatenate([g_q[slot_of(2 * g)], g_q[slot_of(2 * g + 1)]], axis=1).astype(F32)
        query = jnp.where(own_block, jnp.concatenate([query] * 4, axis=0), 0.0).astype(BF16)
        score = lax.dot_general(keys[:, aligned(g, 256)], query, NT, preferred_element_type=F32) * factor
        most = jnp.max(score, axis=0, keepdims=True)
        weight = jnp.exp(score - most).astype(BF16)
        total = jnp.sum(weight.astype(F32), axis=0, keepdims=True)
        spread = jnp.dot(vt_mem[aligned(g, 256), :], weight, preferred_element_type=F32)
        taken = jnp.where(lane_head == 0, spread[0:64], 0.0)
        for head in range(1, 4):
            taken = jnp.where(lane_head == head, spread[head * 64 : head * 64 + 64], taken)
        stat = place(row8, split3(most) + split3(total))
        turned = pltpu.roll(taken, 64, 1)
        turned_stat = pltpu.roll(stat, 64, 1)
        s_g[2 * g, pl.ds(0, 32), :] = jnp.where(left, taken[0:32], turned[32:64]).astype(BF16)
        s_g[2 * g, pl.ds(32, 8), :] = jnp.where(left[0:8], stat, turned_stat).astype(BF16)
        s_g[2 * g + 1, pl.ds(0, 32), :] = jnp.where(left, turned[0:32], taken[32:64]).astype(BF16)
        s_g[2 * g + 1, pl.ds(32, 8), :] = jnp.where(left[0:8], turned_stat, stat).astype(BF16)

    own_group = lax.div(chip, 2)
    other_chip = chip + 1 - 2 * lax.rem(chip, 2)
    offsets = sorted(range(groups), key=lambda k: (min(k % 4, 4 - k % 4), k))
    waiting = []
    for first_at in range(0, groups, AT_ONCE):
        now = [(offset, lax.rem(own_group + offset, groups)) for offset in offsets[first_at : first_at + AT_ONCE]]
        for offset, g in now:
            for other in [2 * g, 2 * g + 1] if offset else [other_chip]:
                arrived(other)
        for target in waiting:
            deliver(target)
        for offset, g in now:
            remember(g)
        waiting = []
        for offset, g in now:
            waiting += [2 * g, 2 * g + 1] if offset else [other_chip]
    for target in waiting:
        deliver(target)
    r_g[chip] = s_g[chip]

    def drain_g():
        for k in steps:
            target = chip_at(k)
            remote(s_g.at[target], r_g.at[chip], g_send.at[target], g_recv.at[chip], peer(k)).wait_send()

    drains.append(drain_g)
    for k in steps:
        source = chip_at(half - k)
        remote(s_g.at[chip], r_g.at[source], g_send.at[chip], g_recv.at[source], peer(half - k)).wait_recv()
    stats = [r_g[source, pl.ds(32, 8), :].astype(F32) for source in range(half)]
    mosts = [stat[0:1] + stat[1:2] + stat[2:3] for stat in stats]
    top = functools.reduce(jnp.maximum, mosts)
    over = jnp.zeros((32, LANES), F32)
    under = jnp.zeros((1, LANES), F32)
    for source in range(half):
        share = jnp.exp(mosts[source] - top)
        stat = stats[source]
        under = under + share * (stat[3:4] + stat[4:5] + stat[5:6])
        over = over + share * r_g[source, pl.ds(0, 32), :].astype(F32)
    turned = (over / under).T
    crossed = jnp.concatenate([turned[rows * at : rows * at + rows] for at in (0, 2, 1, 3)], axis=1).astype(BF16)

    s_h[...] = crossed
    g_h[slot(0)] = crossed
    gather_start(s_h, g_h, h_send, h_recv)

    def products(which, who):
        block = jnp.concatenate([g_h[at] for at in which], axis=1)
        weight = jnp.concatenate([wco[pl.ds(at * LANES, LANES), aligned(who)] for at in which], axis=0)
        return jnp.dot(block, weight, preferred_element_type=F32)

    gather_wait(s_h, g_h, h_send, h_recv, near)
    theirs, mine = products(near, other_core), middle + products(near, core)
    gather_wait(s_h, g_h, h_send, h_recv, far)
    if far:
        theirs = theirs + products(far, other_core)
    s_o[...] = theirs
    pair_start(s_o, r_o, 12)
    if far:
        mine = mine + products(far, core)
    pair_wait(s_o, r_o, 12)
    out_ref[...] = (mine + r_o[...]).astype(BF16)

    for drain in drains:
        drain()


def body(
    nb, nc, hidden_in, self_gain, w_self, w_self_out, cross_gain, w_cross_q, w_cross_out, cache_kv, memory_kv, parents, prefix_len
):
    rows = hidden_in.shape[0]
    d_model = w_self.shape[0]
    hyps = nb * rows
    cache_rows = cache_kv.shape[0] * cache_kv.shape[1] * cache_kv.shape[2]
    mem_count, mem_width = memory_kv.shape
    width = cache_rows // rows
    hbm = pl.BlockSpec(memory_space=pl.ANY)
    wide = nc * LANES
    chips = nc // 2

    def v(*shape):
        return pltpu.VMEM(shape, BF16)

    def f(*shape):
        return pltpu.VMEM(shape, F32)

    def sems(count):
        return pltpu.SemaphoreType.DMA((count,))

    return pl.pallas_call(
        functools.partial(kernel, nb, nc, d_model),
        out_shape=pltpu.VMEM((rows, LANES), BF16),
        in_specs=[hbm] * 11,
        out_specs=pl.BlockSpec(memory_space=pltpu.VMEM),
        scratch_shapes=[
            v(1, LANES), v(1, LANES), pltpu.VMEM((1, hyps), jnp.int32), pltpu.VMEM((1, hyps), jnp.int32),
            v(d_model // 2, 6 * LANES), v(2 * LANES, wide // 2), v(2 * LANES, wide // 2), v(wide // 2, 2 * LANES),
            v(cache_rows, LANES), v(2 * mem_count, wide // 2), v(2 * mem_count, wide // 2), v(wide // 2, 2 * mem_count),
            v(width, rows * LANES), v(width, rows * LANES), v(hyps, rows * LANES), pltpu.VMEM((hyps, LANES), F32),
            v(rows + 8, LANES), v(chips, rows + 8, LANES), pltpu.VMEM((8, LANES), F32), pltpu.VMEM((8, 2 * LANES), F32),
            v(rows, LANES), v(hyps, LANES),
            v(hyps, 2 * LANES), v(nb, rows, 2 * LANES),
            v(rows, LANES), v(rows, 2 * LANES),
            v(chips, rows, LANES), v(chips, rows, LANES),
            v(rows, LANES), v(rows, 2 * LANES),
            v(chips, rows, LANES), v(chips, rows, LANES),
            v(rows, LANES), v(chips, rows, LANES),
            v(chips, 40, LANES), v(chips, 40, LANES),
            v(rows, LANES), v(chips, rows, LANES),
            f(rows, 4 * LANES), f(rows, 4 * LANES), f(rows, LANES), f(rows, LANES), v(8, LANES), v(chips, 8, LANES),
            sems(15), sems(13), sems(13),
            sems(chips), sems(chips), sems(nb), sems(nb), sems(nb), sems(nb), sems(chips), sems(chips),
            sems(chips), sems(chips), sems(chips), sems(chips), sems(chips), sems(chips), sems(chips), sems(chips), sems(chips), sems(chips),
        ],
        compiler_params=pltpu.CompilerParams(
            collective_id=0, has_side_effects=True, vmem_limit_bytes=VMEM_BYTES
        ),
    )(
        hidden_in,
        self_gain.reshape(1, LANES),
        cross_gain.reshape(1, LANES),
        parents.reshape(1, hyps),
        prefix_len.reshape(1, hyps),
        jnp.transpose(w_self, (1, 0, 2)),
        w_self_out,
        w_cross_q,
        w_cross_out,
        cache_kv.reshape(cache_rows, LANES),
        memory_kv,
    )


def solution(mesh):
    return jax.shard_map(
        functools.partial(body, mesh.shape["beam"], mesh.shape["blk"]),
        mesh=mesh,
        in_specs=(
            P("beam", "blk"),
            P("blk"),
            P(None, None, "blk"),
            P("blk", None),
            P("blk"),
            P("blk", None),
            P(None, "blk"),
            P("beam", None, "blk", None),
            P("blk", None),
            P(),
            P(),
        ),
        out_specs=P("beam", "blk"),
        check_vma=False,
    )
```

```python
import functools

import jax
import jax.numpy as jnp
from jax import lax
from jax.experimental import pallas as pl
from jax.experimental.pallas import tpu as pltpu
from jax.sharding import PartitionSpec as P

MESH = pl.DeviceIdType.MESH
F32 = jnp.float32
BF16 = jnp.bfloat16
NEG = -1e30
EPS = 1e-06
LANES = 128
VMEM_BYTES = 64000000
AT_ONCE = 4


def aligned(block, size=LANES):
    return pl.ds(pl.multiple_of(block * size, size), size)


def split3(x):
    high = x.astype(BF16).astype(F32)
    rest = x - high
    middle = rest.astype(BF16).astype(F32)
    return high, middle, rest - middle


def place(index, pieces):
    out = jnp.zeros(index.shape, F32)
    for at, piece in enumerate(pieces):
        out = jnp.where(index == at, piece, out)
    return out


NT = (((1,), (1,)), ((), ()))


def kernel(
    nb, nc, d_model,
    hid_hbm, sgain_hbm, cgain_hbm, parents_hbm, plen_hbm,
    wself_hbm, wso_hbm, wcq_hbm, wco_hbm, cache_hbm, mem_hbm,
    out_ref,
    sgain, cgain, parents, plen,
    wself, wso, wcq, wco, cache, keys, values, vt_mem, kt, vt, lhs_q, acc,
    s_a, g_a, s_x, g_x, s_c, g_c, s_d, r_d, s_t, g_t, s_e, r_e, s_m, g_m, s_f, r_f, s_q, g_q, s_g, r_g, s_h, g_h, s_p, r_p, s_o, r_o,
    load_sem, swap_send, swap_recv,
    a_send, a_recv, c_send, c_recv, d_send, d_recv, e_send, e_recv,
    f_send, f_recv, q_send, q_recv, g_send, g_recv, h_send, h_recv,
):
    rows = hid_hbm.shape[0]
    hyps = nb * rows
    half = nc // 2
    groups = half // 2
    score_scale = 64 ** (-0.5)
    head_width = mem_hbm.shape[1] // 2
    mem_rows = mem_hbm.shape[0]
    b = lax.axis_index("beam")
    c = lax.axis_index("blk")
    chip = lax.div(c, 2)
    core = lax.rem(c, 2)
    partner = c + 1 - 2 * core
    other_core = 1 - core
    def hops(k):
        return min(k % 8, 8 - k % 8)

    def slot(k):
        return (k + 2) % half

    steps = sorted(range(1, half), key=lambda k: -hops(k))
    beam_steps = sorted(range(1, nb), key=lambda k: -min(k % 4, 4 - k % 4))
    far = sorted(slot(k) for k in range(half) if hops(k) >= 3)
    near = [at for at in range(half) if at not in far]

    barrier = pltpu.get_barrier_semaphore()

    def greet_blk(k, carry):
        pl.semaphore_signal(barrier, inc=1, device_id=(b, lax.rem(c + 2 * k, nc)), device_id_type=MESH)
        return carry

    def greet_beam(k, carry):
        pl.semaphore_signal(barrier, inc=1, device_id=(lax.rem(b + k, nb), c), device_id_type=MESH)
        return carry

    for k in steps:
        greet_blk(k, 0)
    lax.fori_loop(1, nb, greet_beam, 0)
    pl.semaphore_signal(barrier, inc=1, device_id=(b, partner), device_id_type=MESH)

    loads = [
        pltpu.make_async_copy(hid_hbm, s_a.at[pl.ds(0, rows), :], load_sem.at[0]),
        pltpu.make_async_copy(sgain_hbm, sgain, load_sem.at[1]),
        pltpu.make_async_copy(cgain_hbm, cgain, load_sem.at[2]),
        pltpu.make_async_copy(parents_hbm, parents, load_sem.at[3]),
        pltpu.make_async_copy(plen_hbm, plen, load_sem.at[4]),
        pltpu.make_async_copy(cache_hbm, cache, load_sem.at[5]),
    ]
    for load in loads:
        load.start()
    loaded = set()
    drains = []
    swap_done = set()
    swap_begun = set()
    pair_open = []

    def ready(*which):
        for at in which:
            loads[at].wait()
            loaded.add(at)

    def columns(source, target, offset=0, absolute=False):
        height = source.shape[0]
        return (
            lambda g, side: source.at[:, aligned(offset + 2 * g + side)],
            lambda k, g, who: target.at[aligned(who, height), aligned(g if absolute else k)],
            lambda who: target.at[aligned(who, height), :],
        )

    def kind(which):
        return (
            lambda g, side: wself_hbm.at[which, aligned(2 * g + side), :],
            lambda k, g, who: wself.at[aligned(k), aligned(3 * who + which)],
            lambda who: wself.at[:, aligned(3 * who + which)],
        )

    out_rows = (
        lambda g, side: wco_hbm.at[aligned(2 * g + side), :],
        lambda k, g, who: wco.at[aligned(k), aligned(who)],
        lambda who: wco.at[:, aligned(who)],
    )
    shared = [
        kind(0), kind(1), kind(2), columns(wso_hbm, wso), columns(wcq_hbm, wcq),
        columns(mem_hbm, keys, 0, True), columns(mem_hbm, values, nc, True), out_rows,
    ]

    def keep(k, carry):
        g, at_slot = lax.rem(chip + k, half), lax.rem(k + 2, half)
        for at, (block, place_at, whole) in enumerate(shared):
            pltpu.make_async_copy(block(g, core), place_at(at_slot, g, core), load_sem.at[6 + at]).start()
        return carry


    def remote(src, dst, send, recv, where):
        return pltpu.make_async_remote_copy(
            src_ref=src, dst_ref=dst, send_sem=send, recv_sem=recv, device_id=where, device_id_type=MESH
        )

    def peer(k):
        return (b, lax.rem(c + 2 * k, nc))

    def chip_at(k):
        return lax.rem(chip + k, half)

    def swap_start(*which):
        def step(k, carry):
            g, at_slot = lax.rem(chip + k, half), lax.rem(k + 2, half)
            for at in which:
                block, place_at, whole = shared[at]
                remote(
                    block(g, other_core), place_at(at_slot, g, core), swap_send.at[at], swap_recv.at[at], (b, partner)
                ).start()
            return carry

        lax.fori_loop(0, half, step, 0)
        swap_begun.update(which)

        def drain():
            for at in which:
                mine = shared[at][2](core)
                remote(mine, mine, swap_send.at[at], swap_recv.at[at], (b, partner)).wait_send()

        drains.append(drain)

    def swap_wait(*which):
        for at in which:
            swap_done.add(at)
            mine, theirs = shared[at][2](core), shared[at][2](other_core)
            pltpu.make_async_copy(mine, mine, load_sem.at[6 + at]).wait()
            if at in swap_begun:
                remote(theirs, theirs, swap_send.at[at], swap_recv.at[at], (b, partner)).wait_recv()

    def pair(src, dst, at):
        return remote(src, dst, swap_send.at[at], swap_recv.at[at], (b, partner))

    def pair_start(src, dst, at):
        pair(src, dst, at).start()
        pair_open.append((src, dst, at))
        drains.append(lambda: pair(src, dst, at).wait_send())

    def pair_wait(src, dst, at):
        pair_open[:] = [p for p in pair_open if p[2] != at]
        pair(src, dst, at).wait_recv()

    def gather_start(src, dst, send, recv):
        for k in steps:
            remote(src, dst.at[slot(half - k)], send.at[k], recv.at[slot(half - k)], peer(k)).start()
        drains.append(functools.partial(simple_drain, src, send))

    def gather_wait(src, dst, send, recv, which):
        for k in reversed(steps):
            at = slot(half - k)
            if at in which:
                remote(src, dst.at[at], send.at[k], recv.at[at], (b, partner)).wait_recv()

    def scatter_send(src, dst, send, recv, which):
        for k in steps:
            if slot(k) in which:
                remote(
                    src.at[slot(k)], dst.at[slot(half - k)], send.at[k], recv.at[slot(half - k)], peer(k)
                ).start()

    def scatter_products(products, src, dst, send, recv):
        for which in (far, near):
            if which:
                terms = products(which)
                for at, which_slot in enumerate(which):
                    src[which_slot] = terms[:, at * LANES : at * LANES + LANES].astype(BF16)
                scatter_send(src, dst, send, recv, which)
        drains.append(functools.partial(simple_drain, src.at[0], send))

    def taken_columns(ref, rows_at, which):
        return jnp.concatenate([ref[rows_at, pl.ds(at * LANES, LANES)] for at in which], axis=1)

    def simple_drain(block, send):
        def step(k, carry):
            remote(block, block, send.at[k], send.at[k], (b, partner)).wait_send()
            return carry

        lax.fori_loop(1, half, step, 0)

    def scatter_sum(src, dst, send, recv):
        total = src[slot(0)].astype(F32)
        for k in reversed(steps):
            at = slot(half - k)
            remote(src.at[at], dst.at[at], send.at[k], recv.at[at], (b, partner)).wait_recv()
            total = total + dst[at].astype(F32)
        return total

    ready(0, 1, 2)
    first = s_a[pl.ds(0, rows), :]
    gain_rows = jnp.broadcast_to(sgain[...].astype(F32), (8, LANES)).astype(BF16)
    s_a[pl.ds(rows, 8), :] = gain_rows
    g_a[slot(0), pl.ds(0, rows), :] = first
    g_a[slot(0), pl.ds(rows, 8), :] = gain_rows
    cgain_rows = jnp.broadcast_to(cgain[...].astype(F32), (8, LANES))
    s_x[...] = cgain_rows
    g_x[:, aligned(core)] = cgain_rows
    pl.semaphore_wait(barrier, half + nb - 1)
    gather_start(s_a, g_a, a_send, a_recv)
    pair_start(s_x, g_x.at[:, aligned(core)], 8)
    lax.fori_loop(0, half, keep, 0)
    swap_start(0, 1, 2)

    ready(5)
    width = cache.shape[0] // rows

    def arrange(r, carry):
        x = cache[aligned(r, width), :].astype(F32)
        rolled = pltpu.roll(x, 64, 1)
        even = lax.rem(lax.broadcasted_iota(jnp.int32, x.shape, 0), 2) == 0
        low = lax.broadcasted_iota(jnp.int32, x.shape, 1) < 64
        kt[:, aligned(r)] = jnp.where(even, jnp.where(low, x, 0.0), jnp.where(low, 0.0, rolled)).astype(BF16)
        vt[:, aligned(r)] = jnp.where(even, jnp.where(low, rolled, 0.0), jnp.where(low, 0.0, x)).astype(BF16)
        return carry

    lax.fori_loop(0, rows, arrange, 0)
    ready(3, 4)
    local_wide = jnp.broadcast_to(parents[...], (LANES, hyps)).T - b * rows
    plen_wide = jnp.broadcast_to(plen[...], (LANES, hyps)).T
    swap_wait(0, 1, 2)

    def project(which):
        wide = jnp.concatenate([g_a[at, pl.ds(0, rows), :] for at in which], axis=1).astype(F32)
        gain = jnp.concatenate([g_a[at, pl.ds(rows, 8), :] for at in which], axis=1).astype(F32)[0:1, :]
        scaled = (wide * gain).astype(BF16)

        def columns_of(who):
            weight = jnp.concatenate([wself[pl.ds(at * LANES, LANES), aligned(who, 384)] for at in which], axis=0)
            return jnp.dot(scaled, weight, preferred_element_type=F32)

        return jnp.sum(wide * wide, axis=1, keepdims=True), columns_of

    gather_wait(s_a, g_a, a_send, a_recv, near)
    squares, columns_of = project(near)
    theirs, mine = columns_of(other_core), columns_of(core)
    gather_wait(s_a, g_a, a_send, a_recv, far)
    if far:
        far_squares, columns_of = project(far)
        squares = squares + far_squares
        theirs = theirs + columns_of(other_core)
    squares = jnp.broadcast_to(squares, (rows, LANES))
    s_p[:, pl.ds(0, 384)] = theirs
    s_p[:, pl.ds(384, LANES)] = squares
    pair_start(s_p, r_p, 9)
    if far:
        mine = mine + columns_of(core)
    pair_wait(s_p, r_p, 9)
    joined = mine + r_p[:, pl.ds(0, 384)]
    self_scale = lax.rsqrt((squares + r_p[:, pl.ds(384, LANES)]) * (1.0 / d_model) + EPS)
    queries = (joined[:, :LANES] * self_scale).astype(BF16)

    s_c[...] = queries
    g_c[aligned(b, rows), :] = queries
    my_queries = g_c.at[aligned(b, rows), :]

    def send_c(k, carry):
        remote(s_c, my_queries, c_send.at[k], c_recv.at[b], (lax.rem(b + k, nb), c)).start()
        return carry

    for k in beam_steps:
        send_c(k, 0)

    def drain_c():
        def step(k, carry):
            remote(s_c, my_queries, c_send.at[k], c_recv.at[b], (b, partner)).wait_send()
            return carry

        lax.fori_loop(1, nb, step, 0)

    drains.append(drain_c)
    swap_start(3, 4, 5, 6, 7)
    own_values = (joined[:, 2 * LANES : 3 * LANES] * self_scale).astype(BF16).astype(F32)
    products = queries.astype(F32) * (joined[:, LANES : 2 * LANES] * self_scale).astype(BF16).astype(F32)
    low = lax.broadcasted_iota(jnp.int32, products.shape, 1) < 64
    own_0 = jnp.sum(jnp.where(low, products, 0.0), axis=1, keepdims=True) * score_scale
    own_1 = jnp.sum(jnp.where(low, 0.0, products), axis=1, keepdims=True) * score_scale

    def wait_c(k, carry):
        source = lax.rem(b + k, nb)
        remote(s_c, g_c.at[aligned(source, rows), :], c_send.at[k], c_recv.at[source], (source, c)).wait_recv()
        return carry

    lax.fori_loop(1, nb, wait_c, 0)

    all_queries = g_c[...]
    nothing = jnp.zeros(all_queries.shape, BF16)
    local_16 = local_wide.astype(F32).astype(BF16)
    for r in range(rows):
        lhs_q[:, pl.ds(r * LANES, LANES)] = jnp.where(local_16 == r, all_queries, nothing)
    scores = lax.dot_general(lhs_q[...], kt[...], NT, preferred_element_type=F32) * score_scale
    lane = lax.broadcasted_iota(jnp.int32, scores.shape, 1)
    even = lax.rem(lane, 2) == 0
    tiles = width // LANES
    visible = lax.div(lane, 2) < jnp.concatenate([plen_wide] * tiles, axis=1)
    masked = jnp.where(visible, scores, NEG)
    max_0 = jnp.max(jnp.where(even, masked, NEG), axis=1, keepdims=True)
    max_1 = jnp.max(jnp.where(even, NEG, masked), axis=1, keepdims=True)
    weights = jnp.where(visible, jnp.exp(masked - jnp.where(even, max_0, max_1)), 0.0).astype(BF16)
    lhs_q[:, pl.ds(0, width)] = weights
    weights = weights.astype(F32)
    total_0 = jnp.sum(jnp.where(even, weights, 0.0), axis=1, keepdims=True)
    total_1 = jnp.sum(jnp.where(even, 0.0, weights), axis=1, keepdims=True)
    weights = lhs_q[:, pl.ds(0, width)]
    acc[...] = jnp.zeros(acc.shape, F32)
    for r in range(0, rows, 2):
        both = jnp.dot(weights, vt[:, pl.ds(r * LANES, 2 * LANES)], preferred_element_type=F32)
        picked = jnp.where(local_wide == r, both[:, :LANES], acc[...])
        acc[...] = jnp.where(local_wide == r + 1, both[:, LANES:], picked)
    summed = acc[...]
    lane = lax.broadcasted_iota(jnp.int32, summed.shape, 1)
    here = (local_wide >= 0) & (local_wide < rows)
    part = summed / jnp.where(lane < 64, total_0, total_1)
    pieces = split3(max_0 + jnp.log(total_0)) + split3(max_1 + jnp.log(total_1))
    s_d[:, pl.ds(0, LANES)] = part.astype(BF16)
    s_d[:, pl.ds(LANES, LANES)] = jnp.where(here, place(lane, pieces), 0.0).astype(BF16)

    def send_d(k, carry):
        target = lax.rem(b + k, nb)
        remote(s_d.at[aligned(target, rows), :], r_d.at[b], d_send.at[k], d_recv.at[b], (target, c)).start()
        return carry

    for k in beam_steps:
        send_d(k, 0)

    def drain_d():
        def step(k, carry):
            remote(s_d.at[aligned(b, rows), :], r_d.at[b], d_send.at[k], d_recv.at[b], (b, partner)).wait_send()
            return carry

        lax.fori_loop(1, nb, step, 0)

    drains.append(drain_d)
    swap_wait(3, 4)

    def wait_d(k, total):
        source = lax.rem(b + k, nb)
        remote(s_d.at[aligned(b, rows), :], r_d.at[source], d_send.at[k], d_recv.at[source], (source, c)).wait_recv()
        return total + r_d[source].astype(F32)

    back = lax.fori_loop(1, nb, wait_d, s_d[aligned(b, rows), :].astype(F32))
    stats = back[:, LANES:]
    log_0 = stats[:, 0:1] + stats[:, 1:2] + stats[:, 2:3]
    log_1 = stats[:, 3:4] + stats[:, 4:5] + stats[:, 5:6]
    cache_log = jnp.where(low, log_0, log_1)
    own_log = jnp.where(low, own_0, own_1)
    top = jnp.maximum(cache_log, own_log)
    cache_weight = jnp.exp(cache_log - top)
    own_weight = jnp.exp(own_log - top)
    attended = (cache_weight * back[:, :LANES] + own_weight * own_values) / (cache_weight + own_weight)
    attended = attended.astype(BF16)
    s_t[...] = attended
    g_t[:, aligned(core)] = attended
    pair_start(s_t, g_t.at[:, aligned(core)], 10)

    mine = {
        len(which): jnp.dot(attended, taken_columns(wso, aligned(core), which), preferred_element_type=F32)
        for which in (far, near) if which
    }
    pair_wait(s_t, g_t.at[:, aligned(other_core)], 10)
    theirs = g_t[:, aligned(other_core)]
    scatter_products(
        lambda which: mine[len(which)]
        + jnp.dot(theirs, taken_columns(wso, aligned(other_core), which), preferred_element_type=F32),
        s_e, r_e, e_send, e_recv,
    )
    swap_wait(5, 6, 7)

    def turn(g, carry):
        vt_mem[aligned(g, 256), :] = values[:, aligned(g, 256)].T
        return carry

    lax.fori_loop(0, groups, turn, 0)
    mixed = scatter_sum(s_e, r_e, e_send, e_recv)
    middle_16 = (first.astype(F32) + mixed).astype(BF16)
    middle = middle_16.astype(F32)

    s_m[...] = middle_16
    g_m[:, aligned(core)] = middle_16
    pair_start(s_m, g_m.at[:, aligned(core)], 11)
    pair_wait(s_x, g_x.at[:, aligned(other_core)], 8)
    pair_wait(s_m, g_m.at[:, aligned(other_core)], 11)
    both_middle = g_m[...].astype(F32)
    cross_scaled = (both_middle * g_x[0:1, :]).astype(BF16)
    scatter_products(
        lambda which: jnp.dot(cross_scaled, taken_columns(wcq, slice(None), which), preferred_element_type=F32),
        s_f, r_f, f_send, f_recv,
    )
    squares = jnp.broadcast_to(jnp.sum(both_middle * both_middle, axis=1, keepdims=True), (rows, LANES))
    squares = jnp.concatenate([squares] * (LANES // rows), axis=0).T[0:1, :]
    row8 = lax.broadcasted_iota(jnp.int32, (8, LANES), 0)
    square_rows = place(row8, split3(squares)).astype(BF16)
    s_q[pl.ds(rows, 8), :] = square_rows
    g_q[slot(0), pl.ds(rows, 8), :] = square_rows
    raw = scatter_sum(s_f, r_f, f_send, f_recv).astype(BF16)
    s_q[pl.ds(0, rows), :] = raw
    g_q[slot(0), pl.ds(0, rows), :] = raw

    gather_start(s_q, g_q, q_send, q_recv)
    gather_wait(s_q, g_q, q_send, q_recv, far + near)
    sums = jnp.zeros((8, LANES), F32)
    for k in range(half):
        sums = sums + g_q[k, pl.ds(rows, 8), :].astype(F32)
    mean = (sums[0:1, :] + sums[1:2, :] + sums[2:3, :]) * (1.0 / d_model)
    factor = lax.rsqrt(mean + EPS) * score_scale

    own_block = (
        lax.div(lax.broadcasted_iota(jnp.int32, (LANES, 256), 0), rows)
        == lax.div(lax.broadcasted_iota(jnp.int32, (LANES, 256), 1), 64)
    )
    lane_head = lax.div(lax.broadcasted_iota(jnp.int32, (64, LANES), 1), rows)
    left = lax.broadcasted_iota(jnp.int32, (32, LANES), 1) < 64

    def deliver(target):
        remote(s_g.at[target], r_g.at[chip], g_send.at[target], g_recv.at[chip], (b, 2 * target + core)).start()

    def remember(g):
        query = jnp.concatenate(
            [g_q[lax.rem(2 * g + which - chip + half + 2, half), pl.ds(0, rows), :] for which in range(2)], axis=1
        ).astype(F32)
        query = jnp.where(own_block, jnp.concatenate([query] * 4, axis=0), 0.0).astype(BF16)
        score = lax.dot_general(keys[:, aligned(g, 256)], query, NT, preferred_element_type=F32) * factor
        most = jnp.max(score, axis=0, keepdims=True)
        weight = jnp.exp(score - most).astype(BF16)
        total = jnp.sum(weight.astype(F32), axis=0, keepdims=True)
        spread = jnp.dot(vt_mem[aligned(g, 256), :], weight, preferred_element_type=F32)
        taken = jnp.where(lane_head == 0, spread[0:64], 0.0)
        for head in range(1, 4):
            taken = jnp.where(lane_head == head, spread[head * 64 : head * 64 + 64], taken)
        stat = place(row8, split3(most) + split3(total))
        turned = pltpu.roll(taken, 64, 1)
        turned_stat = pltpu.roll(stat, 64, 1)
        s_g[2 * g, pl.ds(0, 32), :] = jnp.where(left, taken[0:32], turned[32:64]).astype(BF16)
        s_g[2 * g, pl.ds(32, 8), :] = jnp.where(left[0:8], stat, turned_stat).astype(BF16)
        s_g[2 * g + 1, pl.ds(0, 32), :] = jnp.where(left, turned[0:32], taken[32:64]).astype(BF16)
        s_g[2 * g + 1, pl.ds(32, 8), :] = jnp.where(left[0:8], turned_stat, stat).astype(BF16)

    own_group = lax.div(chip, 2)
    offsets = sorted(range(groups), key=lambda k: -min(k % 4, 4 - k % 4) if k else 1)
    for first_at in range(0, groups, AT_ONCE):
        now = [(offset, lax.rem(own_group + offset, groups)) for offset in offsets[first_at : first_at + AT_ONCE]]
        for offset, g in now:
            remember(g)
        for offset, g in now:
            for target in [2 * g, 2 * g + 1] if offset else [chip + 1 - 2 * lax.rem(chip, 2)]:
                deliver(target)
    r_g[chip] = s_g[chip]

    def drain_g():
        for k in steps:
            target = chip_at(k)
            remote(s_g.at[target], r_g.at[chip], g_send.at[target], g_recv.at[chip], peer(k)).wait_send()

    drains.append(drain_g)
    for k in steps:
        source = chip_at(half - k)
        remote(s_g.at[chip], r_g.at[source], g_send.at[chip], g_recv.at[source], peer(half - k)).wait_recv()
    stats = [r_g[source, pl.ds(32, 8), :].astype(F32) for source in range(half)]
    mosts = [stat[0:1] + stat[1:2] + stat[2:3] for stat in stats]
    top = functools.reduce(jnp.maximum, mosts)
    over = jnp.zeros((32, LANES), F32)
    under = jnp.zeros((1, LANES), F32)
    for source in range(half):
        share = jnp.exp(mosts[source] - top)
        stat = stats[source]
        under = under + share * (stat[3:4] + stat[4:5] + stat[5:6])
        over = over + share * r_g[source, pl.ds(0, 32), :].astype(F32)
    turned = (over / under).T
    crossed = jnp.concatenate([turned[rows * at : rows * at + rows] for at in (0, 2, 1, 3)], axis=1).astype(BF16)

    s_h[...] = crossed
    g_h[slot(0)] = crossed
    earlier = list(drains)
    drains.clear()
    gather_start(s_h, g_h, h_send, h_recv)
    for drain in earlier:
        drain()

    def products(which, who):
        block = jnp.concatenate([g_h[at] for at in which], axis=1)
        weight = jnp.concatenate([wco[pl.ds(at * LANES, LANES), aligned(who)] for at in which], axis=0)
        return jnp.dot(block, weight, preferred_element_type=F32)

    gather_wait(s_h, g_h, h_send, h_recv, near)
    theirs, mine = products(near, other_core), middle + products(near, core)
    gather_wait(s_h, g_h, h_send, h_recv, far)
    if far:
        theirs = theirs + products(far, other_core)
    s_o[...] = theirs
    pair_start(s_o, r_o, 12)
    if far:
        mine = mine + products(far, core)
    pair_wait(s_o, r_o, 12)
    out_ref[...] = (mine + r_o[...]).astype(BF16)

    for drain in drains:
        drain()


def body(
    nb, nc, hidden_in, self_gain, w_self, w_self_out, cross_gain, w_cross_q, w_cross_out, cache_kv, memory_kv, parents, prefix_len
):
    rows = hidden_in.shape[0]
    d_model = w_self.shape[0]
    hyps = nb * rows
    cache_rows = cache_kv.shape[0] * cache_kv.shape[1] * cache_kv.shape[2]
    mem_count, mem_width = memory_kv.shape
    width = cache_rows // rows
    hbm = pl.BlockSpec(memory_space=pl.ANY)
    wide = nc * LANES
    chips = nc // 2

    def v(*shape):
        return pltpu.VMEM(shape, BF16)

    def f(*shape):
        return pltpu.VMEM(shape, F32)

    def sems(count):
        return pltpu.SemaphoreType.DMA((count,))

    return pl.pallas_call(
        functools.partial(kernel, nb, nc, d_model),
        out_shape=pltpu.VMEM((rows, LANES), BF16),
        in_specs=[hbm] * 11,
        out_specs=pl.BlockSpec(memory_space=pltpu.VMEM),
        scratch_shapes=[
            v(1, LANES), v(1, LANES), pltpu.VMEM((1, hyps), jnp.int32), pltpu.VMEM((1, hyps), jnp.int32),
            v(d_model // 2, 6 * LANES), v(2 * LANES, wide // 2), v(2 * LANES, wide // 2), v(wide // 2, 2 * LANES),
            v(cache_rows, LANES), v(2 * mem_count, wide // 2), v(2 * mem_count, wide // 2), v(wide // 2, 2 * mem_count),
            v(width, rows * LANES), v(width, rows * LANES), v(hyps, rows * LANES), pltpu.VMEM((hyps, LANES), F32),
            v(rows + 8, LANES), v(chips, rows + 8, LANES), pltpu.VMEM((8, LANES), F32), pltpu.VMEM((8, 2 * LANES), F32),
            v(rows, LANES), v(hyps, LANES),
            v(hyps, 2 * LANES), v(nb, rows, 2 * LANES),
            v(rows, LANES), v(rows, 2 * LANES),
            v(chips, rows, LANES), v(chips, rows, LANES),
            v(rows, LANES), v(rows, 2 * LANES),
            v(chips, rows, LANES), v(chips, rows, LANES),
            v(rows + 8, LANES), v(chips, rows + 8, LANES),
            v(chips, 40, LANES), v(chips, 40, LANES),
            v(rows, LANES), v(chips, rows, LANES),
            f(rows, 4 * LANES), f(rows, 4 * LANES), f(rows, LANES), f(rows, LANES),
            sems(15), sems(13), sems(13),
            sems(chips), sems(chips), sems(nb), sems(nb), sems(nb), sems(nb), sems(chips), sems(chips),
            sems(chips), sems(chips), sems(chips), sems(chips), sems(chips), sems(chips), sems(chips), sems(chips),
        ],
        compiler_params=pltpu.CompilerParams(
            collective_id=0, has_side_effects=True, vmem_limit_bytes=VMEM_BYTES
        ),
    )(
        hidden_in,
        self_gain.reshape(1, LANES),
        cross_gain.reshape(1, LANES),
        parents.reshape(1, hyps),
        prefix_len.reshape(1, hyps),
        jnp.transpose(w_self, (1, 0, 2)),
        w_self_out,
        w_cross_q,
        w_cross_out,
        cache_kv.reshape(cache_rows, LANES),
        memory_kv,
    )


def solution(mesh):
    return jax.shard_map(
        functools.partial(body, mesh.shape["beam"], mesh.shape["blk"]),
        mesh=mesh,
        in_specs=(
            P("beam", "blk"),
            P("blk"),
            P(None, None, "blk"),
            P("blk", None),
            P("blk"),
            P("blk", None),
            P(None, "blk"),
            P("beam", None, "blk", None),
            P("blk", None),
            P(),
            P(),
        ),
        out_specs=P("beam", "blk"),
        check_vma=False,
    )
```

```python
import functools

import jax
import jax.numpy as jnp
from jax import lax
from jax.experimental import pallas as pl
from jax.experimental.pallas import tpu as pltpu
from jax.sharding import PartitionSpec as P

MESH = pl.DeviceIdType.MESH
F32 = jnp.float32
BF16 = jnp.bfloat16
NEG = -1e30
EPS = 1e-06
LANES = 128
VMEM_BYTES = 64000000
AT_ONCE = 4


def aligned(block, size=LANES):
    return pl.ds(pl.multiple_of(block * size, size), size)


def split3(x):
    high = x.astype(BF16).astype(F32)
    rest = x - high
    middle = rest.astype(BF16).astype(F32)
    return high, middle, rest - middle


def place(index, pieces):
    out = jnp.zeros(index.shape, F32)
    for at, piece in enumerate(pieces):
        out = jnp.where(index == at, piece, out)
    return out


NT = (((1,), (1,)), ((), ()))


def kernel(
    nb, nc, d_model,
    hid_hbm, sgain_hbm, cgain_hbm, parents_hbm, plen_hbm,
    wself_hbm, wso_hbm, wcq_hbm, wco_hbm, cache_hbm, mem_hbm,
    out_ref,
    sgain, cgain, parents, plen,
    wself, wso, wcq, wco, cache, keys, values, vt_mem, kt, vt, lhs_q, acc,
    s_a, g_a, s_x, g_x, s_c, g_c, s_d, r_d, s_t, g_t, s_e, r_e, s_m, g_m, s_f, r_f, s_q, g_q, s_g, r_g, s_h, g_h, s_p, r_p, s_o, r_o,
    load_sem, swap_send, swap_recv,
    a_send, a_recv, c_send, c_recv, d_send, d_recv, e_send, e_recv,
    f_send, f_recv, q_send, q_recv, g_send, g_recv, h_send, h_recv,
):
    rows = hid_hbm.shape[0]
    hyps = nb * rows
    half = nc // 2
    groups = half // 2
    score_scale = 64 ** (-0.5)
    head_width = mem_hbm.shape[1] // 2
    mem_rows = mem_hbm.shape[0]
    b = lax.axis_index("beam")
    c = lax.axis_index("blk")
    chip = lax.div(c, 2)
    core = lax.rem(c, 2)
    partner = c + 1 - 2 * core
    other_core = 1 - core
    def hops(k):
        return min(k % 8, 8 - k % 8)

    def slot(k):
        return (k + 2) % half

    steps = sorted(range(1, half), key=lambda k: -hops(k))
    beam_steps = sorted(range(1, nb), key=lambda k: -min(k % 4, 4 - k % 4))
    far = sorted(slot(k) for k in range(half) if hops(k) >= 3)
    near = [at for at in range(half) if at not in far]

    barrier = pltpu.get_barrier_semaphore()

    def greet_blk(k, carry):
        pl.semaphore_signal(barrier, inc=1, device_id=(b, lax.rem(c + 2 * k, nc)), device_id_type=MESH)
        return carry

    def greet_beam(k, carry):
        pl.semaphore_signal(barrier, inc=1, device_id=(lax.rem(b + k, nb), c), device_id_type=MESH)
        return carry

    for k in steps[: half // 2]:
        greet_blk(k, 0)
    for k in beam_steps:
        greet_beam(k, 0)
    for k in steps[half // 2 :]:
        greet_blk(k, 0)
    pl.semaphore_signal(barrier, inc=1, device_id=(b, partner), device_id_type=MESH)

    loads = [
        pltpu.make_async_copy(hid_hbm, s_a.at[pl.ds(0, rows), :], load_sem.at[0]),
        pltpu.make_async_copy(sgain_hbm, sgain, load_sem.at[1]),
        pltpu.make_async_copy(cgain_hbm, cgain, load_sem.at[2]),
        pltpu.make_async_copy(parents_hbm, parents, load_sem.at[3]),
        pltpu.make_async_copy(plen_hbm, plen, load_sem.at[4]),
        pltpu.make_async_copy(cache_hbm, cache, load_sem.at[5]),
    ]
    for load in loads:
        load.start()
    loaded = set()
    drains = []
    swap_done = set()
    swap_begun = set()
    pair_open = []

    def ready(*which):
        for at in which:
            loads[at].wait()
            loaded.add(at)

    def columns(source, target, offset=0, absolute=False):
        height = source.shape[0]
        return (
            lambda g, side: source.at[:, aligned(offset + 2 * g + side)],
            lambda k, g, who: target.at[aligned(who, height), aligned(g if absolute else k)],
            lambda who: target.at[aligned(who, height), :],
        )

    def kind(which):
        return (
            lambda g, side: wself_hbm.at[which, aligned(2 * g + side), :],
            lambda k, g, who: wself.at[aligned(k), aligned(3 * who + which)],
            lambda who: wself.at[:, aligned(3 * who + which)],
        )

    out_rows = (
        lambda g, side: wco_hbm.at[aligned(2 * g + side), :],
        lambda k, g, who: wco.at[aligned(k), aligned(who)],
        lambda who: wco.at[:, aligned(who)],
    )
    shared = [
        kind(0), kind(1), kind(2), columns(wso_hbm, wso), columns(wcq_hbm, wcq),
        columns(mem_hbm, keys, 0, True), columns(mem_hbm, values, nc, True), out_rows,
    ]

    def keep(k, carry):
        g, at_slot = lax.rem(chip + k, half), lax.rem(k + 2, half)
        for at, (block, place_at, whole) in enumerate(shared):
            pltpu.make_async_copy(block(g, core), place_at(at_slot, g, core), load_sem.at[6 + at]).start()
        return carry


    def remote(src, dst, send, recv, where):
        return pltpu.make_async_remote_copy(
            src_ref=src, dst_ref=dst, send_sem=send, recv_sem=recv, device_id=where, device_id_type=MESH
        )

    def peer(k):
        return (b, lax.rem(c + 2 * k, nc))

    def chip_at(k):
        return lax.rem(chip + k, half)

    def swap_start(*which):
        def step(k, carry):
            g, at_slot = lax.rem(chip + k, half), lax.rem(k + 2, half)
            for at in which:
                block, place_at, whole = shared[at]
                remote(
                    block(g, other_core), place_at(at_slot, g, core), swap_send.at[at], swap_recv.at[at], (b, partner)
                ).start()
            return carry

        lax.fori_loop(0, half, step, 0)
        swap_begun.update(which)

        def drain():
            for at in which:
                mine = shared[at][2](core)
                remote(mine, mine, swap_send.at[at], swap_recv.at[at], (b, partner)).wait_send()

        drains.append(drain)

    def swap_wait(*which):
        for at in which:
            swap_done.add(at)
            mine, theirs = shared[at][2](core), shared[at][2](other_core)
            pltpu.make_async_copy(mine, mine, load_sem.at[6 + at]).wait()
            if at in swap_begun:
                remote(theirs, theirs, swap_send.at[at], swap_recv.at[at], (b, partner)).wait_recv()

    def pair(src, dst, at):
        return remote(src, dst, swap_send.at[at], swap_recv.at[at], (b, partner))

    def pair_start(src, dst, at):
        pair(src, dst, at).start()
        pair_open.append((src, dst, at))
        drains.append(lambda: pair(src, dst, at).wait_send())

    def pair_wait(src, dst, at):
        pair_open[:] = [p for p in pair_open if p[2] != at]
        pair(src, dst, at).wait_recv()

    def gather_start(src, dst, send, recv):
        for k in steps:
            remote(src, dst.at[slot(half - k)], send.at[k], recv.at[slot(half - k)], peer(k)).start()
        drains.append(functools.partial(simple_drain, src, send))

    def gather_wait(src, dst, send, recv, which):
        for k in reversed(steps):
            at = slot(half - k)
            if at in which:
                remote(src, dst.at[at], send.at[k], recv.at[at], (b, partner)).wait_recv()

    def scatter_send(src, dst, send, recv, which):
        for k in steps:
            if slot(k) in which:
                remote(
                    src.at[slot(k)], dst.at[slot(half - k)], send.at[k], recv.at[slot(half - k)], peer(k)
                ).start()

    def scatter_products(products, src, dst, send, recv):
        for which in (far, near):
            if which:
                terms = products(which)
                for at, which_slot in enumerate(which):
                    src[which_slot] = terms[:, at * LANES : at * LANES + LANES].astype(BF16)
                scatter_send(src, dst, send, recv, which)
        drains.append(functools.partial(simple_drain, src.at[0], send))

    def taken_columns(ref, rows_at, which):
        return jnp.concatenate([ref[rows_at, pl.ds(at * LANES, LANES)] for at in which], axis=1)

    def simple_drain(block, send):
        def step(k, carry):
            remote(block, block, send.at[k], send.at[k], (b, partner)).wait_send()
            return carry

        lax.fori_loop(1, half, step, 0)

    def scatter_sum(src, dst, send, recv):
        total = src[slot(0)].astype(F32)
        for k in reversed(steps):
            at = slot(half - k)
            remote(src.at[at], dst.at[at], send.at[k], recv.at[at], (b, partner)).wait_recv()
            total = total + dst[at].astype(F32)
        return total

    ready(0, 1, 2)
    first = s_a[pl.ds(0, rows), :]
    gain_rows = jnp.broadcast_to(sgain[...].astype(F32), (8, LANES)).astype(BF16)
    s_a[pl.ds(rows, 8), :] = gain_rows
    g_a[slot(0), pl.ds(0, rows), :] = first
    g_a[slot(0), pl.ds(rows, 8), :] = gain_rows
    cgain_rows = jnp.broadcast_to(cgain[...].astype(F32), (8, LANES))
    s_x[...] = cgain_rows
    g_x[:, aligned(core)] = cgain_rows
    pl.semaphore_wait(barrier, half + nb - 1)
    gather_start(s_a, g_a, a_send, a_recv)
    pair_start(s_x, g_x.at[:, aligned(core)], 8)
    lax.fori_loop(0, half, keep, 0)
    swap_start(0, 1, 2)

    ready(5)
    width = cache.shape[0] // rows

    def arrange(r, carry):
        x = cache[aligned(r, width), :].astype(F32)
        rolled = pltpu.roll(x, 64, 1)
        even = lax.rem(lax.broadcasted_iota(jnp.int32, x.shape, 0), 2) == 0
        low = lax.broadcasted_iota(jnp.int32, x.shape, 1) < 64
        kt[:, aligned(r)] = jnp.where(even, jnp.where(low, x, 0.0), jnp.where(low, 0.0, rolled)).astype(BF16)
        vt[:, aligned(r)] = jnp.where(even, jnp.where(low, rolled, 0.0), jnp.where(low, 0.0, x)).astype(BF16)
        return carry

    lax.fori_loop(0, rows, arrange, 0)
    ready(3, 4)
    local_wide = jnp.broadcast_to(parents[...], (LANES, hyps)).T - b * rows
    plen_wide = jnp.broadcast_to(plen[...], (LANES, hyps)).T
    swap_wait(0, 1, 2)

    def project(which):
        wide = jnp.concatenate([g_a[at, pl.ds(0, rows), :] for at in which], axis=1).astype(F32)
        gain = jnp.concatenate([g_a[at, pl.ds(rows, 8), :] for at in which], axis=1).astype(F32)[0:1, :]
        scaled = (wide * gain).astype(BF16)

        def columns_of(who):
            weight = jnp.concatenate([wself[pl.ds(at * LANES, LANES), aligned(who, 384)] for at in which], axis=0)
            return jnp.dot(scaled, weight, preferred_element_type=F32)

        return jnp.sum(wide * wide, axis=1, keepdims=True), columns_of

    gather_wait(s_a, g_a, a_send, a_recv, near)
    squares, columns_of = project(near)
    theirs, mine = columns_of(other_core), columns_of(core)
    gather_wait(s_a, g_a, a_send, a_recv, far)
    if far:
        far_squares, columns_of = project(far)
        squares = squares + far_squares
        theirs = theirs + columns_of(other_core)
    squares = jnp.broadcast_to(squares, (rows, LANES))
    s_p[:, pl.ds(0, 384)] = theirs
    s_p[:, pl.ds(384, LANES)] = squares
    pair_start(s_p, r_p, 9)
    if far:
        mine = mine + columns_of(core)
    pair_wait(s_p, r_p, 9)
    joined = mine + r_p[:, pl.ds(0, 384)]
    self_scale = lax.rsqrt((squares + r_p[:, pl.ds(384, LANES)]) * (1.0 / d_model) + EPS)
    queries = (joined[:, :LANES] * self_scale).astype(BF16)

    s_c[...] = queries
    g_c[aligned(b, rows), :] = queries
    my_queries = g_c.at[aligned(b, rows), :]

    def send_c(k, carry):
        remote(s_c, my_queries, c_send.at[k], c_recv.at[b], (lax.rem(b + k, nb), c)).start()
        return carry

    for k in beam_steps:
        send_c(k, 0)

    def drain_c():
        def step(k, carry):
            remote(s_c, my_queries, c_send.at[k], c_recv.at[b], (b, partner)).wait_send()
            return carry

        lax.fori_loop(1, nb, step, 0)

    drains.append(drain_c)
    swap_start(3, 4, 5, 6, 7)
    own_values = (joined[:, 2 * LANES : 3 * LANES] * self_scale).astype(BF16).astype(F32)
    products = queries.astype(F32) * (joined[:, LANES : 2 * LANES] * self_scale).astype(BF16).astype(F32)
    low = lax.broadcasted_iota(jnp.int32, products.shape, 1) < 64
    own_0 = jnp.sum(jnp.where(low, products, 0.0), axis=1, keepdims=True) * score_scale
    own_1 = jnp.sum(jnp.where(low, 0.0, products), axis=1, keepdims=True) * score_scale

    def wait_c(k, carry):
        source = lax.rem(b + k, nb)
        remote(s_c, g_c.at[aligned(source, rows), :], c_send.at[k], c_recv.at[source], (source, c)).wait_recv()
        return carry

    lax.fori_loop(1, nb, wait_c, 0)

    all_queries = g_c[...]
    nothing = jnp.zeros(all_queries.shape, BF16)
    local_16 = local_wide.astype(F32).astype(BF16)
    for r in range(rows):
        lhs_q[:, pl.ds(r * LANES, LANES)] = jnp.where(local_16 == r, all_queries, nothing)
    scores = lax.dot_general(lhs_q[...], kt[...], NT, preferred_element_type=F32) * score_scale
    lane = lax.broadcasted_iota(jnp.int32, scores.shape, 1)
    even = lax.rem(lane, 2) == 0
    tiles = width // LANES
    visible = lax.div(lane, 2) < jnp.concatenate([plen_wide] * tiles, axis=1)
    masked = jnp.where(visible, scores, NEG)
    max_0 = jnp.max(jnp.where(even, masked, NEG), axis=1, keepdims=True)
    max_1 = jnp.max(jnp.where(even, NEG, masked), axis=1, keepdims=True)
    weights = jnp.where(visible, jnp.exp(masked - jnp.where(even, max_0, max_1)), 0.0).astype(BF16)
    lhs_q[:, pl.ds(0, width)] = weights
    weights = weights.astype(F32)
    total_0 = jnp.sum(jnp.where(even, weights, 0.0), axis=1, keepdims=True)
    total_1 = jnp.sum(jnp.where(even, 0.0, weights), axis=1, keepdims=True)
    weights = lhs_q[:, pl.ds(0, width)]
    acc[...] = jnp.zeros(acc.shape, F32)
    for r in range(0, rows, 2):
        both = jnp.dot(weights, vt[:, pl.ds(r * LANES, 2 * LANES)], preferred_element_type=F32)
        picked = jnp.where(local_wide == r, both[:, :LANES], acc[...])
        acc[...] = jnp.where(local_wide == r + 1, both[:, LANES:], picked)
    summed = acc[...]
    lane = lax.broadcasted_iota(jnp.int32, summed.shape, 1)
    here = (local_wide >= 0) & (local_wide < rows)
    part = summed / jnp.where(lane < 64, total_0, total_1)
    pieces = split3(max_0 + jnp.log(total_0)) + split3(max_1 + jnp.log(total_1))
    s_d[:, pl.ds(0, LANES)] = part.astype(BF16)
    s_d[:, pl.ds(LANES, LANES)] = jnp.where(here, place(lane, pieces), 0.0).astype(BF16)

    def send_d(k, carry):
        target = lax.rem(b + k, nb)
        remote(s_d.at[aligned(target, rows), :], r_d.at[b], d_send.at[k], d_recv.at[b], (target, c)).start()
        return carry

    for k in beam_steps:
        send_d(k, 0)

    def drain_d():
        def step(k, carry):
            remote(s_d.at[aligned(b, rows), :], r_d.at[b], d_send.at[k], d_recv.at[b], (b, partner)).wait_send()
            return carry

        lax.fori_loop(1, nb, step, 0)

    drains.append(drain_d)
    swap_wait(3, 4)

    def wait_d(k, total):
        source = lax.rem(b + k, nb)
        remote(s_d.at[aligned(b, rows), :], r_d.at[source], d_send.at[k], d_recv.at[source], (source, c)).wait_recv()
        return total + r_d[source].astype(F32)

    back = lax.fori_loop(1, nb, wait_d, s_d[aligned(b, rows), :].astype(F32))
    stats = back[:, LANES:]
    log_0 = stats[:, 0:1] + stats[:, 1:2] + stats[:, 2:3]
    log_1 = stats[:, 3:4] + stats[:, 4:5] + stats[:, 5:6]
    cache_log = jnp.where(low, log_0, log_1)
    own_log = jnp.where(low, own_0, own_1)
    top = jnp.maximum(cache_log, own_log)
    cache_weight = jnp.exp(cache_log - top)
    own_weight = jnp.exp(own_log - top)
    attended = (cache_weight * back[:, :LANES] + own_weight * own_values) / (cache_weight + own_weight)
    attended = attended.astype(BF16)
    s_t[...] = attended
    g_t[:, aligned(core)] = attended
    pair_start(s_t, g_t.at[:, aligned(core)], 10)

    mine = {
        len(which): jnp.dot(attended, taken_columns(wso, aligned(core), which), preferred_element_type=F32)
        for which in (far, near) if which
    }
    pair_wait(s_t, g_t.at[:, aligned(other_core)], 10)
    theirs = g_t[:, aligned(other_core)]
    scatter_products(
        lambda which: mine[len(which)]
        + jnp.dot(theirs, taken_columns(wso, aligned(other_core), which), preferred_element_type=F32),
        s_e, r_e, e_send, e_recv,
    )
    swap_wait(5, 6, 7)

    def turn(g, carry):
        vt_mem[aligned(g, 256), :] = values[:, aligned(g, 256)].T
        return carry

    lax.fori_loop(0, groups, turn, 0)
    mixed = scatter_sum(s_e, r_e, e_send, e_recv)
    middle_16 = (first.astype(F32) + mixed).astype(BF16)
    middle = middle_16.astype(F32)

    s_m[...] = middle_16
    g_m[:, aligned(core)] = middle_16
    pair_start(s_m, g_m.at[:, aligned(core)], 11)
    pair_wait(s_x, g_x.at[:, aligned(other_core)], 8)
    pair_wait(s_m, g_m.at[:, aligned(other_core)], 11)
    both_middle = g_m[...].astype(F32)
    cross_scaled = (both_middle * g_x[0:1, :]).astype(BF16)
    scatter_products(
        lambda which: jnp.dot(cross_scaled, taken_columns(wcq, slice(None), which), preferred_element_type=F32),
        s_f, r_f, f_send, f_recv,
    )
    squares = jnp.broadcast_to(jnp.sum(both_middle * both_middle, axis=1, keepdims=True), (rows, LANES))
    squares = jnp.concatenate([squares] * (LANES // rows), axis=0).T[0:1, :]
    row8 = lax.broadcasted_iota(jnp.int32, (8, LANES), 0)
    square_rows = place(row8, split3(squares)).astype(BF16)
    s_q[pl.ds(rows, 8), :] = square_rows
    g_q[slot(0), pl.ds(rows, 8), :] = square_rows
    raw = scatter_sum(s_f, r_f, f_send, f_recv).astype(BF16)
    s_q[pl.ds(0, rows), :] = raw
    g_q[slot(0), pl.ds(0, rows), :] = raw

    gather_start(s_q, g_q, q_send, q_recv)
    gather_wait(s_q, g_q, q_send, q_recv, far + near)
    sums = jnp.zeros((8, LANES), F32)
    for k in range(half):
        sums = sums + g_q[k, pl.ds(rows, 8), :].astype(F32)
    mean = (sums[0:1, :] + sums[1:2, :] + sums[2:3, :]) * (1.0 / d_model)
    factor = lax.rsqrt(mean + EPS) * score_scale

    own_block = (
        lax.div(lax.broadcasted_iota(jnp.int32, (LANES, 256), 0), rows)
        == lax.div(lax.broadcasted_iota(jnp.int32, (LANES, 256), 1), 64)
    )
    lane_head = lax.div(lax.broadcasted_iota(jnp.int32, (64, LANES), 1), rows)
    left = lax.broadcasted_iota(jnp.int32, (32, LANES), 1) < 64

    def deliver(target):
        remote(s_g.at[target], r_g.at[chip], g_send.at[target], g_recv.at[chip], (b, 2 * target + core)).start()

    def remember(g):
        query = jnp.concatenate(
            [g_q[lax.rem(2 * g + which - chip + half + 2, half), pl.ds(0, rows), :] for which in range(2)], axis=1
        ).astype(F32)
        query = jnp.where(own_block, jnp.concatenate([query] * 4, axis=0), 0.0).astype(BF16)
        score = lax.dot_general(keys[:, aligned(g, 256)], query, NT, preferred_element_type=F32) * factor
        most = jnp.max(score, axis=0, keepdims=True)
        weight = jnp.exp(score - most).astype(BF16)
        total = jnp.sum(weight.astype(F32), axis=0, keepdims=True)
        spread = jnp.dot(vt_mem[aligned(g, 256), :], weight, preferred_element_type=F32)
        taken = jnp.where(lane_head == 0, spread[0:64], 0.0)
        for head in range(1, 4):
            taken = jnp.where(lane_head == head, spread[head * 64 : head * 64 + 64], taken)
        stat = place(row8, split3(most) + split3(total))
        turned = pltpu.roll(taken, 64, 1)
        turned_stat = pltpu.roll(stat, 64, 1)
        s_g[2 * g, pl.ds(0, 32), :] = jnp.where(left, taken[0:32], turned[32:64]).astype(BF16)
        s_g[2 * g, pl.ds(32, 8), :] = jnp.where(left[0:8], stat, turned_stat).astype(BF16)
        s_g[2 * g + 1, pl.ds(0, 32), :] = jnp.where(left, turned[0:32], taken[32:64]).astype(BF16)
        s_g[2 * g + 1, pl.ds(32, 8), :] = jnp.where(left[0:8], turned_stat, stat).astype(BF16)

    own_group = lax.div(chip, 2)
    offsets = sorted(range(groups), key=lambda k: -min(k % 4, 4 - k % 4) if k else 1)
    for first_at in range(0, groups, AT_ONCE):
        now = [(offset, lax.rem(own_group + offset, groups)) for offset in offsets[first_at : first_at + AT_ONCE]]
        for offset, g in now:
            remember(g)
        for offset, g in now:
            for target in [2 * g, 2 * g + 1] if offset else [chip + 1 - 2 * lax.rem(chip, 2)]:
                deliver(target)
    r_g[chip] = s_g[chip]

    def drain_g():
        for k in steps:
            target = chip_at(k)
            remote(s_g.at[target], r_g.at[chip], g_send.at[target], g_recv.at[chip], peer(k)).wait_send()

    drains.append(drain_g)
    for k in steps:
        source = chip_at(half - k)
        remote(s_g.at[chip], r_g.at[source], g_send.at[chip], g_recv.at[source], peer(half - k)).wait_recv()
    stats = [r_g[source, pl.ds(32, 8), :].astype(F32) for source in range(half)]
    mosts = [stat[0:1] + stat[1:2] + stat[2:3] for stat in stats]
    top = functools.reduce(jnp.maximum, mosts)
    over = jnp.zeros((32, LANES), F32)
    under = jnp.zeros((1, LANES), F32)
    for source in range(half):
        share = jnp.exp(mosts[source] - top)
        stat = stats[source]
        under = under + share * (stat[3:4] + stat[4:5] + stat[5:6])
        over = over + share * r_g[source, pl.ds(0, 32), :].astype(F32)
    turned = (over / under).T
    crossed = jnp.concatenate([turned[rows * at : rows * at + rows] for at in (0, 2, 1, 3)], axis=1).astype(BF16)

    s_h[...] = crossed
    g_h[slot(0)] = crossed
    earlier = list(drains)
    drains.clear()
    gather_start(s_h, g_h, h_send, h_recv)
    for drain in earlier:
        drain()

    def products(which, who):
        block = jnp.concatenate([g_h[at] for at in which], axis=1)
        weight = jnp.concatenate([wco[pl.ds(at * LANES, LANES), aligned(who)] for at in which], axis=0)
        return jnp.dot(block, weight, preferred_element_type=F32)

    gather_wait(s_h, g_h, h_send, h_recv, near)
    theirs, mine = products(near, other_core), middle + products(near, core)
    gather_wait(s_h, g_h, h_send, h_recv, far)
    if far:
        theirs = theirs + products(far, other_core)
    s_o[...] = theirs
    pair_start(s_o, r_o, 12)
    if far:
        mine = mine + products(far, core)
    pair_wait(s_o, r_o, 12)
    out_ref[...] = (mine + r_o[...]).astype(BF16)

    for drain in drains:
        drain()


def body(
    nb, nc, hidden_in, self_gain, w_self, w_self_out, cross_gain, w_cross_q, w_cross_out, cache_kv, memory_kv, parents, prefix_len
):
    rows = hidden_in.shape[0]
    d_model = w_self.shape[0]
    hyps = nb * rows
    cache_rows = cache_kv.shape[0] * cache_kv.shape[1] * cache_kv.shape[2]
    mem_count, mem_width = memory_kv.shape
    width = cache_rows // rows
    hbm = pl.BlockSpec(memory_space=pl.ANY)
    wide = nc * LANES
    chips = nc // 2

    def v(*shape):
        return pltpu.VMEM(shape, BF16)

    def f(*shape):
        return pltpu.VMEM(shape, F32)

    def sems(count):
        return pltpu.SemaphoreType.DMA((count,))

    return pl.pallas_call(
        functools.partial(kernel, nb, nc, d_model),
        out_shape=pltpu.VMEM((rows, LANES), BF16),
        in_specs=[hbm] * 11,
        out_specs=pl.BlockSpec(memory_space=pltpu.VMEM),
        scratch_shapes=[
            v(1, LANES), v(1, LANES), pltpu.VMEM((1, hyps), jnp.int32), pltpu.VMEM((1, hyps), jnp.int32),
            v(d_model // 2, 6 * LANES), v(2 * LANES, wide // 2), v(2 * LANES, wide // 2), v(wide // 2, 2 * LANES),
            v(cache_rows, LANES), v(2 * mem_count, wide // 2), v(2 * mem_count, wide // 2), v(wide // 2, 2 * mem_count),
            v(width, rows * LANES), v(width, rows * LANES), v(hyps, rows * LANES), pltpu.VMEM((hyps, LANES), F32),
            v(rows + 8, LANES), v(chips, rows + 8, LANES), pltpu.VMEM((8, LANES), F32), pltpu.VMEM((8, 2 * LANES), F32),
            v(rows, LANES), v(hyps, LANES),
            v(hyps, 2 * LANES), v(nb, rows, 2 * LANES),
            v(rows, LANES), v(rows, 2 * LANES),
            v(chips, rows, LANES), v(chips, rows, LANES),
            v(rows, LANES), v(rows, 2 * LANES),
            v(chips, rows, LANES), v(chips, rows, LANES),
            v(rows + 8, LANES), v(chips, rows + 8, LANES),
            v(chips, 40, LANES), v(chips, 40, LANES),
            v(rows, LANES), v(chips, rows, LANES),
            f(rows, 4 * LANES), f(rows, 4 * LANES), f(rows, LANES), f(rows, LANES),
            sems(15), sems(13), sems(13),
            sems(chips), sems(chips), sems(nb), sems(nb), sems(nb), sems(nb), sems(chips), sems(chips),
            sems(chips), sems(chips), sems(chips), sems(chips), sems(chips), sems(chips), sems(chips), sems(chips),
        ],
        compiler_params=pltpu.CompilerParams(
            collective_id=0, has_side_effects=True, vmem_limit_bytes=VMEM_BYTES
        ),
    )(
        hidden_in,
        self_gain.reshape(1, LANES),
        cross_gain.reshape(1, LANES),
        parents.reshape(1, hyps),
        prefix_len.reshape(1, hyps),
        jnp.transpose(w_self, (1, 0, 2)),
        w_self_out,
        w_cross_q,
        w_cross_out,
        cache_kv.reshape(cache_rows, LANES),
        memory_kv,
    )


def solution(mesh):
    return jax.shard_map(
        functools.partial(body, mesh.shape["beam"], mesh.shape["blk"]),
        mesh=mesh,
        in_specs=(
            P("beam", "blk"),
            P("blk"),
            P(None, None, "blk"),
            P("blk", None),
            P("blk"),
            P("blk", None),
            P(None, "blk"),
            P("beam", None, "blk", None),
            P("blk", None),
            P(),
            P(),
        ),
        out_specs=P("beam", "blk"),
        check_vma=False,
    )
```
